32 devices in a mesh: clip: 2 (over y), row: 16 (over z, x, core).
Axes of the slice: x: 2, y: 2, z: 4, core: 2. Of those that a mesh axis runs over, the one named last changes fastest.
Arguments:
- frames: bfloat16 [3, 48, 512], P(None, None, ('clip', 'row')), parts along dimension 2, may hold values from -1 to 1
- frame_owner: int32 [32], P('clip'), parts along dimension 0, may hold values from 0 to 15, each once
- picks: int32 [16], P('clip'), parts along dimension 0, may hold values from 0 to 15
- patch_weight: bfloat16 [768, 1024], replicated, may hold values from -0.21875 to 0.21875
- patch_bias: float32 [1024], replicated, may hold values from -6 to 6
- norm_gain: float32 [1024], replicated, may hold values from 0.1 to 1.9
- head_weight: bfloat16 [1024, 1024], replicated, may hold values from -0.1875 to 0.1875
- head_bias: float32 [1024], replicated, may hold values from -6 to 6
- head_out: float32 [1024], replicated, may hold values from -6 to 6
- hidden_state: bfloat16 [96, 16, 16, 128], P(('clip', 'row')), parts along dimension 0
- group_gain: float32 [128], replicated, may hold values from 0.1 to 1.9
- group_shift: float32 [128], replicated, may hold values from -6 to 6
- out_weight: bfloat16 [3, 3, 3, 3, 128], replicated, may hold values from -0.625 to 0.625
- inner_weight: bfloat16 [3, 3, 3, 128, 128], replicated, may hold values from -0.109375 to 0.109375
Outputs:
- inner_grad: bfloat16 [96, 16, 16, 128], P(('clip', 'row')), parts along dimension 0
The draws below stay inside these ranges and needn't reach their ends.
There are 2 independent parts, one for each index of `clip`. The reference program is written for one: setup_inputs(seed, part) draws one part's arguments, and reference() takes and returns one part's arrays. A program takes and returns all parts, laid end to end along the dimension named above; an argument that names none is the same for every part. Nothing has to cross between parts.
Inputs may be any that keep to these rules, and one draw needn't show every extreme that they name: `frame_owner`: each of the 16 frames appears once.
All inputs are finite; a program needn't handle non-finite values.
Results may differ from the reference program's by a relative error of at most 0.0051.
The reference program's roundings to bfloat16 on the way (of `tokens`, `token_grad`, `pixel_grad`, `ordered` and `state_grad`) count: a program that leaves them out, or rounds other values in their place, can miss the bound.
Values may be sent and summed in bfloat16 or wider, within the bound.
A program may use at most 192 MiB of HBM per device.

```python
import jax
import jax.numpy as jnp
from jax import lax

D = 1024
PATCH = 16
PIX = 768
C = 128
GROUPS = 32
FRAMES = 16
NPICK = 8
H = 48
W = 16


def draw_hidden_state(key, part):
    key_a, key_b, key_c = jax.random.split(jax.random.fold_in(key, 11), 3)
    row_pos = jnp.arange(H, dtype=jnp.float32) / (H - 1)
    random_part = jax.random.normal(key_a, (H, FRAMES, W, C), jnp.float32)
    row_scale = jnp.exp(jnp.log(3.0) * row_pos)
    trend = 2.0 * (2.0 * row_pos - 1.0)
    chan_scale = jnp.exp(jax.random.uniform(key_b, (C,), jnp.float32, jnp.log(0.5), jnp.log(2.0)))
    offset = 0.5 * jax.random.normal(key_c, (C,), jnp.float32)
    shaped = random_part * row_scale[:, None, None, None] + trend[:, None, None, None]
    result_values = shaped * chan_scale + offset
    return result_values.astype(jnp.bfloat16)


def touch_ends(result, stream_key, least, largest):
    shape = result.shape
    spot = [jax.random.randint(jax.random.fold_in(stream_key, axis), (), 0, shape[axis]) for axis in range(len(shape))]
    result = result.at[tuple(spot)].set(least)
    longest = shape.index(max(shape))
    spot[longest] = (spot[longest] + 1) % shape[longest]
    return result.at[tuple(spot)].set(largest)


def levels(own_key, extent, cuts, smallest, top_value):
    factor_of = 1.0
    for dim, blocks in cuts:
        draws = jax.random.uniform(jax.random.fold_in(jax.random.fold_in(own_key, 6), dim), (blocks,), jnp.float32, smallest / len(cuts), top_value / len(cuts))
        factor_of = factor_of * jnp.repeat(jnp.exp(draws), extent[dim] // blocks).reshape((-1,) + (1,) * (len(extent) - 1 - dim))
    return factor_of


def scatter_about(key, shape, width, reach, kind=jnp.bfloat16):
    drawn = width * jax.random.normal(key, shape, jnp.float32)
    return jnp.clip(drawn, min=-reach, max=reach).astype(kind)


def setup_inputs(seed: int = 0, part: int = 0) -> dict:
    seeds = jax.random.split(jax.random.key(seed), 15)
    own_keys = jax.random.split(jax.random.fold_in(seeds[14], part), 15)
    frames = jnp.clip(jax.random.uniform(own_keys[0], (3, H, FRAMES * W), jnp.float32, -1.0, 1.0) * levels(own_keys[0], (3, H, FRAMES * W), ((2, 16),), -0.4, 0.0), -1.0, 1.0).astype(jnp.bfloat16)
    frame_owner = jax.random.permutation(own_keys[1], FRAMES).astype(jnp.int32)
    picks = touch_ends(jax.random.randint(own_keys[2], (NPICK,), 0, FRAMES), jax.random.fold_in(own_keys[2], 1), 0, FRAMES - 1).astype(jnp.int32)
    patch_weight = scatter_about(seeds[3], (PIX, D), PIX ** -0.5, 0.21875)
    patch_bias = scatter_about(seeds[4], (D,), 1.0, 6.0, jnp.float32)
    norm_gain = jnp.clip(1.0 + 0.18 * jax.random.normal(seeds[5], (D,), jnp.float32), 0.1, 1.9)
    head_weight = scatter_about(seeds[6], (D, D), D ** -0.5, 0.1875)
    head_bias = scatter_about(seeds[7], (D,), 1.0, 6.0, jnp.float32)
    head_out = scatter_about(seeds[8], (D,), 1.0, 6.0, jnp.float32)
    hidden_state = draw_hidden_state(jax.random.fold_in(jax.random.fold_in(seeds[14], part), 71), part)
    group_gain = jnp.clip(1.0 + 0.18 * jax.random.normal(seeds[10], (C,), jnp.float32), 0.1, 1.9)
    group_shift = scatter_about(seeds[11], (C,), 1.0, 6.0, jnp.float32)
    out_weight = scatter_about(seeds[12], (3, 3, 3, 3, C), (27 * 3) ** -0.5, 0.625)
    inner_weight = scatter_about(seeds[13], (3, 3, 3, C, C), (27 * C) ** -0.5, 0.109375)
    return dict(frames=frames, frame_owner=frame_owner, picks=picks, patch_weight=patch_weight, patch_bias=patch_bias, norm_gain=norm_gain, head_weight=head_weight, head_bias=head_bias, head_out=head_out, hidden_state=hidden_state, group_gain=group_gain, group_shift=group_shift, out_weight=out_weight, inner_weight=inner_weight)


eps_norm = 1e-06

def silu_slope(values):
    sigmoid = jax.nn.sigmoid(values)
    return sigmoid * (1.0 + values * (1.0 - sigmoid))

def pixel_rows(padded, out_weight, amount):
    frame_count = padded.shape[2]
    columns = padded.shape[3]
    widened = jnp.pad(padded, ((0, 0), (0, 0), (0, 2), (1, 1)))
    summed = jnp.zeros((amount * frame_count * columns, out_weight.shape[4]), jnp.float32)
    for time_tap in range(3):
        for row_tap in range(3):
            for col_tap in range(3):
                window = widened[:, 2 - row_tap:2 - row_tap + amount, 2 - time_tap:2 - time_tap + frame_count, 2 - col_tap:2 - col_tap + columns]
                flat_window = window.reshape(3, amount * frame_count * columns).T
                summed = summed + jnp.dot(flat_window, out_weight[time_tap, row_tap, col_tap], preferred_element_type=jnp.float32)
    return summed.reshape(amount, frame_count, columns, out_weight.shape[4])

def inner_rows(padded, inner_weight, amount):
    frame_count = padded.shape[1]
    columns = padded.shape[2]
    channel_count = padded.shape[3]
    widened = jnp.pad(padded, ((0, 0), (0, 2), (1, 1), (0, 0)))
    summed = jnp.zeros((amount * frame_count * columns, inner_weight.shape[3]), jnp.float32)
    for time_tap in range(3):
        for row_tap in range(3):
            for col_tap in range(3):
                window = widened[2 - row_tap:2 - row_tap + amount, 2 - time_tap:2 - time_tap + frame_count, 2 - col_tap:2 - col_tap + columns, :]
                summed = summed + jnp.dot(window.reshape(amount * frame_count * columns, channel_count), inner_weight[time_tap, row_tap, col_tap].T, preferred_element_type=jnp.float32)
    return summed.reshape(amount, frame_count, columns, inner_weight.shape[3])

def by_blocks(padded, row_axis, height, function):
    row_block = 8

    def one_block(start):
        piece = lax.dynamic_slice_in_dim(padded, start, row_block + 2, row_axis)
        return function(piece, row_block)
    starts = jnp.arange(height // row_block, dtype=jnp.int32) * row_block
    blocks = lax.map(one_block, starts)
    return blocks.reshape((height,) + blocks.shape[2:])

def reference(frames, frame_owner, picks, patch_weight, patch_bias, norm_gain, head_weight, head_bias, head_out, hidden_state, group_gain, group_shift, out_weight, inner_weight):
    height = frames.shape[1]
    frame_width = hidden_state.shape[2]
    total_columns = frames.shape[2]
    tokens = frames.reshape(3, height // PATCH, PATCH, total_columns // PATCH, PATCH).transpose(1, 3, 0, 2, 4).reshape(-1, PIX)
    embedded = jnp.dot(tokens, patch_weight, preferred_element_type=jnp.float32) + patch_bias
    centred = embedded - lax.optimization_barrier(jnp.mean(embedded, axis=1, keepdims=True))
    inv_spread = lax.rsqrt(lax.optimization_barrier(jnp.mean(centred * centred, axis=1, keepdims=True)) + eps_norm)
    normed = centred * inv_spread
    per_slot = (normed * norm_gain).reshape(height // PATCH, FRAMES, frame_width // PATCH, D)
    pooled = lax.optimization_barrier(jnp.mean(per_slot, axis=(0, 2)))
    head_full = head_weight.astype(jnp.float32)
    before = jnp.dot(pooled, head_full, precision=lax.Precision.HIGHEST) + head_bias
    pulled = jnp.dot(head_out * silu_slope(before), head_full.T, precision=lax.Precision.HIGHEST)
    picked = lax.optimization_barrier(jnp.sum((picks[:, None] == frame_owner[None, :]).astype(jnp.float32), axis=0))
    slot_grad = picked[:, None] * pulled
    spread_grad = jnp.broadcast_to(slot_grad[None, :, None, :], per_slot.shape).reshape(-1, D)
    scaled = norm_gain * spread_grad
    token_grad = inv_spread * (scaled - lax.optimization_barrier(jnp.mean(scaled, axis=1, keepdims=True)) - normed * lax.optimization_barrier(jnp.mean(scaled * normed, axis=1, keepdims=True)))
    token_grad = token_grad.astype(jnp.bfloat16)
    patch_grad = jnp.dot(token_grad, patch_weight.T, preferred_element_type=jnp.float32)
    pixel_grad = patch_grad.reshape(height // PATCH, total_columns // PATCH, 3, PATCH, PATCH).transpose(2, 0, 3, 1, 4).reshape(3, height, total_columns).astype(jnp.bfloat16)
    by_slot = pixel_grad.reshape(3, height, FRAMES, frame_width)
    owner_table = (frame_owner[:, None] == jnp.arange(FRAMES, dtype=jnp.int32)[None, :]).astype(jnp.float32)
    ordered = jnp.einsum('krbw,bf->krfw', by_slot.astype(jnp.float32), owner_table).astype(jnp.bfloat16)
    grouped = hidden_state.astype(jnp.float32).reshape(hidden_state.shape[:3] + (GROUPS, C // GROUPS))
    cell_total = grouped.size // GROUPS
    group_mean = lax.optimization_barrier(jnp.sum(grouped, axis=(0, 1, 2, 4))) / cell_total
    second_mean = lax.optimization_barrier(jnp.sum(grouped * grouped, axis=(0, 1, 2, 4))) / cell_total
    inverse = lax.rsqrt(second_mean - group_mean * group_mean + eps_norm)
    normed_state = (grouped - group_mean[:, None]) * inverse[:, None]
    gain_table = group_gain.reshape(GROUPS, C // GROUPS)
    affine = normed_state * gain_table + group_shift.reshape(GROUPS, C // GROUPS)
    padded_pixels = jnp.pad(ordered, ((0, 0), (1, 1), (0, 0), (0, 0)))
    slope_in = by_blocks(padded_pixels, 1, height, lambda piece, amount: pixel_rows(piece, out_weight, amount))
    upstream = slope_in.reshape(grouped.shape) * silu_slope(affine) * gain_table
    first_part = lax.optimization_barrier(jnp.sum(upstream, axis=(0, 1, 2, 4))) / cell_total
    second_part = lax.optimization_barrier(jnp.sum(upstream * normed_state, axis=(0, 1, 2, 4))) / cell_total
    state_grad = ((upstream - first_part[:, None] - normed_state * second_part[:, None]) * inverse[:, None]).reshape(hidden_state.shape).astype(jnp.bfloat16)
    padded_state = jnp.pad(state_grad, ((1, 1), (0, 0), (0, 0), (0, 0)))
    inner_grad = by_blocks(padded_state, 0, height, lambda piece, amount: inner_rows(piece, inner_weight, amount))
    return inner_grad.astype(jnp.bfloat16)
```

```python
import functools

import jax
import jax.numpy as jnp
from jax import lax
from jax.experimental import pallas as pl
from jax.experimental.pallas import tpu as pltpu
from jax.sharding import PartitionSpec as P

PATCH = 16
GROUPS = 32
FRAMES = 16


eps_norm = 1e-06
MESH = pl.DeviceIdType.MESH


def extended(block, sides, width):
    for axis, dim in sides:
        count = lax.axis_size(axis)
        forward = [(i, i + 1) for i in range(count - 1)]
        backward = [(target, source) for source, target in forward]
        low = lax.ppermute(
            lax.slice_in_dim(block, block.shape[dim] - width, None, axis=dim), axis, forward
        )
        high = lax.ppermute(lax.slice_in_dim(block, 0, width, axis=dim), axis, backward)
        block = jnp.concatenate([low, block, high], axis=dim)
    return block


def silu_slope(values):
    sigmoid = jax.nn.sigmoid(values)
    return sigmoid * (1.0 + values * (1.0 - sigmoid))


def to_tokens(pixels):
    channels, height, columns = pixels.shape
    shaped = pixels.reshape(channels, height // PATCH, PATCH, columns // PATCH, PATCH)
    return shaped.transpose(1, 3, 0, 2, 4).reshape(
        height // PATCH * (columns // PATCH), channels * PATCH * PATCH
    )


def from_tokens(token_grads, height, columns):
    shaped = token_grads.reshape(height // PATCH, columns // PATCH, 3, PATCH, PATCH)
    return shaped.transpose(2, 0, 3, 1, 4).reshape(3, height, columns)


def pixel_back(padded, out_weight, amount):
    frame_count = padded.shape[2]
    columns = padded.shape[3]
    widened = jnp.pad(padded, ((0, 0), (0, 0), (0, 2), (1, 1)))
    windows = []
    for time_tap in range(3):
        for row_tap in range(3):
            for col_tap in range(3):
                windows.append(
                    widened[
                        :,
                        2 - row_tap : 2 - row_tap + amount,
                        2 - time_tap : 2 - time_tap + frame_count,
                        2 - col_tap : 2 - col_tap + columns,
                    ]
                )
    stacked = jnp.stack(windows, 0).reshape(27 * 3, amount * frame_count * columns)
    kernel = out_weight.reshape(27 * 3, out_weight.shape[4])
    summed = lax.dot_general(
        stacked, kernel, (((0,), (0,)), ((), ())), preferred_element_type=jnp.float32
    )
    return summed.reshape(amount, frame_count, columns, out_weight.shape[4])


def inner_back(padded, inner_weight, amount):
    frame_count = padded.shape[1]
    columns = padded.shape[2]
    channel_count = padded.shape[3]
    widened = jnp.pad(padded, ((0, 0), (0, 2), (1, 1), (0, 0)))
    summed = jnp.zeros((amount * frame_count * columns, inner_weight.shape[3]), jnp.float32)
    for time_tap in range(3):
        windows = []
        for row_tap in range(3):
            for col_tap in range(3):
                windows.append(
                    widened[
                        2 - row_tap : 2 - row_tap + amount,
                        2 - time_tap : 2 - time_tap + frame_count,
                        2 - col_tap : 2 - col_tap + columns,
                        :,
                    ]
                )
        joined = jnp.concatenate(windows, axis=3).reshape(
            amount * frame_count * columns, 9 * channel_count
        )
        kernel = jnp.transpose(inner_weight[time_tap], (0, 1, 3, 2)).reshape(
            9 * channel_count, inner_weight.shape[3]
        )
        summed = summed + jnp.dot(joined, kernel, preferred_element_type=jnp.float32)
    return summed.reshape(amount, frame_count, columns, inner_weight.shape[3])


def group_back(state_rows, slope_in, group_mean, inverse, group_gain, group_shift, cell_total):
    grouped = state_rows.astype(jnp.float32).reshape(state_rows.shape[:3] + (GROUPS, -1))
    gain_table = group_gain.reshape(GROUPS, -1)
    shift_table = group_shift.reshape(GROUPS, -1)
    normed_state = (grouped - group_mean[:, None]) * inverse[:, None]
    affine = normed_state * gain_table + shift_table
    upstream = slope_in.reshape(grouped.shape) * silu_slope(affine) * gain_table
    group_terms = lax.psum(
        (jnp.sum(upstream, axis=(0, 1, 2, 4)), jnp.sum(upstream * normed_state, axis=(0, 1, 2, 4))),
        "row",
    )
    first_part = group_terms[0] / cell_total
    second_part = group_terms[1] / cell_total
    state_grad = (upstream - first_part[:, None] - normed_state * second_part[:, None]) * inverse[
        :, None
    ]
    return state_grad.reshape(state_rows.shape).astype(jnp.bfloat16)


def per_device(
    frames,
    frame_owner,
    picks,
    patch_weight,
    patch_bias,
    norm_gain,
    head_weight,
    head_bias,
    head_out,
    hidden_state,
    group_gain,
    group_shift,
    out_weight,
    inner_weight,
):
    devices = lax.axis_size("row")
    position = lax.axis_index("row")
    per_frame = devices // FRAMES
    slot = position // per_frame
    height = frames.shape[1]
    strip = frames.shape[2]
    own_rows = hidden_state.shape[0]
    frame_width = hidden_state.shape[2]
    tokens = to_tokens(frames)
    embedded = jnp.dot(tokens, patch_weight, preferred_element_type=jnp.float32) + patch_bias
    centred = embedded - jnp.mean(embedded, axis=1, keepdims=True)
    inv_spread = lax.rsqrt(jnp.mean(centred * centred, axis=1, keepdims=True) + eps_norm)
    normed = centred * inv_spread
    slot_mask = (jnp.arange(FRAMES, dtype=jnp.int32) == slot).astype(jnp.float32)
    partial_pool = slot_mask[:, None] * jnp.sum(normed * norm_gain, axis=0)[None, :]
    grouped = hidden_state.reshape(own_rows, FRAMES, frame_width, GROUPS, -1)
    first_sum = jnp.sum(grouped, axis=(0, 1, 2, 4), dtype=jnp.float32)
    second_sum = jnp.sum(jnp.square(grouped.astype(jnp.float32)), axis=(0, 1, 2, 4))
    pooled_sum, first_total, second_total = lax.psum((partial_pool, first_sum, second_sum), "row")
    frame_tokens = height // PATCH * (strip * per_frame // PATCH)
    pooled = pooled_sum / frame_tokens
    head_full = head_weight.astype(jnp.float32)
    before = jnp.dot(pooled, head_full, precision=lax.Precision.HIGHEST) + head_bias
    pulled = jnp.dot(head_out * silu_slope(before), head_full.T, precision=lax.Precision.HIGHEST)
    picked = jnp.sum((picks[:, None] == frame_owner[None, :]).astype(jnp.float32), axis=0)
    slot_grad = jnp.dot(slot_mask * picked, pulled, precision=lax.Precision.HIGHEST)
    scaled = norm_gain * slot_grad
    token_grad = inv_spread * (
        scaled - jnp.mean(scaled) - normed * jnp.mean(scaled * normed, axis=1, keepdims=True)
    )
    patch_grad = lax.dot_general(
        token_grad.astype(jnp.bfloat16),
        patch_weight,
        (((1,), (1,)), ((), ())),
        preferred_element_type=jnp.float32,
    )
    pixel_local = from_tokens(patch_grad, height, strip).astype(jnp.bfloat16)
    arrived = lax.all_to_all(pixel_local, "row", split_axis=1, concat_axis=2, tiled=True)
    by_slot = arrived.reshape(3, own_rows, FRAMES, frame_width)
    owner_table = (frame_owner[:, None] == jnp.arange(FRAMES, dtype=jnp.int32)[None, :]).astype(
        jnp.bfloat16
    )
    ordered = jnp.einsum(
        "krbw,bf->krfw", by_slot, owner_table, preferred_element_type=jnp.float32
    ).astype(jnp.bfloat16)
    cell_total = own_rows * devices * FRAMES * frame_width * (hidden_state.shape[3] // GROUPS)
    group_mean = first_total / cell_total
    inverse = lax.rsqrt(second_total / cell_total - group_mean * group_mean + eps_norm)
    pixel_padded = extended(ordered, (("row", 1),), 1)
    slope_in = pixel_back(pixel_padded, out_weight, own_rows)
    state_grad = group_back(
        hidden_state, slope_in, group_mean, inverse, group_gain, group_shift, cell_total
    )
    grad_padded = extended(state_grad, (("row", 0),), 1)
    return inner_back(grad_padded, inner_weight, own_rows).astype(jnp.bfloat16)


def split_rows(row):
    high = row.astype(jnp.bfloat16).astype(jnp.float32)
    rest = row - high
    middle = rest.astype(jnp.bfloat16).astype(jnp.float32)
    low = rest - middle
    index = lax.broadcasted_iota(jnp.int32, (8, row.shape[1]), 0)
    stacked = jnp.where(
        index == 0, high, jnp.where(index == 1, middle, jnp.where(index == 2, low, 0.0))
    )
    return stacked.astype(jnp.bfloat16)


def fused_kernel(
    n,
    frames_any,
    owner_any,
    picks_any,
    patch_any,
    patch_bias_any,
    norm_gain_any,
    head_any,
    head_bias_any,
    head_out_any,
    hidden_any,
    group_gain_any,
    group_shift_any,
    out_weight_any,
    inner_any,
    out,
    frames,
    owner,
    picks,
    patch_bias,
    norm_gain,
    head_bias,
    head_out,
    group_gain,
    group_shift,
    out_weight,
    patch_w,
    head_w,
    hidden,
    inner_w,
    pixels,
    tokens,
    sent,
    arrived,
    by_frame,
    columns,
    band,
    slope,
    factor,
    normed_ref,
    turned,
    windows,
    sums_one,
    sums_two,
    local_sem,
    small_sem,
    halo_send,
    halo_recv,
    one_send,
    one_recv,
    pix_send,
    pix_recv,
    two_send,
    two_recv,
):
    me = lax.axis_index("row")
    strip, height = frames.shape[1], frames.shape[2]
    patch_rows = height // PATCH
    own = out.shape[0]
    wide = out.shape[3]
    channels = out.shape[4]
    line = FRAMES * wide
    per_group = channels // GROUPS
    cell_total = own * n * FRAMES * wide * per_group
    piece = 3 * strip
    half = arrived.shape[1]

    def peer(offset):
        target = me
        step = 1
        while step < n:
            if offset // step % 2:
                target = target + step * (1 - 2 * lax.rem(lax.div(me, step), 2))
            step *= 2
        return target

    farthest_first = range(n - 1, 0, -1)

    barrier = pltpu.get_barrier_semaphore()
    for offset in farthest_first:
        pl.semaphore_signal(barrier, inc=1, device_id={"row": peer(offset)}, device_id_type=MESH)

    loads = [
        pltpu.make_async_copy(hidden_any, hidden.at[pl.ds(1, own)], local_sem.at[0]),
        pltpu.make_async_copy(patch_any, patch_w, local_sem.at[1]),
        pltpu.make_async_copy(head_any, head_w, local_sem.at[2]),
        pltpu.make_async_copy(inner_any, inner_w, local_sem.at[3]),
    ]
    small = [
        pltpu.make_async_copy(source, target, small_sem.at[index])
        for index, (source, target) in enumerate(
            (
                (frames_any, frames),
                (owner_any, owner),
                (picks_any, picks),
                (patch_bias_any, patch_bias),
                (norm_gain_any, norm_gain),
                (head_bias_any, head_bias),
                (head_out_any, head_out),
                (group_gain_any, group_gain),
                (group_shift_any, group_shift),
                (out_weight_any, out_weight),
            )
        )
    ]
    small[0].start()
    loads[0].start()
    loads[1].start()
    for load in small[1:]:
        load.start()
    loads[2].start()
    loads[3].start()

    small[0].wait()
    for colour in range(3):
        pixels[colour] = frames[colour].astype(jnp.float32).T
    tokens[...] = jnp.zeros_like(tokens)
    for colour in range(3):
        for line_in in range(PATCH):
            at = (colour * PATCH + line_in) * PATCH
            tokens[0:patch_rows, at : at + PATCH] = pixels[
                colour, pl.ds(line_in, patch_rows, stride=PATCH), :
            ]
    sent[...] = jnp.zeros_like(sent)

    loads[0].wait()
    first = jnp.zeros((1, channels), jnp.float32)
    second = jnp.zeros((1, channels), jnp.float32)
    for row in range(own):
        state = hidden[1 + row].reshape(line, channels).astype(jnp.float32)
        first = first + jnp.sum(state, axis=0, keepdims=True)
        second = second + jnp.sum(state * state, axis=0, keepdims=True)
    spot = lax.broadcasted_iota(jnp.int32, (2, channels), 0)
    sums_one[me] = jnp.where(spot == 0, first, second)

    for load in small[1:]:
        load.wait()
    loads[1].wait()
    embedded = (
        jnp.dot(
            tokens[...].astype(jnp.bfloat16), patch_w[...], preferred_element_type=jnp.float32
        )
        + patch_bias[...]
    )
    centred = embedded - jnp.mean(embedded, axis=1, keepdims=True)
    inv_spread = lax.rsqrt(jnp.mean(centred * centred, axis=1, keepdims=True) + eps_norm)
    normed = centred * inv_spread
    gain = norm_gain[...]
    pooled = jnp.sum((normed * gain)[0:patch_rows], axis=0, keepdims=True) / patch_rows
    loads[2].wait()
    before = (
        jnp.sum(
            jnp.dot(split_rows(pooled), head_w[...], preferred_element_type=jnp.float32),
            axis=0,
            keepdims=True,
        )
        + head_bias[...]
    )
    pulled = jnp.sum(
        lax.dot_general(
            split_rows(head_out[...] * silu_slope(before)),
            head_w[...],
            (((1,), (1,)), ((), ())),
            preferred_element_type=jnp.float32,
        ),
        axis=0,
        keepdims=True,
    )
    mine = owner[me]
    picked = jnp.float32(0.0)
    for pick in range(picks.shape[0]):
        picked = picked + jnp.where(picks[pick] == mine, jnp.float32(1.0), jnp.float32(0.0))
    scaled = gain * (picked * pulled)
    token_grad = inv_spread * (
        scaled
        - jnp.mean(scaled, axis=1, keepdims=True)
        - normed * jnp.mean(scaled * normed, axis=1, keepdims=True)
    )
    patch_grad = lax.dot_general(
        token_grad.astype(jnp.bfloat16),
        patch_w[...],
        (((1,), (1,)), ((), ())),
        preferred_element_type=jnp.float32,
    )
    patch_grad = patch_grad.astype(jnp.bfloat16).astype(jnp.float32)
    for line_in in range(PATCH):
        joined = jnp.concatenate(
            [
                patch_grad[:, (colour * PATCH + line_in) * PATCH : (colour * PATCH + line_in + 1) * PATCH]
                for colour in range(3)
            ],
            axis=1,
        )
        for patch_row in range(patch_rows):
            at = 2 + patch_row * PATCH + line_in
            sent[at, :, 0:piece] = joined[patch_row : patch_row + 1]
            if at >= half:
                sent[at - half, :, 64 : 64 + piece] = joined[patch_row : patch_row + 1]

    pl.semaphore_wait(barrier, n - 1)

    def broadcast(buffer, send_sem, recv_sem):
        copies = []
        for offset in farthest_first:
            copy = pltpu.make_async_remote_copy(
                src_ref=buffer.at[me],
                dst_ref=buffer.at[me],
                send_sem=send_sem.at[offset],
                recv_sem=recv_sem.at[offset],
                device_id={"row": peer(offset)},
                device_id_type=MESH,
            )
            copy.start()
            copies.append(copy)
        return copies

    pix_copies = []
    for offset in farthest_first:
        target = peer(offset)
        copy = pltpu.make_async_remote_copy(
            src_ref=sent.at[pl.ds(target * own, half)],
            dst_ref=arrived.at[me],
            send_sem=pix_send.at[offset],
            recv_sem=pix_recv.at[offset],
            device_id={"row": target},
            device_id_type=MESH,
        )
        copy.start()
        pix_copies.append(copy)
    one_copies = broadcast(sums_one, one_send, one_recv)
    to_right = pltpu.make_async_remote_copy(
        src_ref=hidden_any.at[pl.ds(own - 1, 1)],
        dst_ref=hidden.at[pl.ds(0, 1)],
        send_sem=halo_send.at[0],
        recv_sem=halo_recv.at[0],
        device_id={"row": lax.rem(me + 1, n)},
        device_id_type=MESH,
    )
    to_left = pltpu.make_async_remote_copy(
        src_ref=hidden_any.at[pl.ds(0, 1)],
        dst_ref=hidden.at[pl.ds(own + 1, 1)],
        send_sem=halo_send.at[1],
        recv_sem=halo_recv.at[1],
        device_id={"row": lax.rem(me + n - 1, n)},
        device_id_type=MESH,
    )

    @pl.when(me < n - 1)
    def _():
        to_right.start()

    @pl.when(me > 0)
    def _():
        to_left.start()

    @pl.when(me == 0)
    def _():
        hidden[0] = jnp.zeros(hidden.shape[1:], hidden.dtype)

    @pl.when(me == n - 1)
    def _():
        hidden[own + 1] = jnp.zeros(hidden.shape[1:], hidden.dtype)

    arrived[me] = sent[pl.ds(me * own, half)]

    column = lax.broadcasted_iota(jnp.int32, (wide, channels), 0)
    for row_tap in range(3):
        for time_tap in range(3):
            taps = [out_weight[time_tap, row_tap, col_tap].astype(jnp.float32) for col_tap in range(3)]
            for colour in range(3):
                at = ((row_tap * 3 + time_tap) * 3 + colour) * wide
                spread = [
                    jnp.broadcast_to(tap[colour : colour + 1], (wide, channels)) for tap in taps
                ]
                for w in range(wide):
                    block = jnp.where(
                        column == w + 1,
                        spread[0],
                        jnp.where(
                            column == w, spread[1], jnp.where(column == w - 1, spread[2], 0.0)
                        ),
                    )
                    band[at : at + wide, w * channels : (w + 1) * channels] = block.astype(
                        jnp.bfloat16
                    )
    depth = band.shape[0]
    if depth > 27 * wide:
        band[27 * wide :, :] = jnp.zeros((depth - 27 * wide, wide * channels), jnp.bfloat16)
    columns[...] = jnp.zeros_like(columns)
    by_frame[...] = jnp.zeros_like(by_frame)

    group_row = lax.broadcasted_iota(jnp.int32, (channels, channels), 0) // per_group
    group_col = lax.broadcasted_iota(jnp.int32, (channels, channels), 1) // per_group
    same_group = (group_row == group_col).astype(jnp.float32)

    def group_sums(buffer):
        total = buffer[0]
        for slot in range(1, n):
            total = total + buffer[slot]
        return jnp.dot(total, same_group, precision=lax.Precision.HIGHEST) / cell_total

    for copy in one_copies:
        copy.wait()
    means = group_sums(sums_one)
    group_mean = means[0:1]
    inverse = lax.rsqrt(means[1:2] - group_mean * group_mean + eps_norm)

    @pl.when(me < n - 1)
    def _():
        to_right.wait_send()
        to_left.wait_recv()

    @pl.when(me > 0)
    def _():
        to_left.wait_send()
        to_right.wait_recv()

    for row in range(own + 2):
        state = hidden[row].reshape(line, channels).astype(jnp.float32)
        normed_state = (state - group_mean) * inverse
        normed_ref[row * line : (row + 1) * line] = normed_state
        affine = normed_state * group_gain[...] + group_shift[...]
        factor[row * line : (row + 1) * line] = silu_slope(affine) * group_gain[...]

    slot_of = []
    for frame in range(FRAMES):
        found = jnp.int32(0)
        for slot in range(n):
            found = jnp.where(owner[slot] == frame, jnp.int32(slot), found)
        slot_of.append(found)

    for copy in pix_copies:
        copy.wait()
    for frame in range(FRAMES):
        for row in range(half):
            by_frame[row, frame : frame + 1, :] = arrived[slot_of[frame], row]
    for row_tap in range(3):
        for time_tap in range(3):
            at = (row_tap * 3 + time_tap) * piece
            for row in range(own + 2):
                source = row - row_tap + 2
                lane = source // half * 64
                columns[row * FRAMES : (row + 1) * FRAMES, at : at + piece] = by_frame[
                    source % half, 2 - time_tap : 2 - time_tap + FRAMES, lane : lane + piece
                ]
    left = columns[...].astype(jnp.bfloat16)
    for w in range(0, wide, 2):
        both = jnp.dot(
            left,
            band[:, w * channels : (w + 2) * channels],
            preferred_element_type=jnp.float32,
        )
        for side in range(2):
            slope[pl.ds(w + side, (own + 2) * FRAMES, stride=wide), :] = both[
                :, side * channels : (side + 1) * channels
            ]

    first = jnp.zeros((1, channels), jnp.float32)
    second = jnp.zeros((1, channels), jnp.float32)
    for row in range(own + 2):
        part = pl.ds(row * line, line)
        upstream = slope[part] * factor[part]
        slope[part] = upstream
        if 1 <= row <= own:
            first = first + jnp.sum(upstream, axis=0, keepdims=True)
            second = second + jnp.sum(upstream * normed_ref[part], axis=0, keepdims=True)
    sums_two[me] = jnp.where(spot == 0, first, second)
    two_copies = broadcast(sums_two, two_send, two_recv)

    loads[3].wait()
    for row_tap in range(3):
        for col_tap in range(3):
            part = pl.ds(col_tap * channels, channels)
            for time_tap in range(3):
                block = inner_w[time_tap, row_tap, col_tap].T
                turned[row_tap, 2 - time_tap, part, 0:channels] = block
                turned[row_tap, 3 - time_tap, part, channels:] = block
            empty = jnp.zeros((channels, channels), jnp.bfloat16)
            turned[row_tap, 3, part, 0:channels] = empty
            turned[row_tap, 0, part, channels:] = empty
    windows[:, FRAMES // 2] = jnp.zeros((own + 2, 2, wide, 3 * channels), jnp.bfloat16)

    for copy in two_copies:
        copy.wait()
    parts = group_sums(sums_two)
    position = lax.rem(lax.broadcasted_iota(jnp.int32, (line, channels), 0), wide)
    for row in range(own + 2):
        part = pl.ds(row * line, line)
        state_grad = (slope[part] - parts[0:1] - normed_ref[part] * parts[1:2]) * inverse
        if row == 0:
            state_grad = jnp.where(me > 0, state_grad, 0.0)
        if row == own + 1:
            state_grad = jnp.where(me < n - 1, state_grad, 0.0)
        after = jnp.where(position == wide - 1, 0.0, pltpu.roll(state_grad, line - 1, 0))
        earlier = jnp.where(position == 0, 0.0, pltpu.roll(state_grad, 1, 0))
        for col_tap, shifted in enumerate((after, state_grad, earlier)):
            windows[row, 0 : FRAMES // 2, :, :, col_tap * channels : (col_tap + 1) * channels] = (
                shifted.astype(jnp.bfloat16).reshape(FRAMES // 2, 2, wide, channels)
            )
    rows = own * line // 2
    taken = jnp.concatenate(
        [
            windows[
                2 - row_tap : 2 - row_tap + own, ahead // 2 : ahead // 2 + FRAMES // 2, ahead % 2
            ].reshape(rows, 3 * channels)
            for row_tap in range(3)
            for ahead in range(4)
        ],
        axis=1,
    )
    summed = jnp.dot(
        taken,
        turned[...].reshape(12 * 3 * channels, 2 * channels),
        preferred_element_type=jnp.float32,
    )
    for side in range(2):
        out[:, :, side] = (
            summed[:, side * channels : (side + 1) * channels]
            .reshape(own, FRAMES // 2, wide, channels)
            .astype(jnp.bfloat16)
        )


def one_frame_each(
    frames,
    frame_owner,
    picks,
    patch_weight,
    patch_bias,
    norm_gain,
    head_weight,
    head_bias,
    head_out,
    hidden_state,
    group_gain,
    group_shift,
    out_weight,
    inner_weight,
):
    n = lax.axis_size("row")
    own, frame_count, wide, channels = hidden_state.shape
    height, strip = frames.shape[1:]
    pix, width = patch_weight.shape
    depth = -(-27 * wide // 128) * 128
    cells = (own + 2) * frame_count * wide
    f32, bf16 = jnp.float32, jnp.bfloat16
    vmem = pl.BlockSpec(memory_space=pltpu.VMEM)
    dma = pltpu.SemaphoreType.DMA
    return pl.pallas_call(
        functools.partial(fused_kernel, n),
        out_shape=jax.ShapeDtypeStruct((own, frame_count // 2, 2, wide, channels), bf16),
        in_specs=[pl.BlockSpec(memory_space=pltpu.HBM)] * 14,
        out_specs=vmem,
        scratch_shapes=[
            pltpu.VMEM((3, strip, height), bf16),
            pltpu.SMEM(frame_owner.shape, jnp.int32),
            pltpu.SMEM(picks.shape, jnp.int32),
            pltpu.VMEM((1, width), f32),
            pltpu.VMEM((1, width), f32),
            pltpu.VMEM((1, width), f32),
            pltpu.VMEM((1, width), f32),
            pltpu.VMEM((1, channels), f32),
            pltpu.VMEM((1, channels), f32),
            pltpu.VMEM(out_weight.shape, bf16),
            pltpu.VMEM((pix, width), bf16),
            pltpu.VMEM(head_weight.shape, bf16),
            pltpu.VMEM((own + 2, frame_count, wide, channels), bf16),
            pltpu.VMEM(inner_weight.shape, bf16),
            pltpu.VMEM(frames.shape, f32),
            pltpu.VMEM((-(-(height // PATCH) // 8) * 8, pix), f32),
            pltpu.VMEM((height + 4, 1, 128), f32),
            pltpu.VMEM((n, (own + 5) // 2, 1, 128), f32),
            pltpu.VMEM(((own + 5) // 2, frame_count + 8, 128), f32),
            pltpu.VMEM(((own + 2) * frame_count, depth), f32),
            pltpu.VMEM((depth, wide * channels), bf16),
            pltpu.VMEM((cells, channels), f32),
            pltpu.VMEM((cells, channels), f32),
            pltpu.VMEM((cells, channels), f32),
            pltpu.VMEM((3, 4, 3 * channels, 2 * channels), bf16),
            pltpu.VMEM((own + 2, frame_count // 2 + 1, 2, wide, 3 * channels), bf16),
            pltpu.VMEM((n, 2, channels), f32),
            pltpu.VMEM((n, 2, channels), f32),
            dma((4,)),
            dma((10,)),
            dma((2,)),
            dma((2,)),
            dma((n,)),
            dma((n,)),
            dma((n,)),
            dma((n,)),
            dma((n,)),
            dma((n,)),
        ],
        compiler_params=pltpu.CompilerParams(
            collective_id=0, has_side_effects=True
        ),
    )(
        frames.transpose(0, 2, 1),
        frame_owner,
        picks,
        patch_weight,
        patch_bias[None],
        norm_gain[None],
        head_weight,
        head_bias[None],
        head_out[None],
        hidden_state,
        group_gain[None],
        group_shift[None],
        out_weight,
        inner_weight,
    ).reshape(hidden_state.shape)


def solution(mesh):
    body = one_frame_each if mesh.shape["row"] == FRAMES else per_device
    return jax.shard_map(
        body,
        mesh=mesh,
        in_specs=(
            P(None, None, ("clip", "row")),
            P("clip"),
            P("clip"),
            P(),
            P(),
            P(),
            P(),
            P(),
            P(),
            P(("clip", "row"), None, None, None),
            P(),
            P(),
            P(),
            P(),
        ),
        out_specs=P(("clip", "row"), None, None, None),
        check_vma=False,
    )
```

```python
import functools

import jax
import jax.numpy as jnp
from jax import lax
from jax.experimental import pallas as pl
from jax.experimental.pallas import tpu as pltpu
from jax.sharding import PartitionSpec as P

PATCH = 16
GROUPS = 32
FRAMES = 16


eps_norm = 1e-06
MESH = pl.DeviceIdType.MESH


def extended(block, sides, width):
    for axis, dim in sides:
        count = lax.axis_size(axis)
        forward = [(i, i + 1) for i in range(count - 1)]
        backward = [(target, source) for source, target in forward]
        low = lax.ppermute(
            lax.slice_in_dim(block, block.shape[dim] - width, None, axis=dim), axis, forward
        )
        high = lax.ppermute(lax.slice_in_dim(block, 0, width, axis=dim), axis, backward)
        block = jnp.concatenate([low, block, high], axis=dim)
    return block


def silu_slope(values):
    sigmoid = jax.nn.sigmoid(values)
    return sigmoid * (1.0 + values * (1.0 - sigmoid))


def to_tokens(pixels):
    channels, height, columns = pixels.shape
    shaped = pixels.reshape(channels, height // PATCH, PATCH, columns // PATCH, PATCH)
    return shaped.transpose(1, 3, 0, 2, 4).reshape(
        height // PATCH * (columns // PATCH), channels * PATCH * PATCH
    )


def from_tokens(token_grads, height, columns):
    shaped = token_grads.reshape(height // PATCH, columns // PATCH, 3, PATCH, PATCH)
    return shaped.transpose(2, 0, 3, 1, 4).reshape(3, height, columns)


def pixel_back(padded, out_weight, amount):
    frame_count = padded.shape[2]
    columns = padded.shape[3]
    widened = jnp.pad(padded, ((0, 0), (0, 0), (0, 2), (1, 1)))
    windows = []
    for time_tap in range(3):
        for row_tap in range(3):
            for col_tap in range(3):
                windows.append(
                    widened[
                        :,
                        2 - row_tap : 2 - row_tap + amount,
                        2 - time_tap : 2 - time_tap + frame_count,
                        2 - col_tap : 2 - col_tap + columns,
                    ]
                )
    stacked = jnp.stack(windows, 0).reshape(27 * 3, amount * frame_count * columns)
    kernel = out_weight.reshape(27 * 3, out_weight.shape[4])
    summed = lax.dot_general(
        stacked, kernel, (((0,), (0,)), ((), ())), preferred_element_type=jnp.float32
    )
    return summed.reshape(amount, frame_count, columns, out_weight.shape[4])


def inner_back(padded, inner_weight, amount):
    frame_count = padded.shape[1]
    columns = padded.shape[2]
    channel_count = padded.shape[3]
    widened = jnp.pad(padded, ((0, 0), (0, 2), (1, 1), (0, 0)))
    summed = jnp.zeros((amount * frame_count * columns, inner_weight.shape[3]), jnp.float32)
    for time_tap in range(3):
        windows = []
        for row_tap in range(3):
            for col_tap in range(3):
                windows.append(
                    widened[
                        2 - row_tap : 2 - row_tap + amount,
                        2 - time_tap : 2 - time_tap + frame_count,
                        2 - col_tap : 2 - col_tap + columns,
                        :,
                    ]
                )
        joined = jnp.concatenate(windows, axis=3).reshape(
            amount * frame_count * columns, 9 * channel_count
        )
        kernel = jnp.transpose(inner_weight[time_tap], (0, 1, 3, 2)).reshape(
            9 * channel_count, inner_weight.shape[3]
        )
        summed = summed + jnp.dot(joined, kernel, preferred_element_type=jnp.float32)
    return summed.reshape(amount, frame_count, columns, inner_weight.shape[3])


def group_back(state_rows, slope_in, group_mean, inverse, group_gain, group_shift, cell_total):
    grouped = state_rows.astype(jnp.float32).reshape(state_rows.shape[:3] + (GROUPS, -1))
    gain_table = group_gain.reshape(GROUPS, -1)
    shift_table = group_shift.reshape(GROUPS, -1)
    normed_state = (grouped - group_mean[:, None]) * inverse[:, None]
    affine = normed_state * gain_table + shift_table
    upstream = slope_in.reshape(grouped.shape) * silu_slope(affine) * gain_table
    group_terms = lax.psum(
        (jnp.sum(upstream, axis=(0, 1, 2, 4)), jnp.sum(upstream * normed_state, axis=(0, 1, 2, 4))),
        "row",
    )
    first_part = group_terms[0] / cell_total
    second_part = group_terms[1] / cell_total
    state_grad = (upstream - first_part[:, None] - normed_state * second_part[:, None]) * inverse[
        :, None
    ]
    return state_grad.reshape(state_rows.shape).astype(jnp.bfloat16)


def per_device(
    frames,
    frame_owner,
    picks,
    patch_weight,
    patch_bias,
    norm_gain,
    head_weight,
    head_bias,
    head_out,
    hidden_state,
    group_gain,
    group_shift,
    out_weight,
    inner_weight,
):
    devices = lax.axis_size("row")
    position = lax.axis_index("row")
    per_frame = devices // FRAMES
    slot = position // per_frame
    height = frames.shape[1]
    strip = frames.shape[2]
    own_rows = hidden_state.shape[0]
    frame_width = hidden_state.shape[2]
    tokens = to_tokens(frames)
    embedded = jnp.dot(tokens, patch_weight, preferred_element_type=jnp.float32) + patch_bias
    centred = embedded - jnp.mean(embedded, axis=1, keepdims=True)
    inv_spread = lax.rsqrt(jnp.mean(centred * centred, axis=1, keepdims=True) + eps_norm)
    normed = centred * inv_spread
    slot_mask = (jnp.arange(FRAMES, dtype=jnp.int32) == slot).astype(jnp.float32)
    partial_pool = slot_mask[:, None] * jnp.sum(normed * norm_gain, axis=0)[None, :]
    grouped = hidden_state.reshape(own_rows, FRAMES, frame_width, GROUPS, -1)
    first_sum = jnp.sum(grouped, axis=(0, 1, 2, 4), dtype=jnp.float32)
    second_sum = jnp.sum(jnp.square(grouped.astype(jnp.float32)), axis=(0, 1, 2, 4))
    pooled_sum, first_total, second_total = lax.psum((partial_pool, first_sum, second_sum), "row")
    frame_tokens = height // PATCH * (strip * per_frame // PATCH)
    pooled = pooled_sum / frame_tokens
    head_full = head_weight.astype(jnp.float32)
    before = jnp.dot(pooled, head_full, precision=lax.Precision.HIGHEST) + head_bias
    pulled = jnp.dot(head_out * silu_slope(before), head_full.T, precision=lax.Precision.HIGHEST)
    picked = jnp.sum((picks[:, None] == frame_owner[None, :]).astype(jnp.float32), axis=0)
    slot_grad = jnp.dot(slot_mask * picked, pulled, precision=lax.Precision.HIGHEST)
    scaled = norm_gain * slot_grad
    token_grad = inv_spread * (
        scaled - jnp.mean(scaled) - normed * jnp.mean(scaled * normed, axis=1, keepdims=True)
    )
    patch_grad = lax.dot_general(
        token_grad.astype(jnp.bfloat16),
        patch_weight,
        (((1,), (1,)), ((), ())),
        preferred_element_type=jnp.float32,
    )
    pixel_local = from_tokens(patch_grad, height, strip).astype(jnp.bfloat16)
    arrived = lax.all_to_all(pixel_local, "row", split_axis=1, concat_axis=2, tiled=True)
    by_slot = arrived.reshape(3, own_rows, FRAMES, frame_width)
    owner_table = (frame_owner[:, None] == jnp.arange(FRAMES, dtype=jnp.int32)[None, :]).astype(
        jnp.bfloat16
    )
    ordered = jnp.einsum(
        "krbw,bf->krfw", by_slot, owner_table, preferred_element_type=jnp.float32
    ).astype(jnp.bfloat16)
    cell_total = own_rows * devices * FRAMES * frame_width * (hidden_state.shape[3] // GROUPS)
    group_mean = first_total / cell_total
    inverse = lax.rsqrt(second_total / cell_total - group_mean * group_mean + eps_norm)
    pixel_padded = extended(ordered, (("row", 1),), 1)
    slope_in = pixel_back(pixel_padded, out_weight, own_rows)
    state_grad = group_back(
        hidden_state, slope_in, group_mean, inverse, group_gain, group_shift, cell_total
    )
    grad_padded = extended(state_grad, (("row", 0),), 1)
    return inner_back(grad_padded, inner_weight, own_rows).astype(jnp.bfloat16)


def split_rows(row):
    high = row.astype(jnp.bfloat16).astype(jnp.float32)
    rest = row - high
    middle = rest.astype(jnp.bfloat16).astype(jnp.float32)
    low = rest - middle
    index = lax.broadcasted_iota(jnp.int32, (8, row.shape[1]), 0)
    stacked = jnp.where(
        index == 0, high, jnp.where(index == 1, middle, jnp.where(index == 2, low, 0.0))
    )
    return stacked.astype(jnp.bfloat16)


def fused_kernel(
    n,
    frames_any,
    owner_any,
    picks_any,
    patch_any,
    patch_bias_any,
    norm_gain_any,
    head_any,
    head_bias_any,
    head_out_any,
    hidden_any,
    group_gain_any,
    group_shift_any,
    out_weight_any,
    inner_any,
    ready,
    normed_ref,
    terms,
    turned,
    frames,
    owner,
    picks,
    wide_rows,
    group_rows,
    out_weight,
    patch_w,
    head_w,
    hidden,
    inner_w,
    pixels,
    tokens,
    sent,
    arrived,
    by_frame,
    columns,
    band,
    slope,
    factor,
    sums_one,
    sums_two,
    local_sem,
    halo_send,
    halo_recv,
    send_sem,
    recv_sem,
):
    me = lax.axis_index("row")
    strip, height = frames.shape[1], frames.shape[2]
    patch_rows = height // PATCH
    own = hidden.shape[0] - 2
    wide = hidden.shape[2]
    channels = hidden.shape[3]
    line = FRAMES * wide
    per_group = channels // GROUPS
    cell_total = own * n * FRAMES * wide * per_group
    piece = 3 * strip
    half = arrived.shape[1]

    def peer(offset):
        target = me
        step = 1
        while step < n:
            if offset // step % 2:
                target = target + step * (1 - 2 * lax.rem(lax.div(me, step), 2))
            step *= 2
        return target

    farthest_first = range(n - 1, 0, -1)

    barrier = pltpu.get_barrier_semaphore()
    for offset in farthest_first:
        pl.semaphore_signal(barrier, inc=1, device_id={"row": peer(offset)}, device_id_type=MESH)

    load_frames = pltpu.make_async_copy(frames_any, frames, local_sem.at[0])
    load_hidden = pltpu.make_async_copy(hidden_any, hidden.at[pl.ds(1, own)], local_sem.at[1])
    load_patch = pltpu.make_async_copy(patch_any, patch_w, local_sem.at[2])
    load_head = pltpu.make_async_copy(head_any, head_w, local_sem.at[3])
    load_inner = pltpu.make_async_copy(inner_any, inner_w, local_sem.at[4])
    load_out = pltpu.make_async_copy(out_weight_any, out_weight, local_sem.at[5])
    load_owner = pltpu.make_async_copy(owner_any, owner, local_sem.at[6])
    load_picks = pltpu.make_async_copy(picks_any, picks, local_sem.at[7])
    load_wide = [
        pltpu.make_async_copy(source, wide_rows.at[index], local_sem.at[8])
        for index, source in enumerate((patch_bias_any, norm_gain_any, head_bias_any, head_out_any))
    ]
    load_group = [
        pltpu.make_async_copy(source, group_rows.at[index], local_sem.at[9])
        for index, source in enumerate((group_gain_any, group_shift_any))
    ]
    load_frames.start()
    load_hidden.start()
    load_patch.start()
    for load in load_wide + load_group:
        load.start()
    load_owner.start()
    load_picks.start()
    load_out.start()
    load_head.start()
    load_inner.start()

    group_row = lax.broadcasted_iota(jnp.int32, (channels, channels), 0) // per_group
    group_col = lax.broadcasted_iota(jnp.int32, (channels, channels), 1) // per_group
    same_group = (group_row == group_col).astype(jnp.bfloat16)
    eight = lax.broadcasted_iota(jnp.int32, (8, channels), 0)
    spot = lax.broadcasted_iota(jnp.int32, (2, channels), 0)

    def group_sums(first, second):
        part = lax.rem(eight, 4)
        row = jnp.where(eight < 4, first, second)
        high = row.astype(jnp.bfloat16).astype(jnp.float32)
        rest = row - high
        middle = rest.astype(jnp.bfloat16).astype(jnp.float32)
        stacked = jnp.where(
            part == 0, high, jnp.where(part == 1, middle, jnp.where(part == 2, rest - middle, 0.0))
        )
        summed = jnp.dot(
            stacked.astype(jnp.bfloat16), same_group, preferred_element_type=jnp.float32
        )
        return (
            jnp.sum(summed[0:4], axis=0, keepdims=True),
            jnp.sum(summed[4:8], axis=0, keepdims=True),
        )

    def over_devices(buffer):
        blocks = [buffer[slot] for slot in range(n)]
        while len(blocks) > 1:
            blocks = [
                blocks[at] + blocks[at + 1] if at + 1 < len(blocks) else blocks[at]
                for at in range(0, len(blocks), 2)
            ]
        return blocks[0]

    load_frames.wait()
    for colour in range(3):
        pixels[colour] = frames[colour].astype(jnp.float32).T
    tokens[...] = jnp.zeros_like(tokens)
    for colour in range(3):
        for line_in in range(PATCH):
            at = (colour * PATCH + line_in) * PATCH
            tokens[0:patch_rows, at : at + PATCH] = pixels[
                colour, pl.ds(line_in, patch_rows, stride=PATCH), :
            ]
    sent[...] = jnp.zeros_like(sent)

    load_hidden.wait()
    first = jnp.zeros((1, channels), jnp.float32)
    second = jnp.zeros((1, channels), jnp.float32)
    for row in range(own):
        state = hidden[1 + row].reshape(line, channels).astype(jnp.float32)
        first = first + jnp.sum(state, axis=0, keepdims=True)
        second = second + jnp.sum(state * state, axis=0, keepdims=True)
    first, second = group_sums(first, second)
    sums_one[me] = jnp.where(spot == 0, first, second)

    pltpu.make_async_copy(wide_rows, wide_rows, local_sem.at[8]).wait()
    pltpu.make_async_copy(group_rows, group_rows, local_sem.at[9]).wait()
    load_owner.wait()
    load_picks.wait()
    load_out.wait()
    load_patch.wait()
    embedded = (
        jnp.dot(
            tokens[...].astype(jnp.bfloat16), patch_w[...], preferred_element_type=jnp.float32
        )
        + wide_rows[0]
    )
    centred = embedded - jnp.mean(embedded, axis=1, keepdims=True)
    inv_spread = lax.rsqrt(jnp.mean(centred * centred, axis=1, keepdims=True) + eps_norm)
    normed = centred * inv_spread
    gain = wide_rows[1]
    pooled = jnp.sum((normed * gain)[0:patch_rows], axis=0, keepdims=True) / patch_rows
    load_head.wait()
    before = (
        jnp.sum(
            jnp.dot(split_rows(pooled), head_w[...], preferred_element_type=jnp.float32),
            axis=0,
            keepdims=True,
        )
        + wide_rows[2]
    )
    pulled = jnp.sum(
        lax.dot_general(
            split_rows(wide_rows[3] * silu_slope(before)),
            head_w[...],
            (((1,), (1,)), ((), ())),
            preferred_element_type=jnp.float32,
        ),
        axis=0,
        keepdims=True,
    )
    mine = owner[me]
    picked = jnp.float32(0.0)
    for pick in range(picks.shape[0]):
        picked = picked + jnp.where(picks[pick] == mine, jnp.float32(1.0), jnp.float32(0.0))
    scaled = gain * (picked * pulled)
    token_grad = inv_spread * (
        scaled
        - jnp.mean(scaled, axis=1, keepdims=True)
        - normed * jnp.mean(scaled * normed, axis=1, keepdims=True)
    )
    patch_grad = lax.dot_general(
        token_grad.astype(jnp.bfloat16),
        patch_w[...],
        (((1,), (1,)), ((), ())),
        preferred_element_type=jnp.float32,
    )
    patch_grad = patch_grad.astype(jnp.bfloat16).astype(jnp.float32)
    for line_in in range(PATCH):
        joined = jnp.concatenate(
            [
                patch_grad[:, (colour * PATCH + line_in) * PATCH : (colour * PATCH + line_in + 1) * PATCH]
                for colour in range(3)
            ],
            axis=1,
        )
        for patch_row in range(patch_rows):
            at = 2 + patch_row * PATCH + line_in
            sent[at, :, 0:piece] = joined[patch_row : patch_row + 1]
            if at >= half:
                sent[at - half, :, 64 : 64 + piece] = joined[patch_row : patch_row + 1]

    pl.semaphore_wait(barrier, n - 1)

    def broadcast(buffer, kind):
        for offset in farthest_first:
            pltpu.make_async_remote_copy(
                src_ref=buffer.at[me],
                dst_ref=buffer.at[me],
                send_sem=send_sem.at[kind],
                recv_sem=recv_sem.at[kind],
                device_id={"row": peer(offset)},
                device_id_type=MESH,
            ).start()

    def from_peers(buffer, kind):
        others = buffer.at[pl.ds(0, n - 1)]
        pltpu.make_async_copy(others, others, recv_sem.at[kind]).wait()

    def to_peers(buffer, kind):
        others = buffer.at[pl.ds(0, n - 1)]
        pltpu.make_async_copy(others, others, send_sem.at[kind]).wait()

    for offset in farthest_first:
        target = peer(offset)
        pltpu.make_async_remote_copy(
            src_ref=sent.at[pl.ds(target * own, half)],
            dst_ref=arrived.at[me],
            send_sem=send_sem.at[1],
            recv_sem=recv_sem.at[1],
            device_id={"row": target},
            device_id_type=MESH,
        ).start()
    broadcast(sums_one, 0)
    to_right = pltpu.make_async_remote_copy(
        src_ref=hidden_any.at[pl.ds(own - 1, 1)],
        dst_ref=hidden.at[pl.ds(0, 1)],
        send_sem=halo_send.at[0],
        recv_sem=halo_recv.at[0],
        device_id={"row": lax.rem(me + 1, n)},
        device_id_type=MESH,
    )
    to_left = pltpu.make_async_remote_copy(
        src_ref=hidden_any.at[pl.ds(0, 1)],
        dst_ref=hidden.at[pl.ds(own + 1, 1)],
        send_sem=halo_send.at[1],
        recv_sem=halo_recv.at[1],
        device_id={"row": lax.rem(me + n - 1, n)},
        device_id_type=MESH,
    )

    @pl.when(me < n - 1)
    def _():
        to_right.start()

    @pl.when(me > 0)
    def _():
        to_left.start()

    @pl.when(me == 0)
    def _():
        hidden[0] = jnp.zeros(hidden.shape[1:], hidden.dtype)

    @pl.when(me == n - 1)
    def _():
        hidden[own + 1] = jnp.zeros(hidden.shape[1:], hidden.dtype)

    arrived[me] = sent[pl.ds(me * own, half)]

    column = lax.broadcasted_iota(jnp.int32, (wide, channels), 0)
    for row_tap in range(3):
        for time_tap in range(3):
            taps = [out_weight[time_tap, row_tap, col_tap].astype(jnp.float32) for col_tap in range(3)]
            for colour in range(3):
                at = ((row_tap * 3 + time_tap) * 3 + colour) * wide
                spread = [
                    jnp.broadcast_to(tap[colour : colour + 1], (wide, channels)) for tap in taps
                ]
                for w in range(wide):
                    block = jnp.where(
                        column == w + 1,
                        spread[0],
                        jnp.where(
                            column == w, spread[1], jnp.where(column == w - 1, spread[2], 0.0)
                        ),
                    )
                    band[at : at + wide, w * channels : (w + 1) * channels] = block.astype(
                        jnp.bfloat16
                    )
    depth = band.shape[0]
    if depth > 27 * wide:
        band[27 * wide :, :] = jnp.zeros((depth - 27 * wide, wide * channels), jnp.bfloat16)
    columns[...] = jnp.zeros_like(columns)
    by_frame[...] = jnp.zeros_like(by_frame)

    slot_of = []
    for frame in range(FRAMES):
        found = jnp.int32(0)
        for slot in range(n):
            found = jnp.where(owner[slot] == frame, jnp.int32(slot), found)
        slot_of.append(found)

    from_peers(sums_one, 0)
    from_peers(arrived, 1)
    means = over_devices(sums_one) / cell_total
    group_mean = means[0:1]
    inverse = lax.rsqrt(means[1:2] - group_mean * group_mean + eps_norm)
    group_gain = group_rows[0]
    group_shift = group_rows[1]

    def state_terms(row):
        state = hidden[row].reshape(line, channels).astype(jnp.float32)
        normed_state = (state - group_mean) * inverse
        normed_ref[row * line : (row + 1) * line] = normed_state
        affine = normed_state * group_gain + group_shift
        factor[row * line : (row + 1) * line] = silu_slope(affine) * group_gain

    def pixel_taps(row):
        for row_tap in range(3):
            for time_tap in range(3):
                at = (row_tap * 3 + time_tap) * piece
                source = row - row_tap + 2
                lane = source // half * 64
                columns[row * FRAMES : (row + 1) * FRAMES, at : at + piece] = by_frame[
                    source % half, 2 - time_tap : 2 - time_tap + FRAMES, lane : lane + piece
                ]

    for frame in range(FRAMES):
        for row in range(half):
            by_frame[row, frame : frame + 1, :] = arrived[slot_of[frame], row]
    for row in range(1, own + 1):
        pixel_taps(row)
        state_terms(row)
    left = columns[FRAMES : (own + 1) * FRAMES].astype(jnp.bfloat16)
    first = jnp.zeros((1, channels), jnp.float32)
    second = jnp.zeros((1, channels), jnp.float32)
    for w in range(0, wide, 2):
        both = jnp.dot(
            left,
            band[:, w * channels : (w + 2) * channels],
            preferred_element_type=jnp.float32,
        )
        for side in range(2):
            part = pl.ds(line + w + side, own * FRAMES, stride=wide)
            upstream = both[:, side * channels : (side + 1) * channels] * factor[part]
            slope[part] = upstream
            first = first + jnp.sum(upstream, axis=0, keepdims=True)
            second = second + jnp.sum(upstream * normed_ref[part], axis=0, keepdims=True)
    sums_two[me] = jnp.where(spot == 0, first, second)
    broadcast(sums_two, 2)


    @pl.when(me < n - 1)
    def _():
        to_right.wait_send()
        to_left.wait_recv()

    @pl.when(me > 0)
    def _():
        to_left.wait_send()
        to_right.wait_recv()

    for row in (0, own + 1):
        pixel_taps(row)
        state_terms(row)
    left = jnp.concatenate(
        [columns[0:FRAMES], columns[(own + 1) * FRAMES : (own + 2) * FRAMES]], axis=0
    ).astype(jnp.bfloat16)
    for w in range(0, wide, 2):
        both = jnp.dot(
            left,
            band[:, w * channels : (w + 2) * channels],
            preferred_element_type=jnp.float32,
        )
        for side in range(2):
            for index, row in enumerate((0, own + 1)):
                part = pl.ds(row * line + w + side, FRAMES, stride=wide)
                slope[part] = (
                    both[
                        index * FRAMES : (index + 1) * FRAMES,
                        side * channels : (side + 1) * channels,
                    ]
                    * factor[part]
                )

    load_inner.wait()
    for row_tap in range(3):
        for col_tap in range(3):
            part = pl.ds(col_tap * channels, channels)
            for time_tap in range(3):
                block = inner_w[time_tap, row_tap, col_tap].T
                turned[row_tap, 2 - time_tap, part, 0:channels] = block
                turned[row_tap, 3 - time_tap, part, channels:] = block
            empty = jnp.zeros((channels, channels), jnp.bfloat16)
            turned[row_tap, 3, part, 0:channels] = empty
            turned[row_tap, 0, part, channels:] = empty
    for row in range(own + 2):
        part = pl.ds(row * line, line)
        ready[part] = slope[part] * inverse

    to_peers(sums_one, 0)
    to_peers(arrived, 1)
    to_peers(sums_two, 2)
    from_peers(sums_two, 2)
    total = over_devices(sums_two)
    first, second = group_sums(total[0:1], total[1:2])
    terms[0:2] = jnp.where(spot == 0, first, second) * (inverse / cell_total)


def last_kernel(n, ready, normed_ref, terms, turned, out_any, windows, out, out_sem):
    me = lax.axis_index("row")
    own = out.shape[0]
    wide = out.shape[3]
    channels = out.shape[4]
    line = FRAMES * wide
    windows[:, FRAMES // 2] = jnp.zeros((own + 2, 2, wide, 3 * channels), jnp.bfloat16)
    position = lax.rem(lax.broadcasted_iota(jnp.int32, (line, channels), 0), wide)
    for row in range(own + 2):
        part = pl.ds(row * line, line)
        state_grad = ready[part] - terms[0:1] - normed_ref[part] * terms[1:2]
        if row == 0:
            state_grad = jnp.where(me > 0, state_grad, 0.0)
        if row == own + 1:
            state_grad = jnp.where(me < n - 1, state_grad, 0.0)
        after = jnp.where(position == wide - 1, 0.0, pltpu.roll(state_grad, line - 1, 0))
        earlier = jnp.where(position == 0, 0.0, pltpu.roll(state_grad, 1, 0))
        for col_tap, shifted in enumerate((after, state_grad, earlier)):
            windows[row, 0 : FRAMES // 2, :, :, col_tap * channels : (col_tap + 1) * channels] = (
                shifted.astype(jnp.bfloat16).reshape(FRAMES // 2, 2, wide, channels)
            )
    for row in range(own):
        taken = jnp.concatenate(
            [
                windows[
                    row + 2 - row_tap, ahead // 2 : ahead // 2 + FRAMES // 2, ahead % 2
                ].reshape(line // 2, 3 * channels)
                for row_tap in range(3)
                for ahead in range(4)
            ],
            axis=1,
        )
        summed = jnp.dot(
            taken,
            turned[...].reshape(12 * 3 * channels, 2 * channels),
            preferred_element_type=jnp.float32,
        )
        for side in range(2):
            out[row, :, side] = (
                summed[:, side * channels : (side + 1) * channels]
                .reshape(FRAMES // 2, wide, channels)
                .astype(jnp.bfloat16)
            )
        copy = pltpu.make_async_copy(out.at[row], out_any.at[row], out_sem)
        copy.start()
    pltpu.make_async_copy(out, out_any, out_sem).wait()


def one_frame_each(
    frames,
    frame_owner,
    picks,
    patch_weight,
    patch_bias,
    norm_gain,
    head_weight,
    head_bias,
    head_out,
    hidden_state,
    group_gain,
    group_shift,
    out_weight,
    inner_weight,
):
    n = lax.axis_size("row")
    own, frame_count, wide, channels = hidden_state.shape
    height, strip = frames.shape[1:]
    pix, width = patch_weight.shape
    depth = -(-27 * wide // 128) * 128
    cells = (own + 2) * frame_count * wide
    f32, bf16 = jnp.float32, jnp.bfloat16
    vmem = pl.BlockSpec(memory_space=pltpu.VMEM)
    dma = pltpu.SemaphoreType.DMA
    passed = [
        pltpu.VMEM((cells, channels), f32),
        pltpu.VMEM((cells, channels), f32),
        pltpu.VMEM((8, channels), f32),
        pltpu.VMEM((3, 4, 3 * channels, 2 * channels), bf16),
    ]
    kept = pl.pallas_call(
        functools.partial(fused_kernel, n),
        out_shape=passed,
        in_specs=[pl.BlockSpec(memory_space=pltpu.HBM)] * 14,
        out_specs=[vmem] * 4,
        scratch_shapes=[
            pltpu.VMEM((3, strip, height), bf16),
            pltpu.SMEM(frame_owner.shape, jnp.int32),
            pltpu.SMEM(picks.shape, jnp.int32),
            pltpu.VMEM((4, 1, width), f32),
            pltpu.VMEM((2, 1, channels), f32),
            pltpu.VMEM(out_weight.shape, bf16),
            pltpu.VMEM((pix, width), bf16),
            pltpu.VMEM(head_weight.shape, bf16),
            pltpu.VMEM((own + 2, frame_count, wide, channels), bf16),
            pltpu.VMEM(inner_weight.shape, bf16),
            pltpu.VMEM(frames.shape, f32),
            pltpu.VMEM((-(-(height // PATCH) // 8) * 8, pix), f32),
            pltpu.VMEM((height + 4, 1, 128), f32),
            pltpu.VMEM((n, (own + 5) // 2, 1, 128), f32),
            pltpu.VMEM(((own + 5) // 2, frame_count + 8, 128), f32),
            pltpu.VMEM(((own + 2) * frame_count, depth), f32),
            pltpu.VMEM((depth, wide * channels), bf16),
            pltpu.VMEM((cells, channels), f32),
            pltpu.VMEM((cells, channels), f32),
            pltpu.VMEM((n, 2, channels), f32),
            pltpu.VMEM((n, 2, channels), f32),
            dma((10,)),
            dma((2,)),
            dma((2,)),
            dma((3,)),
            dma((3,)),
        ],
        compiler_params=pltpu.CompilerParams(
            collective_id=0, has_side_effects=True, vmem_limit_bytes=32 << 20
        ),
    )(
        *(
            pltpu.with_memory_space_constraint(array, pltpu.HBM)
            for array in (
                frames.transpose(0, 2, 1),
                frame_owner,
                picks,
                patch_weight,
                patch_bias[None],
                norm_gain[None],
                head_weight,
                head_bias[None],
                head_out[None],
                hidden_state,
                group_gain[None],
                group_shift[None],
                out_weight,
                inner_weight,
            )
        )
    )
    out_shape = (own, frame_count // 2, 2, wide, channels)
    return pl.pallas_call(
        functools.partial(last_kernel, n),
        out_shape=jax.ShapeDtypeStruct(out_shape, bf16),
        in_specs=[vmem] * 4,
        out_specs=pl.BlockSpec(memory_space=pltpu.HBM),
        scratch_shapes=[
            pltpu.VMEM((own + 2, frame_count // 2 + 1, 2, wide, 3 * channels), bf16),
            pltpu.VMEM(out_shape, bf16),
            dma,
        ],
        compiler_params=pltpu.CompilerParams(vmem_limit_bytes=32 << 20),
    )(*kept).reshape(hidden_state.shape)


def solution(mesh):
    body = one_frame_each if mesh.shape["row"] == FRAMES else per_device
    return jax.shard_map(
        body,
        mesh=mesh,
        in_specs=(
            P(None, None, ("clip", "row")),
            P("clip"),
            P("clip"),
            P(),
            P(),
            P(),
            P(),
            P(),
            P(),
            P(("clip", "row"), None, None, None),
            P(),
            P(),
            P(),
            P(),
        ),
        out_specs=P(("clip", "row"), None, None, None),
        check_vma=False,
    )
```

```python
import functools

import jax
import jax.numpy as jnp
from jax import lax
from jax.experimental import pallas as pl
from jax.experimental.pallas import tpu as pltpu
from jax.sharding import PartitionSpec as P

PATCH = 16
GROUPS = 32
FRAMES = 16


eps_norm = 1e-06
MESH = pl.DeviceIdType.MESH


def extended(block, sides, width):
    for axis, dim in sides:
        count = lax.axis_size(axis)
        forward = [(i, i + 1) for i in range(count - 1)]
        backward = [(target, source) for source, target in forward]
        low = lax.ppermute(
            lax.slice_in_dim(block, block.shape[dim] - width, None, axis=dim), axis, forward
        )
        high = lax.ppermute(lax.slice_in_dim(block, 0, width, axis=dim), axis, backward)
        block = jnp.concatenate([low, block, high], axis=dim)
    return block


def silu_slope(values):
    sigmoid = jax.nn.sigmoid(values)
    return sigmoid * (1.0 + values * (1.0 - sigmoid))


def to_tokens(pixels):
    channels, height, columns = pixels.shape
    shaped = pixels.reshape(channels, height // PATCH, PATCH, columns // PATCH, PATCH)
    return shaped.transpose(1, 3, 0, 2, 4).reshape(
        height // PATCH * (columns // PATCH), channels * PATCH * PATCH
    )


def from_tokens(token_grads, height, columns):
    shaped = token_grads.reshape(height // PATCH, columns // PATCH, 3, PATCH, PATCH)
    return shaped.transpose(2, 0, 3, 1, 4).reshape(3, height, columns)


def pixel_back(padded, out_weight, amount):
    frame_count = padded.shape[2]
    columns = padded.shape[3]
    widened = jnp.pad(padded, ((0, 0), (0, 0), (0, 2), (1, 1)))
    windows = []
    for time_tap in range(3):
        for row_tap in range(3):
            for col_tap in range(3):
                windows.append(
                    widened[
                        :,
                        2 - row_tap : 2 - row_tap + amount,
                        2 - time_tap : 2 - time_tap + frame_count,
                        2 - col_tap : 2 - col_tap + columns,
                    ]
                )
    stacked = jnp.stack(windows, 0).reshape(27 * 3, amount * frame_count * columns)
    kernel = out_weight.reshape(27 * 3, out_weight.shape[4])
    summed = lax.dot_general(
        stacked, kernel, (((0,), (0,)), ((), ())), preferred_element_type=jnp.float32
    )
    return summed.reshape(amount, frame_count, columns, out_weight.shape[4])


def inner_back(padded, inner_weight, amount):
    frame_count = padded.shape[1]
    columns = padded.shape[2]
    channel_count = padded.shape[3]
    widened = jnp.pad(padded, ((0, 0), (0, 2), (1, 1), (0, 0)))
    summed = jnp.zeros((amount * frame_count * columns, inner_weight.shape[3]), jnp.float32)
    for time_tap in range(3):
        windows = []
        for row_tap in range(3):
            for col_tap in range(3):
                windows.append(
                    widened[
                        2 - row_tap : 2 - row_tap + amount,
                        2 - time_tap : 2 - time_tap + frame_count,
                        2 - col_tap : 2 - col_tap + columns,
                        :,
                    ]
                )
        joined = jnp.concatenate(windows, axis=3).reshape(
            amount * frame_count * columns, 9 * channel_count
        )
        kernel = jnp.transpose(inner_weight[time_tap], (0, 1, 3, 2)).reshape(
            9 * channel_count, inner_weight.shape[3]
        )
        summed = summed + jnp.dot(joined, kernel, preferred_element_type=jnp.float32)
    return summed.reshape(amount, frame_count, columns, inner_weight.shape[3])


def group_back(state_rows, slope_in, group_mean, inverse, group_gain, group_shift, cell_total):
    grouped = state_rows.astype(jnp.float32).reshape(state_rows.shape[:3] + (GROUPS, -1))
    gain_table = group_gain.reshape(GROUPS, -1)
    shift_table = group_shift.reshape(GROUPS, -1)
    normed_state = (grouped - group_mean[:, None]) * inverse[:, None]
    affine = normed_state * gain_table + shift_table
    upstream = slope_in.reshape(grouped.shape) * silu_slope(affine) * gain_table
    group_terms = lax.psum(
        (jnp.sum(upstream, axis=(0, 1, 2, 4)), jnp.sum(upstream * normed_state, axis=(0, 1, 2, 4))),
        "row",
    )
    first_part = group_terms[0] / cell_total
    second_part = group_terms[1] / cell_total
    state_grad = (upstream - first_part[:, None] - normed_state * second_part[:, None]) * inverse[
        :, None
    ]
    return state_grad.reshape(state_rows.shape).astype(jnp.bfloat16)


def per_device(
    frames,
    frame_owner,
    picks,
    patch_weight,
    patch_bias,
    norm_gain,
    head_weight,
    head_bias,
    head_out,
    hidden_state,
    group_gain,
    group_shift,
    out_weight,
    inner_weight,
):
    devices = lax.axis_size("row")
    position = lax.axis_index("row")
    per_frame = devices // FRAMES
    slot = position // per_frame
    height = frames.shape[1]
    strip = frames.shape[2]
    own_rows = hidden_state.shape[0]
    frame_width = hidden_state.shape[2]
    tokens = to_tokens(frames)
    embedded = jnp.dot(tokens, patch_weight, preferred_element_type=jnp.float32) + patch_bias
    centred = embedded - jnp.mean(embedded, axis=1, keepdims=True)
    inv_spread = lax.rsqrt(jnp.mean(centred * centred, axis=1, keepdims=True) + eps_norm)
    normed = centred * inv_spread
    slot_mask = (jnp.arange(FRAMES, dtype=jnp.int32) == slot).astype(jnp.float32)
    partial_pool = slot_mask[:, None] * jnp.sum(normed * norm_gain, axis=0)[None, :]
    grouped = hidden_state.reshape(own_rows, FRAMES, frame_width, GROUPS, -1)
    first_sum = jnp.sum(grouped, axis=(0, 1, 2, 4), dtype=jnp.float32)
    second_sum = jnp.sum(jnp.square(grouped.astype(jnp.float32)), axis=(0, 1, 2, 4))
    pooled_sum, first_total, second_total = lax.psum((partial_pool, first_sum, second_sum), "row")
    frame_tokens = height // PATCH * (strip * per_frame // PATCH)
    pooled = pooled_sum / frame_tokens
    head_full = head_weight.astype(jnp.float32)
    before = jnp.dot(pooled, head_full, precision=lax.Precision.HIGHEST) + head_bias
    pulled = jnp.dot(head_out * silu_slope(before), head_full.T, precision=lax.Precision.HIGHEST)
    picked = jnp.sum((picks[:, None] == frame_owner[None, :]).astype(jnp.float32), axis=0)
    slot_grad = jnp.dot(slot_mask * picked, pulled, precision=lax.Precision.HIGHEST)
    scaled = norm_gain * slot_grad
    token_grad = inv_spread * (
        scaled - jnp.mean(scaled) - normed * jnp.mean(scaled * normed, axis=1, keepdims=True)
    )
    patch_grad = lax.dot_general(
        token_grad.astype(jnp.bfloat16),
        patch_weight,
        (((1,), (1,)), ((), ())),
        preferred_element_type=jnp.float32,
    )
    pixel_local = from_tokens(patch_grad, height, strip).astype(jnp.bfloat16)
    arrived = lax.all_to_all(pixel_local, "row", split_axis=1, concat_axis=2, tiled=True)
    by_slot = arrived.reshape(3, own_rows, FRAMES, frame_width)
    owner_table = (frame_owner[:, None] == jnp.arange(FRAMES, dtype=jnp.int32)[None, :]).astype(
        jnp.bfloat16
    )
    ordered = jnp.einsum(
        "krbw,bf->krfw", by_slot, owner_table, preferred_element_type=jnp.float32
    ).astype(jnp.bfloat16)
    cell_total = own_rows * devices * FRAMES * frame_width * (hidden_state.shape[3] // GROUPS)
    group_mean = first_total / cell_total
    inverse = lax.rsqrt(second_total / cell_total - group_mean * group_mean + eps_norm)
    pixel_padded = extended(ordered, (("row", 1),), 1)
    slope_in = pixel_back(pixel_padded, out_weight, own_rows)
    state_grad = group_back(
        hidden_state, slope_in, group_mean, inverse, group_gain, group_shift, cell_total
    )
    grad_padded = extended(state_grad, (("row", 0),), 1)
    return inner_back(grad_padded, inner_weight, own_rows).astype(jnp.bfloat16)


def split_rows(row):
    high = row.astype(jnp.bfloat16).astype(jnp.float32)
    rest = row - high
    middle = rest.astype(jnp.bfloat16).astype(jnp.float32)
    low = rest - middle
    index = lax.broadcasted_iota(jnp.int32, (8, row.shape[1]), 0)
    stacked = jnp.where(
        index == 0, high, jnp.where(index == 1, middle, jnp.where(index == 2, low, 0.0))
    )
    return stacked.astype(jnp.bfloat16)


def fused_kernel(
    n,
    frames_any,
    owner_any,
    picks_any,
    patch_any,
    patch_bias_any,
    norm_gain_any,
    head_any,
    head_bias_any,
    head_out_any,
    hidden_any,
    group_gain_any,
    group_shift_any,
    out_weight_any,
    inner_any,
    ready,
    normed_ref,
    terms,
    turned,
    frames,
    owner,
    picks,
    wide_rows,
    group_rows,
    out_weight,
    patch_w,
    head_w,
    hidden,
    inner_w,
    pixels,
    tokens,
    sent,
    arrived,
    by_frame,
    columns,
    taps,
    band,
    slope,
    cells,
    factor,
    normed_cells,
    sums_one,
    sums_two,
    local_sem,
    halo_send,
    halo_recv,
    send_sem,
    recv_sem,
):
    me = lax.axis_index("row")
    strip, height = frames.shape[1], frames.shape[2]
    patch_rows = height // PATCH
    own = hidden.shape[0] - 2
    wide = hidden.shape[2]
    channels = hidden.shape[3]
    line = FRAMES * wide
    pitch = wide + 1
    per_group = channels // GROUPS
    cell_total = own * n * FRAMES * wide * per_group
    window = wide // 2 + 1
    piece = 3 * window
    slot_lanes = 64
    half = arrived.shape[1]

    def peer(offset):
        target = me
        step = 1
        while step < n:
            if offset // step % 2:
                target = target + step * (1 - 2 * lax.rem(lax.div(me, step), 2))
            step *= 2
        return target

    farthest_first = range(n - 1, 0, -1)

    barrier = pltpu.get_barrier_semaphore()
    for offset in farthest_first:
        pl.semaphore_signal(barrier, inc=1, device_id={"row": peer(offset)}, device_id_type=MESH)

    load_frames = pltpu.make_async_copy(frames_any, frames, local_sem.at[0])
    load_hidden = pltpu.make_async_copy(hidden_any, hidden.at[pl.ds(1, own)], local_sem.at[1])
    pix, width = patch_w.shape
    third, part_rows = pix // 3, width // 2
    load_patch = [
        pltpu.make_async_copy(
            patch_any.at[pl.ds(part * third, third)],
            patch_w.at[pl.ds(part * third, third)],
            local_sem.at[10 + part],
        )
        for part in range(3)
    ]
    load_head = [
        pltpu.make_async_copy(
            head_any.at[pl.ds(part * part_rows, part_rows)],
            head_w.at[pl.ds(part * part_rows, part_rows)],
            local_sem.at[13 + part],
        )
        for part in range(2)
    ]
    load_inner = pltpu.make_async_copy(inner_any, inner_w, local_sem.at[4])
    load_out = pltpu.make_async_copy(out_weight_any, out_weight, local_sem.at[5])
    load_owner = pltpu.make_async_copy(owner_any, owner, local_sem.at[6])
    load_picks = pltpu.make_async_copy(picks_any, picks, local_sem.at[7])
    load_wide = [
        pltpu.make_async_copy(source, wide_rows.at[index], local_sem.at[8])
        for index, source in enumerate((patch_bias_any, norm_gain_any, head_bias_any, head_out_any))
    ]
    load_group = [
        pltpu.make_async_copy(source, group_rows.at[index], local_sem.at[9])
        for index, source in enumerate((group_gain_any, group_shift_any))
    ]
    load_frames.start()
    load_hidden.start()
    for load in load_patch:
        load.start()
    for load in load_wide:
        load.start()
    for load in load_head:
        load.start()
    load_owner.start()
    load_picks.start()
    for load in load_group:
        load.start()
    load_out.start()
    load_inner.start()

    group_row = lax.broadcasted_iota(jnp.int32, (channels, channels), 0) // per_group
    group_col = lax.broadcasted_iota(jnp.int32, (channels, channels), 1) // per_group
    same_group = (group_row == group_col).astype(jnp.bfloat16)
    eight = lax.broadcasted_iota(jnp.int32, (8, channels), 0)
    spot = lax.broadcasted_iota(jnp.int32, (2, channels), 0)

    def group_sums(first, second):
        part = lax.rem(eight, 4)
        row = jnp.where(eight < 4, first, second)
        high = row.astype(jnp.bfloat16).astype(jnp.float32)
        rest = row - high
        middle = rest.astype(jnp.bfloat16).astype(jnp.float32)
        stacked = jnp.where(
            part == 0, high, jnp.where(part == 1, middle, jnp.where(part == 2, rest - middle, 0.0))
        )
        summed = jnp.dot(
            stacked.astype(jnp.bfloat16), same_group, preferred_element_type=jnp.float32
        )
        return (
            jnp.sum(summed[0:4], axis=0, keepdims=True),
            jnp.sum(summed[4:8], axis=0, keepdims=True),
        )

    def tree_sum(blocks):
        while len(blocks) > 1:
            blocks = [
                blocks[at] + blocks[at + 1] if at + 1 < len(blocks) else blocks[at]
                for at in range(0, len(blocks), 2)
            ]
        return blocks[0]

    def over_devices(buffer):
        return tree_sum([buffer[slot] for slot in range(n)])

    load_frames.wait()
    for colour in range(3):
        pixels[colour] = frames[colour].astype(jnp.float32).T
    tokens[...] = jnp.zeros_like(tokens)
    for colour in range(3):
        for line_in in range(PATCH):
            at = (colour * PATCH + line_in) * PATCH
            tokens[0:patch_rows, at : at + PATCH] = pixels[
                colour, pl.ds(line_in, patch_rows, stride=PATCH), :
            ]
    sent[...] = jnp.zeros_like(sent)

    load_hidden.wait()
    first = jnp.zeros((1, channels), jnp.float32)
    second = jnp.zeros((1, channels), jnp.float32)
    for row in range(own):
        state = hidden[1 + row].reshape(line, channels).astype(jnp.float32)
        first = first + jnp.sum(state, axis=0, keepdims=True)
        second = second + jnp.sum(state * state, axis=0, keepdims=True)
    first, second = group_sums(first, second)
    sums_one[me] = jnp.where(spot == 0, first, second)

    pltpu.make_async_copy(wide_rows, wide_rows, local_sem.at[8]).wait()
    embedded = wide_rows[0]
    for part in range(3):
        load_patch[part].wait()
        embedded = embedded + jnp.dot(
            tokens[:, part * third : (part + 1) * third].astype(jnp.bfloat16),
            patch_w[part * third : (part + 1) * third],
            preferred_element_type=jnp.float32,
        )
    centred = embedded - jnp.mean(embedded, axis=1, keepdims=True)
    inv_spread = lax.rsqrt(jnp.mean(centred * centred, axis=1, keepdims=True) + eps_norm)
    normed = centred * inv_spread
    gain = wide_rows[1]
    pooled = jnp.sum((normed * gain)[0:patch_rows], axis=0, keepdims=True) / patch_rows
    split_pool = split_rows(pooled)
    before = wide_rows[2]
    for part in range(2):
        load_head[part].wait()
        before = before + jnp.sum(
            jnp.dot(
                split_pool[:, part * part_rows : (part + 1) * part_rows],
                head_w[part * part_rows : (part + 1) * part_rows],
                preferred_element_type=jnp.float32,
            ),
            axis=0,
            keepdims=True,
        )
    pulled = jnp.sum(
        lax.dot_general(
            split_rows(wide_rows[3] * silu_slope(before)),
            head_w[...],
            (((1,), (1,)), ((), ())),
            preferred_element_type=jnp.float32,
        ),
        axis=0,
        keepdims=True,
    )
    load_owner.wait()
    load_picks.wait()
    mine = owner[me]
    picked = jnp.float32(0.0)
    for pick in range(picks.shape[0]):
        picked = picked + jnp.where(picks[pick] == mine, jnp.float32(1.0), jnp.float32(0.0))
    scaled = gain * (picked * pulled)
    token_grad = inv_spread * (
        scaled
        - jnp.mean(scaled, axis=1, keepdims=True)
        - normed * jnp.mean(scaled * normed, axis=1, keepdims=True)
    )
    patch_grad = lax.dot_general(
        token_grad.astype(jnp.bfloat16),
        patch_w[...],
        (((1,), (1,)), ((), ())),
        preferred_element_type=jnp.float32,
    )
    patch_grad = patch_grad.astype(jnp.bfloat16).astype(jnp.float32)
    for line_in in range(PATCH):
        lines = [
            patch_grad[:, (colour * PATCH + line_in) * PATCH : (colour * PATCH + line_in + 1) * PATCH]
            for colour in range(3)
        ]
        joined = jnp.concatenate(
            [line_of[:, 0:window] for line_of in lines]
            + [jnp.zeros((lines[0].shape[0], slot_lanes - 2 * piece), jnp.float32)]
            + [line_of[:, wide - window : wide] for line_of in lines],
            axis=1,
        )
        for patch_row in range(patch_rows):
            at = 2 + patch_row * PATCH + line_in
            sent[at, :, 0:slot_lanes] = joined[patch_row : patch_row + 1]
            if at >= half:
                sent[at - half, :, slot_lanes : 2 * slot_lanes] = joined[patch_row : patch_row + 1]

    pl.semaphore_wait(barrier, n - 1)

    def broadcast(buffer, kind):
        for offset in farthest_first:
            pltpu.make_async_remote_copy(
                src_ref=buffer.at[me],
                dst_ref=buffer.at[me],
                send_sem=send_sem.at[kind],
                recv_sem=recv_sem.at[kind],
                device_id={"row": peer(offset)},
                device_id_type=MESH,
            ).start()

    def from_peers(buffer, kind):
        others = buffer.at[pl.ds(0, n - 1)]
        pltpu.make_async_copy(others, others, recv_sem.at[kind]).wait()

    def to_peers(buffer, kind):
        others = buffer.at[pl.ds(0, n - 1)]
        pltpu.make_async_copy(others, others, send_sem.at[kind]).wait()

    for offset in farthest_first:
        target = peer(offset)
        pltpu.make_async_remote_copy(
            src_ref=sent.at[pl.ds(target * own, half)],
            dst_ref=arrived.at[me],
            send_sem=send_sem.at[1],
            recv_sem=recv_sem.at[1],
            device_id={"row": target},
            device_id_type=MESH,
        ).start()
    broadcast(sums_one, 0)
    to_right = pltpu.make_async_remote_copy(
        src_ref=hidden_any.at[pl.ds(own - 1, 1)],
        dst_ref=hidden.at[pl.ds(0, 1)],
        send_sem=halo_send.at[0],
        recv_sem=halo_recv.at[0],
        device_id={"row": lax.rem(me + 1, n)},
        device_id_type=MESH,
    )
    to_left = pltpu.make_async_remote_copy(
        src_ref=hidden_any.at[pl.ds(0, 1)],
        dst_ref=hidden.at[pl.ds(own + 1, 1)],
        send_sem=halo_send.at[1],
        recv_sem=halo_recv.at[1],
        device_id={"row": lax.rem(me + n - 1, n)},
        device_id_type=MESH,
    )

    @pl.when(me < n - 1)
    def _():
        to_right.start()

    @pl.when(me > 0)
    def _():
        to_left.start()

    @pl.when(me == 0)
    def _():
        hidden[0] = jnp.zeros(hidden.shape[1:], hidden.dtype)

    @pl.when(me == n - 1)
    def _():
        hidden[own + 1] = jnp.zeros(hidden.shape[1:], hidden.dtype)

    arrived[me] = sent[pl.ds(me * own, half)]

    load_out.wait()
    taps[...] = jnp.zeros_like(taps)
    for time_tap in range(3):
        for row_tap in range(3):
            for col_tap in range(3):
                at = ((time_tap * 3 + row_tap) * 3 + col_tap) * 3
                taps[at : at + 3] = out_weight[time_tap, row_tap, col_tap].astype(jnp.float32)
    flat_taps = taps[...].astype(jnp.bfloat16)
    depth = band.shape[0]
    entry = lax.broadcasted_iota(jnp.int32, (depth, channels), 0)
    tap_lane = lax.broadcasted_iota(jnp.int32, (depth, channels), 1)
    tap_of = entry // piece
    column = lax.rem(entry, window)
    first_lane = (
        (lax.rem(tap_of, 3) * 3 + tap_of // 3) * 9 + lax.rem(entry, piece) // window - 3 * column
    )
    for output in range(window):
        col_tap = output + 1 - column
        chosen = (
            (tap_lane == first_lane + 3 * (output + 1))
            & (col_tap >= 0)
            & (col_tap < 3)
            & (entry < 9 * piece)
        )
        band[:, output * channels : (output + 1) * channels] = jnp.dot(
            chosen.astype(jnp.float32).astype(jnp.bfloat16),
            flat_taps,
            preferred_element_type=jnp.float32,
        ).astype(jnp.bfloat16)
    columns[...] = jnp.zeros_like(columns)
    by_frame[...] = jnp.zeros_like(by_frame)

    slot_of = []
    for frame in range(FRAMES):
        found = jnp.int32(0)
        for slot in range(n):
            found = jnp.where(owner[slot] == frame, jnp.int32(slot), found)
        slot_of.append(found)


    def spread_cells(row):
        for frame in range(FRAMES):
            at = (row * FRAMES + frame) * pitch
            cells[at : at + wide] = hidden[row, frame].astype(jnp.float32)

    for row in range(1, own + 1):
        spread_cells(row)

    load_inner.wait()
    for row_tap in range(3):
        for col_tap in range(3):
            part = pl.ds(col_tap * channels, channels)
            for time_tap in range(3):
                block = inner_w[time_tap, row_tap, col_tap].T
                turned[row_tap, 2 - time_tap, part, 0:channels] = block
                turned[row_tap, 3 - time_tap, part, channels:] = block
            empty = jnp.zeros((channels, channels), jnp.bfloat16)
            turned[row_tap, 3, part, 0:channels] = empty
            turned[row_tap, 0, part, channels:] = empty
    pltpu.make_async_copy(group_rows, group_rows, local_sem.at[9]).wait()
    from_peers(sums_one, 0)
    from_peers(arrived, 1)
    means = over_devices(sums_one) / cell_total
    group_mean = means[0:1]
    inverse = lax.rsqrt(means[1:2] - group_mean * group_mean + eps_norm)
    group_gain = group_rows[0]
    group_shift = group_rows[1]

    def pixel_taps(row, block):
        for row_tap in range(3):
            for time_tap in range(3):
                at = (row_tap * 3 + time_tap) * piece
                source = row - row_tap + 2
                for side in range(2):
                    lane = source // half * slot_lanes + side * (slot_lanes - piece)
                    columns[block[side] : block[side] + FRAMES, at : at + piece] = by_frame[
                        source % half, 2 - time_tap : 2 - time_tap + FRAMES, lane : lane + piece
                    ]

    def state_terms(part):
        normed_state = (cells[part] - group_mean) * inverse
        return normed_state, silu_slope(normed_state * group_gain + group_shift) * group_gain

    own_cells = own * FRAMES
    for w in range(wide):
        normed_state, slope_factor = state_terms(
            pl.ds(FRAMES * pitch + w, own_cells, stride=pitch)
        )
        normed_cells[w] = normed_state
        factor[w] = slope_factor
    for frame in range(FRAMES):
        for row in range(half):
            by_frame[row, frame : frame + 1, :] = arrived[slot_of[frame], row]
    for row in range(1, own + 1):
        pixel_taps(row, ((row - 1) * FRAMES, own_cells + (row - 1) * FRAMES))
    left = columns[0 : 2 * own_cells].astype(jnp.bfloat16)
    firsts, seconds = [], []
    for output in range(0, window, 2):
        lanes = pl.ds(output * channels, min(2, window - output) * channels)
        several = jnp.dot(left, band[:, lanes], preferred_element_type=jnp.float32)
        for index in range(several.shape[1] // channels):
            for side in range(2):
                w = output + index + side * (wide - window)
                if side == 0 and output + index == window - 1 or side == 1 and output + index == 0:
                    continue
                upstream = (
                    several[
                        side * own_cells : (side + 1) * own_cells,
                        index * channels : (index + 1) * channels,
                    ]
                    * factor[w]
                )
                slope[pl.ds(FRAMES * pitch + w, own_cells, stride=pitch)] = upstream
                firsts.append(jnp.sum(upstream.reshape(-1, 8, channels), axis=0))
                seconds.append(
                    jnp.sum((upstream * normed_cells[w]).reshape(-1, 8, channels), axis=0)
                )
    first = tree_sum(firsts)
    second = tree_sum(seconds)
    first = jnp.sum(first, axis=0, keepdims=True)
    second = jnp.sum(second, axis=0, keepdims=True)
    sums_two[me] = jnp.where(spot == 0, first, second)
    broadcast(sums_two, 2)


    @pl.when(me < n - 1)
    def _():
        to_right.wait_send()
        to_left.wait_recv()

    @pl.when(me > 0)
    def _():
        to_left.wait_send()
        to_right.wait_recv()

    for index, row in enumerate((0, own + 1)):
        pixel_taps(row, (2 * own_cells + index * FRAMES, 2 * own_cells + (2 + index) * FRAMES))
        spread_cells(row)
    left = columns[2 * own_cells :].astype(jnp.bfloat16)
    for output in range(window):
        several = jnp.dot(
            left,
            band[:, output * channels : (output + 1) * channels],
            preferred_element_type=jnp.float32,
        )
        for side in range(2):
            if side == 0 and output == window - 1 or side == 1 and output == 0:
                continue
            for index, row in enumerate((0, own + 1)):
                part = pl.ds(
                    row * FRAMES * pitch + output + side * (wide - window), FRAMES, stride=pitch
                )
                at = (2 * side + index) * FRAMES
                slope[part] = several[at : at + FRAMES] * state_terms(part)[1]
    for cell in range((own + 2) * FRAMES):
        part = pl.ds(cell * wide, wide)
        ready[part] = slope[cell * pitch : cell * pitch + wide] * inverse
        state = hidden[cell // FRAMES, cell % FRAMES].astype(jnp.float32)
        normed_ref[part] = (state - group_mean) * inverse

    to_peers(sums_one, 0)
    to_peers(arrived, 1)
    to_peers(sums_two, 2)
    from_peers(sums_two, 2)
    total = over_devices(sums_two)
    first, second = group_sums(total[0:1], total[1:2])
    terms[0:2] = jnp.where(spot == 0, first, second) * (inverse / cell_total)


def last_kernel(n, ready, normed_ref, terms, turned, out_any, windows, out, out_sem):
    me = lax.axis_index("row")
    own = out.shape[0]
    wide = out.shape[3]
    channels = out.shape[4]
    line = FRAMES * wide
    windows[:, FRAMES // 2] = jnp.zeros((own + 2, 2, wide, 3 * channels), jnp.bfloat16)
    position = lax.rem(lax.broadcasted_iota(jnp.int32, (line, channels), 0), wide)
    for row in range(own + 2):
        part = pl.ds(row * line, line)
        state_grad = ready[part] - terms[0:1] - normed_ref[part] * terms[1:2]
        if row == 0:
            state_grad = jnp.where(me > 0, state_grad, 0.0)
        if row == own + 1:
            state_grad = jnp.where(me < n - 1, state_grad, 0.0)
        after = jnp.where(position == wide - 1, 0.0, pltpu.roll(state_grad, line - 1, 0))
        earlier = jnp.where(position == 0, 0.0, pltpu.roll(state_grad, 1, 0))
        for col_tap, shifted in enumerate((after, state_grad, earlier)):
            windows[row, 0 : FRAMES // 2, :, :, col_tap * channels : (col_tap + 1) * channels] = (
                shifted.astype(jnp.bfloat16).reshape(FRAMES // 2, 2, wide, channels)
            )
    for row in range(own):
        taken = jnp.concatenate(
            [
                windows[
                    row + 2 - row_tap, ahead // 2 : ahead // 2 + FRAMES // 2, ahead % 2
                ].reshape(line // 2, 3 * channels)
                for row_tap in range(3)
                for ahead in range(4)
            ],
            axis=1,
        )
        summed = jnp.dot(
            taken,
            turned[...].reshape(12 * 3 * channels, 2 * channels),
            preferred_element_type=jnp.float32,
        )
        for side in range(2):
            out[row, :, side] = (
                summed[:, side * channels : (side + 1) * channels]
                .reshape(FRAMES // 2, wide, channels)
                .astype(jnp.bfloat16)
            )
        copy = pltpu.make_async_copy(out.at[row], out_any.at[row], out_sem)
        copy.start()
    pltpu.make_async_copy(out, out_any, out_sem).wait()


def one_frame_each(
    frames,
    frame_owner,
    picks,
    patch_weight,
    patch_bias,
    norm_gain,
    head_weight,
    head_bias,
    head_out,
    hidden_state,
    group_gain,
    group_shift,
    out_weight,
    inner_weight,
):
    n = lax.axis_size("row")
    own, frame_count, wide, channels = hidden_state.shape
    height, strip = frames.shape[1:]
    pix, width = patch_weight.shape
    window = wide // 2 + 1
    depth = -(-27 * window // 128) * 128
    cells = (own + 2) * frame_count * wide
    f32, bf16 = jnp.float32, jnp.bfloat16
    vmem = pl.BlockSpec(memory_space=pltpu.VMEM)
    dma = pltpu.SemaphoreType.DMA
    passed = [
        pltpu.VMEM((cells, channels), f32),
        pltpu.VMEM((cells, channels), f32),
        pltpu.VMEM((8, channels), f32),
        pltpu.VMEM((3, 4, 3 * channels, 2 * channels), bf16),
    ]
    kept = pl.pallas_call(
        functools.partial(fused_kernel, n),
        out_shape=passed,
        in_specs=[pl.BlockSpec(memory_space=pltpu.HBM)] * 14,
        out_specs=[vmem] * 4,
        scratch_shapes=[
            pltpu.VMEM((3, strip, height), bf16),
            pltpu.SMEM(frame_owner.shape, jnp.int32),
            pltpu.SMEM(picks.shape, jnp.int32),
            pltpu.VMEM((4, 1, width), f32),
            pltpu.VMEM((2, 1, channels), f32),
            pltpu.VMEM(out_weight.shape, bf16),
            pltpu.VMEM((pix, width), bf16),
            pltpu.VMEM(head_weight.shape, bf16),
            pltpu.VMEM((own + 2, frame_count, wide, channels), bf16),
            pltpu.VMEM(inner_weight.shape, bf16),
            pltpu.VMEM(frames.shape, f32),
            pltpu.VMEM((-(-(height // PATCH) // 8) * 8, pix), f32),
            pltpu.VMEM((height + 4, 1, 128), f32),
            pltpu.VMEM((n, (own + 5) // 2, 1, 128), f32),
            pltpu.VMEM(((own + 5) // 2, frame_count + 8, 128), f32),
            pltpu.VMEM((2 * (own + 2) * frame_count, depth), f32),
            pltpu.VMEM((128, channels), f32),
            pltpu.VMEM((depth, window * channels), bf16),
            pltpu.VMEM(((own + 2) * frame_count * (wide + 1), channels), f32),
            pltpu.VMEM(((own + 2) * frame_count * (wide + 1), channels), f32),
            pltpu.VMEM((wide, own * frame_count, channels), f32),
            pltpu.VMEM((wide, own * frame_count, channels), f32),
            pltpu.VMEM((n, 2, channels), f32),
            pltpu.VMEM((n, 2, channels), f32),
            dma((15,)),
            dma((2,)),
            dma((2,)),
            dma((3,)),
            dma((3,)),
        ],
        compiler_params=pltpu.CompilerParams(
            collective_id=0, has_side_effects=True, vmem_limit_bytes=32 << 20
        ),
    )(
        *(
            pltpu.with_memory_space_constraint(array, pltpu.HBM)
            for array in (
                frames.transpose(0, 2, 1),
                frame_owner,
                picks,
                patch_weight,
                patch_bias[None],
                norm_gain[None],
                head_weight,
                head_bias[None],
                head_out[None],
                hidden_state,
                group_gain[None],
                group_shift[None],
                out_weight,
                inner_weight,
            )
        )
    )
    out_shape = (own, frame_count // 2, 2, wide, channels)
    return pl.pallas_call(
        functools.partial(last_kernel, n),
        out_shape=jax.ShapeDtypeStruct(out_shape, bf16),
        in_specs=[vmem] * 4,
        out_specs=pl.BlockSpec(memory_space=pltpu.HBM),
        scratch_shapes=[
            pltpu.VMEM((own + 2, frame_count // 2 + 1, 2, wide, 3 * channels), bf16),
            pltpu.VMEM(out_shape, bf16),
            dma,
        ],
        compiler_params=pltpu.CompilerParams(vmem_limit_bytes=32 << 20),
    )(*kept).reshape(hidden_state.shape)


def solution(mesh):
    body = one_frame_each if mesh.shape["row"] == FRAMES else per_device
    return jax.shard_map(
        body,
        mesh=mesh,
        in_specs=(
            P(None, None, ("clip", "row")),
            P("clip"),
            P("clip"),
            P(),
            P(),
            P(),
            P(),
            P(),
            P(),
            P(("clip", "row"), None, None, None),
            P(),
            P(),
            P(),
            P(),
        ),
        out_specs=P(("clip", "row"), None, None, None),
        check_vma=False,
    )
```

```python
import functools

import jax
import jax.numpy as jnp
from jax import lax
from jax.experimental import pallas as pl
from jax.experimental.pallas import tpu as pltpu
from jax.sharding import PartitionSpec as P

PATCH = 16
GROUPS = 32
FRAMES = 16


eps_norm = 1e-06
MESH = pl.DeviceIdType.MESH


def extended(block, sides, width):
    for axis, dim in sides:
        count = lax.axis_size(axis)
        forward = [(i, i + 1) for i in range(count - 1)]
        backward = [(target, source) for source, target in forward]
        low = lax.ppermute(
            lax.slice_in_dim(block, block.shape[dim] - width, None, axis=dim), axis, forward
        )
        high = lax.ppermute(lax.slice_in_dim(block, 0, width, axis=dim), axis, backward)
        block = jnp.concatenate([low, block, high], axis=dim)
    return block


def silu_slope(values):
    sigmoid = jax.nn.sigmoid(values)
    return sigmoid * (1.0 + values * (1.0 - sigmoid))


def to_tokens(pixels):
    channels, height, columns = pixels.shape
    shaped = pixels.reshape(channels, height // PATCH, PATCH, columns // PATCH, PATCH)
    return shaped.transpose(1, 3, 0, 2, 4).reshape(
        height // PATCH * (columns // PATCH), channels * PATCH * PATCH
    )


def from_tokens(token_grads, height, columns):
    shaped = token_grads.reshape(height // PATCH, columns // PATCH, 3, PATCH, PATCH)
    return shaped.transpose(2, 0, 3, 1, 4).reshape(3, height, columns)


def pixel_back(padded, out_weight, amount):
    frame_count = padded.shape[2]
    columns = padded.shape[3]
    widened = jnp.pad(padded, ((0, 0), (0, 0), (0, 2), (1, 1)))
    windows = []
    for time_tap in range(3):
        for row_tap in range(3):
            for col_tap in range(3):
                windows.append(
                    widened[
                        :,
                        2 - row_tap : 2 - row_tap + amount,
                        2 - time_tap : 2 - time_tap + frame_count,
                        2 - col_tap : 2 - col_tap + columns,
                    ]
                )
    stacked = jnp.stack(windows, 0).reshape(27 * 3, amount * frame_count * columns)
    kernel = out_weight.reshape(27 * 3, out_weight.shape[4])
    summed = lax.dot_general(
        stacked, kernel, (((0,), (0,)), ((), ())), preferred_element_type=jnp.float32
    )
    return summed.reshape(amount, frame_count, columns, out_weight.shape[4])


def inner_back(padded, inner_weight, amount):
    frame_count = padded.shape[1]
    columns = padded.shape[2]
    channel_count = padded.shape[3]
    widened = jnp.pad(padded, ((0, 0), (0, 2), (1, 1), (0, 0)))
    summed = jnp.zeros((amount * frame_count * columns, inner_weight.shape[3]), jnp.float32)
    for time_tap in range(3):
        windows = []
        for row_tap in range(3):
            for col_tap in range(3):
                windows.append(
                    widened[
                        2 - row_tap : 2 - row_tap + amount,
                        2 - time_tap : 2 - time_tap + frame_count,
                        2 - col_tap : 2 - col_tap + columns,
                        :,
                    ]
                )
        joined = jnp.concatenate(windows, axis=3).reshape(
            amount * frame_count * columns, 9 * channel_count
        )
        kernel = jnp.transpose(inner_weight[time_tap], (0, 1, 3, 2)).reshape(
            9 * channel_count, inner_weight.shape[3]
        )
        summed = summed + jnp.dot(joined, kernel, preferred_element_type=jnp.float32)
    return summed.reshape(amount, frame_count, columns, inner_weight.shape[3])


def group_back(state_rows, slope_in, group_mean, inverse, group_gain, group_shift, cell_total):
    grouped = state_rows.astype(jnp.float32).reshape(state_rows.shape[:3] + (GROUPS, -1))
    gain_table = group_gain.reshape(GROUPS, -1)
    shift_table = group_shift.reshape(GROUPS, -1)
    normed_state = (grouped - group_mean[:, None]) * inverse[:, None]
    affine = normed_state * gain_table + shift_table
    upstream = slope_in.reshape(grouped.shape) * silu_slope(affine) * gain_table
    group_terms = lax.psum(
        (jnp.sum(upstream, axis=(0, 1, 2, 4)), jnp.sum(upstream * normed_state, axis=(0, 1, 2, 4))),
        "row",
    )
    first_part = group_terms[0] / cell_total
    second_part = group_terms[1] / cell_total
    state_grad = (upstream - first_part[:, None] - normed_state * second_part[:, None]) * inverse[
        :, None
    ]
    return state_grad.reshape(state_rows.shape).astype(jnp.bfloat16)


def per_device(
    frames,
    frame_owner,
    picks,
    patch_weight,
    patch_bias,
    norm_gain,
    head_weight,
    head_bias,
    head_out,
    hidden_state,
    group_gain,
    group_shift,
    out_weight,
    inner_weight,
):
    devices = lax.axis_size("row")
    position = lax.axis_index("row")
    per_frame = devices // FRAMES
    slot = position // per_frame
    height = frames.shape[1]
    strip = frames.shape[2]
    own_rows = hidden_state.shape[0]
    frame_width = hidden_state.shape[2]
    tokens = to_tokens(frames)
    embedded = jnp.dot(tokens, patch_weight, preferred_element_type=jnp.float32) + patch_bias
    centred = embedded - jnp.mean(embedded, axis=1, keepdims=True)
    inv_spread = lax.rsqrt(jnp.mean(centred * centred, axis=1, keepdims=True) + eps_norm)
    normed = centred * inv_spread
    slot_mask = (jnp.arange(FRAMES, dtype=jnp.int32) == slot).astype(jnp.float32)
    partial_pool = slot_mask[:, None] * jnp.sum(normed * norm_gain, axis=0)[None, :]
    grouped = hidden_state.reshape(own_rows, FRAMES, frame_width, GROUPS, -1)
    first_sum = jnp.sum(grouped, axis=(0, 1, 2, 4), dtype=jnp.float32)
    second_sum = jnp.sum(jnp.square(grouped.astype(jnp.float32)), axis=(0, 1, 2, 4))
    pooled_sum, first_total, second_total = lax.psum((partial_pool, first_sum, second_sum), "row")
    frame_tokens = height // PATCH * (strip * per_frame // PATCH)
    pooled = pooled_sum / frame_tokens
    head_full = head_weight.astype(jnp.float32)
    before = jnp.dot(pooled, head_full, precision=lax.Precision.HIGHEST) + head_bias
    pulled = jnp.dot(head_out * silu_slope(before), head_full.T, precision=lax.Precision.HIGHEST)
    picked = jnp.sum((picks[:, None] == frame_owner[None, :]).astype(jnp.float32), axis=0)
    slot_grad = jnp.dot(slot_mask * picked, pulled, precision=lax.Precision.HIGHEST)
    scaled = norm_gain * slot_grad
    token_grad = inv_spread * (
        scaled - jnp.mean(scaled) - normed * jnp.mean(scaled * normed, axis=1, keepdims=True)
    )
    patch_grad = lax.dot_general(
        token_grad.astype(jnp.bfloat16),
        patch_weight,
        (((1,), (1,)), ((), ())),
        preferred_element_type=jnp.float32,
    )
    pixel_local = from_tokens(patch_grad, height, strip).astype(jnp.bfloat16)
    arrived = lax.all_to_all(pixel_local, "row", split_axis=1, concat_axis=2, tiled=True)
    by_slot = arrived.reshape(3, own_rows, FRAMES, frame_width)
    owner_table = (frame_owner[:, None] == jnp.arange(FRAMES, dtype=jnp.int32)[None, :]).astype(
        jnp.bfloat16
    )
    ordered = jnp.einsum(
        "krbw,bf->krfw", by_slot, owner_table, preferred_element_type=jnp.float32
    ).astype(jnp.bfloat16)
    cell_total = own_rows * devices * FRAMES * frame_width * (hidden_state.shape[3] // GROUPS)
    group_mean = first_total / cell_total
    inverse = lax.rsqrt(second_total / cell_total - group_mean * group_mean + eps_norm)
    pixel_padded = extended(ordered, (("row", 1),), 1)
    slope_in = pixel_back(pixel_padded, out_weight, own_rows)
    state_grad = group_back(
        hidden_state, slope_in, group_mean, inverse, group_gain, group_shift, cell_total
    )
    grad_padded = extended(state_grad, (("row", 0),), 1)
    return inner_back(grad_padded, inner_weight, own_rows).astype(jnp.bfloat16)


def split_rows(row):
    high = row.astype(jnp.bfloat16).astype(jnp.float32)
    rest = row - high
    middle = rest.astype(jnp.bfloat16).astype(jnp.float32)
    low = rest - middle
    index = lax.broadcasted_iota(jnp.int32, (8, row.shape[1]), 0)
    stacked = jnp.where(
        index == 0, high, jnp.where(index == 1, middle, jnp.where(index == 2, low, 0.0))
    )
    return stacked.astype(jnp.bfloat16)


def fused_kernel(
    n,
    frames_any,
    owner_any,
    picks_any,
    patch_any,
    patch_bias_any,
    norm_gain_any,
    head_any,
    head_bias_any,
    head_out_any,
    hidden_any,
    group_gain_any,
    group_shift_any,
    out_weight_any,
    inner_any,
    ready,
    normed_ref,
    terms,
    turned,
    frames,
    owner,
    picks,
    wide_rows,
    group_rows,
    out_weight,
    patch_w,
    head_w,
    hidden,
    inner_w,
    pixels,
    tokens,
    sent,
    arrived,
    by_frame,
    columns,
    taps,
    band,
    slope,
    cells,
    factor,
    centred_cells,
    sums_one,
    sums_two,
    local_sem,
    halo_recv,
    send_sem,
    recv_sem,
):
    me = lax.axis_index("row")
    strip, height = frames.shape[1], frames.shape[2]
    patch_rows = height // PATCH
    own = hidden.shape[0] - 2
    wide = hidden.shape[2]
    channels = hidden.shape[3]
    line = FRAMES * wide
    pitch = wide + 1
    per_group = channels // GROUPS
    cell_total = own * n * FRAMES * wide * per_group
    window = wide // 2 + 1
    piece = 3 * window
    slot_lanes = 64
    half = arrived.shape[1]

    def peer(offset):
        target = me
        step = 1
        while step < n:
            if offset // step % 2:
                target = target + step * (1 - 2 * lax.rem(lax.div(me, step), 2))
            step *= 2
        return target

    farthest_first = range(n - 1, 0, -1)

    barrier = pltpu.get_barrier_semaphore()
    for offset in farthest_first:
        pl.semaphore_signal(barrier, inc=1, device_id={"row": peer(offset)}, device_id_type=MESH)

    load_frames = pltpu.make_async_copy(frames_any, frames, local_sem.at[0])
    load_hidden = pltpu.make_async_copy(hidden_any, hidden.at[pl.ds(1, own)], local_sem.at[1])
    pix, width = patch_w.shape
    third, part_rows = pix // 3, width // 2
    load_patch = [
        pltpu.make_async_copy(
            patch_any.at[pl.ds(part * third, third)],
            patch_w.at[pl.ds(part * third, third)],
            local_sem.at[7 + part],
        )
        for part in range(3)
    ]
    load_head = [
        pltpu.make_async_copy(
            head_any.at[pl.ds(part * part_rows, part_rows)],
            head_w.at[pl.ds(part * part_rows, part_rows)],
            local_sem.at[10 + part],
        )
        for part in range(2)
    ]
    load_inner = pltpu.make_async_copy(inner_any, inner_w, local_sem.at[4])
    load_out = pltpu.make_async_copy(out_weight_any, out_weight, local_sem.at[5])
    load_owner = pltpu.make_async_copy(owner_any, owner, local_sem.at[5])
    load_picks = pltpu.make_async_copy(picks_any, picks, local_sem.at[5])
    load_wide = [
        pltpu.make_async_copy(source, wide_rows.at[index], local_sem.at[6])
        for index, source in enumerate((patch_bias_any, norm_gain_any, head_bias_any, head_out_any))
    ]
    load_group = [
        pltpu.make_async_copy(source, group_rows.at[index], local_sem.at[5])
        for index, source in enumerate((group_gain_any, group_shift_any))
    ]
    load_frames.start()
    load_hidden.start()
    for load in load_patch:
        load.start()
    for load in load_wide:
        load.start()
    for load in load_head:
        load.start()
    load_owner.start()
    load_picks.start()
    for load in load_group:
        load.start()
    load_out.start()
    load_inner.start()

    group_row = lax.broadcasted_iota(jnp.int32, (channels, channels), 0) // per_group
    group_col = lax.broadcasted_iota(jnp.int32, (channels, channels), 1) // per_group
    same_group = (group_row == group_col).astype(jnp.bfloat16)
    eight = lax.broadcasted_iota(jnp.int32, (8, channels), 0)
    spot = lax.broadcasted_iota(jnp.int32, (2, channels), 0)

    def group_sums(first, second):
        part = lax.rem(eight, 4)
        row = jnp.where(eight < 4, first, second)
        high = row.astype(jnp.bfloat16).astype(jnp.float32)
        rest = row - high
        middle = rest.astype(jnp.bfloat16).astype(jnp.float32)
        stacked = jnp.where(
            part == 0, high, jnp.where(part == 1, middle, jnp.where(part == 2, rest - middle, 0.0))
        )
        summed = jnp.dot(
            stacked.astype(jnp.bfloat16), same_group, preferred_element_type=jnp.float32
        )
        return (
            jnp.sum(summed[0:4], axis=0, keepdims=True),
            jnp.sum(summed[4:8], axis=0, keepdims=True),
        )

    def tree_sum(blocks):
        while len(blocks) > 1:
            blocks = [
                blocks[at] + blocks[at + 1] if at + 1 < len(blocks) else blocks[at]
                for at in range(0, len(blocks), 2)
            ]
        return blocks[0]

    def over_devices(buffer):
        return tree_sum([buffer[slot] for slot in range(n)])

    load_frames.wait()
    for colour in range(3):
        pixels[colour] = frames[colour].astype(jnp.float32).T
    tokens[...] = jnp.zeros_like(tokens)
    for colour in range(3):
        for line_in in range(PATCH):
            at = (colour * PATCH + line_in) * PATCH
            tokens[0:patch_rows, at : at + PATCH] = pixels[
                colour, pl.ds(line_in, patch_rows, stride=PATCH), :
            ]
    sent[...] = jnp.zeros_like(sent)

    load_hidden.wait()
    first = jnp.zeros((1, channels), jnp.float32)
    second = jnp.zeros((1, channels), jnp.float32)
    for row in range(own):
        state = hidden[1 + row].reshape(line, channels).astype(jnp.float32)
        first = first + jnp.sum(state, axis=0, keepdims=True)
        second = second + jnp.sum(state * state, axis=0, keepdims=True)
    first, second = group_sums(first, second)
    sums_one[me] = jnp.where(spot == 0, first, second)

    pltpu.make_async_copy(wide_rows, wide_rows, local_sem.at[6]).wait()
    embedded = wide_rows[0]
    for part in range(3):
        load_patch[part].wait()
        embedded = embedded + jnp.dot(
            tokens[:, part * third : (part + 1) * third].astype(jnp.bfloat16),
            patch_w[part * third : (part + 1) * third],
            preferred_element_type=jnp.float32,
        )
    centred = embedded - jnp.mean(embedded, axis=1, keepdims=True)
    inv_spread = lax.rsqrt(jnp.mean(centred * centred, axis=1, keepdims=True) + eps_norm)
    normed = centred * inv_spread
    gain = wide_rows[1]
    pooled = jnp.sum((normed * gain)[0:patch_rows], axis=0, keepdims=True) / patch_rows
    split_pool = split_rows(pooled)
    before = wide_rows[2]
    for part in range(2):
        load_head[part].wait()
        before = before + jnp.sum(
            jnp.dot(
                split_pool[:, part * part_rows : (part + 1) * part_rows],
                head_w[part * part_rows : (part + 1) * part_rows],
                preferred_element_type=jnp.float32,
            ),
            axis=0,
            keepdims=True,
        )
    pulled = jnp.sum(
        lax.dot_general(
            split_rows(wide_rows[3] * silu_slope(before)),
            head_w[...],
            (((1,), (1,)), ((), ())),
            preferred_element_type=jnp.float32,
        ),
        axis=0,
        keepdims=True,
    )
    load_owner.wait()
    load_picks.wait()
    pltpu.make_async_copy(group_rows, group_rows, local_sem.at[5]).wait()
    load_out.wait()
    mine = owner[me]
    picked = jnp.float32(0.0)
    for pick in range(picks.shape[0]):
        picked = picked + jnp.where(picks[pick] == mine, jnp.float32(1.0), jnp.float32(0.0))
    scaled = gain * (picked * pulled)
    token_grad = inv_spread * (
        scaled
        - jnp.mean(scaled, axis=1, keepdims=True)
        - normed * jnp.mean(scaled * normed, axis=1, keepdims=True)
    )
    token_grad = token_grad.astype(jnp.bfloat16)
    sixth = pix // 6
    cuts = (0, 3, 6)
    patch_grad = jnp.concatenate(
        [
            lax.dot_general(
                token_grad,
                patch_w[low * sixth : high * sixth],
                (((1,), (1,)), ((), ())),
                preferred_element_type=jnp.float32,
            )
            for low, high in zip(cuts[:-1], cuts[1:])
        ],
        axis=1,
    )
    patch_grad = patch_grad.astype(jnp.bfloat16).astype(jnp.float32)
    for line_in in range(PATCH):
        lines = [
            patch_grad[:, (colour * PATCH + line_in) * PATCH : (colour * PATCH + line_in + 1) * PATCH]
            for colour in range(3)
        ]
        joined = jnp.concatenate(
            [line_of[:, 0:window] for line_of in lines]
            + [jnp.zeros((lines[0].shape[0], slot_lanes - 2 * piece), jnp.float32)]
            + [line_of[:, wide - window : wide] for line_of in lines],
            axis=1,
        )
        for patch_row in range(patch_rows):
            at = 2 + patch_row * PATCH + line_in
            sent[at, :, 0:slot_lanes] = joined[patch_row : patch_row + 1]
            if at >= half:
                sent[at - half, :, slot_lanes : 2 * slot_lanes] = joined[patch_row : patch_row + 1]

    pl.semaphore_wait(barrier, n - 1)

    def send_sums(buffer, kind, offset):
        pltpu.make_async_remote_copy(
            src_ref=buffer.at[me],
            dst_ref=buffer.at[me],
            send_sem=send_sem,
            recv_sem=recv_sem.at[kind],
            device_id={"row": peer(offset)},
            device_id_type=MESH,
        ).start()

    def from_peers(buffer, kind):
        others = buffer.at[pl.ds(0, n - 1)]
        pltpu.make_async_copy(others, others, recv_sem.at[kind]).wait()

    def to_peers(buffer):
        others = buffer.at[pl.ds(0, n - 1)]
        pltpu.make_async_copy(others, others, send_sem).wait()

    for offset in farthest_first:
        target = peer(offset)
        pltpu.make_async_remote_copy(
            src_ref=sent.at[pl.ds(target * own, half)],
            dst_ref=arrived.at[me],
            send_sem=send_sem,
            recv_sem=recv_sem.at[1],
            device_id={"row": target},
            device_id_type=MESH,
        ).start()
        send_sums(sums_one, 0, offset)
    to_right = pltpu.make_async_remote_copy(
        src_ref=hidden_any.at[pl.ds(own - 1, 1)],
        dst_ref=hidden.at[pl.ds(0, 1)],
        send_sem=send_sem,
        recv_sem=halo_recv.at[0],
        device_id={"row": lax.rem(me + 1, n)},
        device_id_type=MESH,
    )
    to_left = pltpu.make_async_remote_copy(
        src_ref=hidden_any.at[pl.ds(0, 1)],
        dst_ref=hidden.at[pl.ds(own + 1, 1)],
        send_sem=send_sem,
        recv_sem=halo_recv.at[1],
        device_id={"row": lax.rem(me + n - 1, n)},
        device_id_type=MESH,
    )

    @pl.when(me < n - 1)
    def _():
        to_right.start()

    @pl.when(me > 0)
    def _():
        to_left.start()

    @pl.when(me == 0)
    def _():
        hidden[0] = jnp.zeros(hidden.shape[1:], hidden.dtype)

    @pl.when(me == n - 1)
    def _():
        hidden[own + 1] = jnp.zeros(hidden.shape[1:], hidden.dtype)

    arrived[me] = sent[pl.ds(me * own, half)]

    taps[...] = jnp.zeros_like(taps)
    for time_tap in range(3):
        for row_tap in range(3):
            for col_tap in range(3):
                at = ((time_tap * 3 + row_tap) * 3 + col_tap) * 3
                taps[at : at + 3] = out_weight[time_tap, row_tap, col_tap].astype(jnp.float32)
    flat_taps = taps[...].astype(jnp.bfloat16)
    depth = band.shape[0]
    entry = lax.broadcasted_iota(jnp.int32, (depth, channels), 0)
    tap_lane = lax.broadcasted_iota(jnp.int32, (depth, channels), 1)
    tap_of = entry // piece
    column = lax.rem(entry, window)
    first_lane = (
        (lax.rem(tap_of, 3) * 3 + tap_of // 3) * 9 + lax.rem(entry, piece) // window - 3 * column
    )
    for output in range(window):
        col_tap = output + 1 - column
        chosen = (
            (tap_lane == first_lane + 3 * (output + 1))
            & (col_tap >= 0)
            & (col_tap < 3)
            & (entry < 9 * piece)
        )
        band[:, output * channels : (output + 1) * channels] = jnp.dot(
            chosen.astype(jnp.float32).astype(jnp.bfloat16),
            flat_taps,
            preferred_element_type=jnp.float32,
        ).astype(jnp.bfloat16)
    columns[...] = jnp.zeros_like(columns)
    by_frame[...] = jnp.zeros_like(by_frame)

    slot_of = []
    for frame in range(FRAMES):
        found = jnp.int32(0)
        for slot in range(n):
            found = jnp.where(owner[slot] == frame, jnp.int32(slot), found)
        slot_of.append(found)


    def spread_cells(row):
        for frame in range(FRAMES):
            at = (row * FRAMES + frame) * pitch
            cells[at : at + wide] = hidden[row, frame].astype(jnp.float32)

    for row in range(1, own + 1):
        spread_cells(row)

    load_inner.wait()
    for row_tap in range(3):
        for col_tap in range(3):
            part = pl.ds(col_tap * channels, channels)
            for time_tap in range(3):
                block = inner_w[time_tap, row_tap, col_tap].T
                turned[row_tap, 2 - time_tap, part, 0:channels] = block
                turned[row_tap, 3 - time_tap, part, channels:] = block
            empty = jnp.zeros((channels, channels), jnp.bfloat16)
            turned[row_tap, 3, part, 0:channels] = empty
            turned[row_tap, 0, part, channels:] = empty
    from_peers(sums_one, 0)
    means = over_devices(sums_one) / cell_total
    group_mean = means[0:1]
    inverse = lax.rsqrt(means[1:2] - group_mean * group_mean + eps_norm)
    group_gain = group_rows[0]
    group_shift = group_rows[1]
    from_peers(arrived, 1)
    def pixel_taps(row, block):
        for row_tap in range(3):
            for time_tap in range(3):
                at = (row_tap * 3 + time_tap) * piece
                source = row - row_tap + 2
                for side in range(2):
                    lane = source // half * slot_lanes + side * (slot_lanes - piece)
                    columns[block[side] : block[side] + FRAMES, at : at + piece] = by_frame[
                        source % half, 2 - time_tap : 2 - time_tap + FRAMES, lane : lane + piece
                    ]

    spread = inverse * group_gain

    def state_terms(part):
        centred = cells[part] - group_mean
        return centred, silu_slope(centred * spread + group_shift)

    own_cells = own * FRAMES
    for w in range(wide):
        part = pl.ds(FRAMES * pitch + w, own_cells, stride=pitch)
        centred_cells[w], factor[w] = state_terms(part)
    for frame in range(FRAMES):
        for row in range(half):
            by_frame[row, frame : frame + 1, :] = arrived[slot_of[frame], row]
    for row in range(1, own + 1):
        pixel_taps(row, ((row - 1) * FRAMES, own_cells + (row - 1) * FRAMES))
    left = columns[0 : 2 * own_cells].astype(jnp.bfloat16)
    firsts, seconds = [], []
    for output in range(0, window, 2):
        lanes = pl.ds(output * channels, min(2, window - output) * channels)
        several = jnp.dot(left, band[:, lanes], preferred_element_type=jnp.float32)
        for index in range(several.shape[1] // channels):
            for side in range(2):
                w = output + index + side * (wide - window)
                if side == 0 and output + index == window - 1 or side == 1 and output + index == 0:
                    continue
                upstream = (
                    several[
                        side * own_cells : (side + 1) * own_cells,
                        index * channels : (index + 1) * channels,
                    ]
                    * factor[w]
                )
                slope[pl.ds(FRAMES * pitch + w, own_cells, stride=pitch)] = upstream
                firsts.append(jnp.sum(upstream.reshape(-1, 8, channels), axis=0))
                seconds.append(
                    jnp.sum((upstream * centred_cells[w]).reshape(-1, 8, channels), axis=0)
                )
    first = tree_sum(firsts)
    second = tree_sum(seconds)
    first = jnp.sum(first, axis=0, keepdims=True) * group_gain
    second = jnp.sum(second, axis=0, keepdims=True) * spread
    sums_two[me] = jnp.where(spot == 0, first, second)
    for offset in farthest_first:
        send_sums(sums_two, 2, offset)


    @pl.when(me < n - 1)
    def _():
        to_left.wait_recv()

    @pl.when(me > 0)
    def _():
        to_right.wait_recv()

    for index, row in enumerate((0, own + 1)):
        pixel_taps(row, (2 * own_cells + index * FRAMES, 2 * own_cells + (2 + index) * FRAMES))
        spread_cells(row)
    left = columns[2 * own_cells :].astype(jnp.bfloat16)
    for output in range(window):
        several = jnp.dot(
            left,
            band[:, output * channels : (output + 1) * channels],
            preferred_element_type=jnp.float32,
        )
        for side in range(2):
            if side == 0 and output == window - 1 or side == 1 and output == 0:
                continue
            for index, row in enumerate((0, own + 1)):
                part = pl.ds(
                    row * FRAMES * pitch + output + side * (wide - window), FRAMES, stride=pitch
                )
                at = (2 * side + index) * FRAMES
                slope[part] = several[at : at + FRAMES] * state_terms(part)[1]
    for cell in range((own + 2) * FRAMES):
        part = pl.ds(cell * wide, wide)
        ready[part] = slope[cell * pitch : cell * pitch + wide] * spread
        state = hidden[cell // FRAMES, cell % FRAMES].astype(jnp.float32)
        normed_ref[part] = (state - group_mean) * inverse

    to_peers(sums_one)
    to_peers(arrived)
    to_peers(sums_two)

    @pl.when(me < n - 1)
    def _():
        to_right.wait_send()

    @pl.when(me > 0)
    def _():
        to_left.wait_send()

    from_peers(sums_two, 2)
    total = over_devices(sums_two)
    lane = lax.broadcasted_iota(jnp.int32, total.shape, 1)
    step = 1
    while step < per_group:
        total = total + jnp.where(
            lax.rem(lane // step, 2) == 0,
            pltpu.roll(total, channels - step, 1),
            pltpu.roll(total, step, 1),
        )
        step *= 2
    terms[0:2] = total * (inverse / cell_total)


def last_kernel(n, ready, normed_ref, terms, turned, out_any, windows, out, out_sem):
    me = lax.axis_index("row")
    own = out.shape[0]
    wide = out.shape[3]
    channels = out.shape[4]
    line = FRAMES * wide
    windows[:, FRAMES // 2] = jnp.zeros((own + 2, 2, wide, 3 * channels), jnp.bfloat16)
    position = lax.rem(lax.broadcasted_iota(jnp.int32, (line, channels), 0), wide)
    for row in range(own + 2):
        part = pl.ds(row * line, line)
        state_grad = ready[part] - terms[0:1] - normed_ref[part] * terms[1:2]
        if row == 0:
            state_grad = jnp.where(me > 0, state_grad, 0.0)
        if row == own + 1:
            state_grad = jnp.where(me < n - 1, state_grad, 0.0)
        after = jnp.where(position == wide - 1, 0.0, pltpu.roll(state_grad, line - 1, 0))
        earlier = jnp.where(position == 0, 0.0, pltpu.roll(state_grad, 1, 0))
        for col_tap, shifted in enumerate((after, state_grad, earlier)):
            windows[row, 0 : FRAMES // 2, :, :, col_tap * channels : (col_tap + 1) * channels] = (
                shifted.astype(jnp.bfloat16).reshape(FRAMES // 2, 2, wide, channels)
            )
    for row in range(own):
        taken = jnp.concatenate(
            [
                windows[
                    row + 2 - row_tap, ahead // 2 : ahead // 2 + FRAMES // 2, ahead % 2
                ].reshape(line // 2, 3 * channels)
                for row_tap in range(3)
                for ahead in range(4)
            ],
            axis=1,
        )
        summed = jnp.dot(
            taken,
            turned[...].reshape(12 * 3 * channels, 2 * channels),
            preferred_element_type=jnp.float32,
        )
        for side in range(2):
            out[row, :, side] = (
                summed[:, side * channels : (side + 1) * channels]
                .reshape(FRAMES // 2, wide, channels)
                .astype(jnp.bfloat16)
            )
        copy = pltpu.make_async_copy(out.at[row], out_any.at[row], out_sem)
        copy.start()
    pltpu.make_async_copy(out, out_any, out_sem).wait()


def one_frame_each(
    frames,
    frame_owner,
    picks,
    patch_weight,
    patch_bias,
    norm_gain,
    head_weight,
    head_bias,
    head_out,
    hidden_state,
    group_gain,
    group_shift,
    out_weight,
    inner_weight,
):
    n = lax.axis_size("row")
    own, frame_count, wide, channels = hidden_state.shape
    height, strip = frames.shape[1:]
    pix, width = patch_weight.shape
    window = wide // 2 + 1
    depth = -(-27 * window // 128) * 128
    cells = (own + 2) * frame_count * wide
    f32, bf16 = jnp.float32, jnp.bfloat16
    vmem = pl.BlockSpec(memory_space=pltpu.VMEM)
    dma = pltpu.SemaphoreType.DMA
    passed = [
        pltpu.VMEM((cells, channels), f32),
        pltpu.VMEM((cells, channels), f32),
        pltpu.VMEM((8, channels), f32),
        pltpu.VMEM((3, 4, 3 * channels, 2 * channels), bf16),
    ]
    kept = pl.pallas_call(
        functools.partial(fused_kernel, n),
        out_shape=passed,
        in_specs=[pl.BlockSpec(memory_space=pltpu.HBM)] * 14,
        out_specs=[vmem] * 4,
        scratch_shapes=[
            pltpu.VMEM((3, strip, height), bf16),
            pltpu.SMEM(frame_owner.shape, jnp.int32),
            pltpu.SMEM(picks.shape, jnp.int32),
            pltpu.VMEM((4, 1, width), f32),
            pltpu.VMEM((2, 1, channels), f32),
            pltpu.VMEM(out_weight.shape, bf16),
            pltpu.VMEM((pix, width), bf16),
            pltpu.VMEM(head_weight.shape, bf16),
            pltpu.VMEM((own + 2, frame_count, wide, channels), bf16),
            pltpu.VMEM(inner_weight.shape, bf16),
            pltpu.VMEM(frames.shape, f32),
            pltpu.VMEM((-(-(height // PATCH) // 8) * 8, pix), f32),
            pltpu.VMEM((height + 4, 1, 128), f32),
            pltpu.VMEM((n, (own + 5) // 2, 1, 128), f32),
            pltpu.VMEM(((own + 5) // 2, frame_count + 8, 128), f32),
            pltpu.VMEM((2 * (own + 2) * frame_count, depth), f32),
            pltpu.VMEM((128, channels), f32),
            pltpu.VMEM((depth, window * channels), bf16),
            pltpu.VMEM(((own + 2) * frame_count * (wide + 1), channels), f32),
            pltpu.VMEM(((own + 2) * frame_count * (wide + 1), channels), f32),
            pltpu.VMEM((wide, own * frame_count, channels), f32),
            pltpu.VMEM((wide, own * frame_count, channels), f32),
            pltpu.VMEM((n, 2, channels), f32),
            pltpu.VMEM((n, 2, channels), f32),
            dma((12,)),
            dma((2,)),
            dma,
            dma((3,)),
        ],
        compiler_params=pltpu.CompilerParams(
            collective_id=0, has_side_effects=True, vmem_limit_bytes=32 << 20
        ),
    )(
        *(
            pltpu.with_memory_space_constraint(array, pltpu.HBM)
            for array in (
                frames.transpose(0, 2, 1),
                frame_owner,
                picks,
                patch_weight,
                patch_bias[None],
                norm_gain[None],
                head_weight,
                head_bias[None],
                head_out[None],
                hidden_state,
                group_gain[None],
                group_shift[None],
                out_weight,
                inner_weight,
            )
        )
    )
    out_shape = (own, frame_count // 2, 2, wide, channels)
    return pl.pallas_call(
        functools.partial(last_kernel, n),
        out_shape=jax.ShapeDtypeStruct(out_shape, bf16),
        in_specs=[vmem] * 4,
        out_specs=pl.BlockSpec(memory_space=pltpu.HBM),
        scratch_shapes=[
            pltpu.VMEM((own + 2, frame_count // 2 + 1, 2, wide, 3 * channels), bf16),
            pltpu.VMEM(out_shape, bf16),
            dma,
        ],
        compiler_params=pltpu.CompilerParams(vmem_limit_bytes=32 << 20),
    )(*kept).reshape(hidden_state.shape)


def solution(mesh):
    body = one_frame_each if mesh.shape["row"] == FRAMES else per_device
    return jax.shard_map(
        body,
        mesh=mesh,
        in_specs=(
            P(None, None, ("clip", "row")),
            P("clip"),
            P("clip"),
            P(),
            P(),
            P(),
            P(),
            P(),
            P(),
            P(("clip", "row"), None, None, None),
            P(),
            P(),
            P(),
            P(),
        ),
        out_specs=P(("clip", "row"), None, None, None),
        check_vma=False,
    )
```

```python
import functools

import jax
import jax.numpy as jnp
from jax import lax
from jax.experimental import pallas as pl
from jax.experimental.pallas import tpu as pltpu
from jax.sharding import PartitionSpec as P

PATCH = 16
GROUPS = 32
FRAMES = 16


eps_norm = 1e-06
MESH = pl.DeviceIdType.MESH


def extended(block, sides, width):
    for axis, dim in sides:
        count = lax.axis_size(axis)
        forward = [(i, i + 1) for i in range(count - 1)]
        backward = [(target, source) for source, target in forward]
        low = lax.ppermute(
            lax.slice_in_dim(block, block.shape[dim] - width, None, axis=dim), axis, forward
        )
        high = lax.ppermute(lax.slice_in_dim(block, 0, width, axis=dim), axis, backward)
        block = jnp.concatenate([low, block, high], axis=dim)
    return block


def silu_slope(values):
    sigmoid = jax.nn.sigmoid(values)
    return sigmoid * (1.0 + values * (1.0 - sigmoid))


def to_tokens(pixels):
    channels, height, columns = pixels.shape
    shaped = pixels.reshape(channels, height // PATCH, PATCH, columns // PATCH, PATCH)
    return shaped.transpose(1, 3, 0, 2, 4).reshape(
        height // PATCH * (columns // PATCH), channels * PATCH * PATCH
    )


def from_tokens(token_grads, height, columns):
    shaped = token_grads.reshape(height // PATCH, columns // PATCH, 3, PATCH, PATCH)
    return shaped.transpose(2, 0, 3, 1, 4).reshape(3, height, columns)


def pixel_back(padded, out_weight, amount):
    frame_count = padded.shape[2]
    columns = padded.shape[3]
    widened = jnp.pad(padded, ((0, 0), (0, 0), (0, 2), (1, 1)))
    windows = []
    for time_tap in range(3):
        for row_tap in range(3):
            for col_tap in range(3):
                windows.append(
                    widened[
                        :,
                        2 - row_tap : 2 - row_tap + amount,
                        2 - time_tap : 2 - time_tap + frame_count,
                        2 - col_tap : 2 - col_tap + columns,
                    ]
                )
    stacked = jnp.stack(windows, 0).reshape(27 * 3, amount * frame_count * columns)
    kernel = out_weight.reshape(27 * 3, out_weight.shape[4])
    summed = lax.dot_general(
        stacked, kernel, (((0,), (0,)), ((), ())), preferred_element_type=jnp.float32
    )
    return summed.reshape(amount, frame_count, columns, out_weight.shape[4])


def inner_back(padded, inner_weight, amount):
    frame_count = padded.shape[1]
    columns = padded.shape[2]
    channel_count = padded.shape[3]
    widened = jnp.pad(padded, ((0, 0), (0, 2), (1, 1), (0, 0)))
    summed = jnp.zeros((amount * frame_count * columns, inner_weight.shape[3]), jnp.float32)
    for time_tap in range(3):
        windows = []
        for row_tap in range(3):
            for col_tap in range(3):
                windows.append(
                    widened[
                        2 - row_tap : 2 - row_tap + amount,
                        2 - time_tap : 2 - time_tap + frame_count,
                        2 - col_tap : 2 - col_tap + columns,
                        :,
                    ]
                )
        joined = jnp.concatenate(windows, axis=3).reshape(
            amount * frame_count * columns, 9 * channel_count
        )
        kernel = jnp.transpose(inner_weight[time_tap], (0, 1, 3, 2)).reshape(
            9 * channel_count, inner_weight.shape[3]
        )
        summed = summed + jnp.dot(joined, kernel, preferred_element_type=jnp.float32)
    return summed.reshape(amount, frame_count, columns, inner_weight.shape[3])


def group_back(state_rows, slope_in, group_mean, inverse, group_gain, group_shift, cell_total):
    grouped = state_rows.astype(jnp.float32).reshape(state_rows.shape[:3] + (GROUPS, -1))
    gain_table = group_gain.reshape(GROUPS, -1)
    shift_table = group_shift.reshape(GROUPS, -1)
    normed_state = (grouped - group_mean[:, None]) * inverse[:, None]
    affine = normed_state * gain_table + shift_table
    upstream = slope_in.reshape(grouped.shape) * silu_slope(affine) * gain_table
    group_terms = lax.psum(
        (jnp.sum(upstream, axis=(0, 1, 2, 4)), jnp.sum(upstream * normed_state, axis=(0, 1, 2, 4))),
        "row",
    )
    first_part = group_terms[0] / cell_total
    second_part = group_terms[1] / cell_total
    state_grad = (upstream - first_part[:, None] - normed_state * second_part[:, None]) * inverse[
        :, None
    ]
    return state_grad.reshape(state_rows.shape).astype(jnp.bfloat16)


def per_device(
    frames,
    frame_owner,
    picks,
    patch_weight,
    patch_bias,
    norm_gain,
    head_weight,
    head_bias,
    head_out,
    hidden_state,
    group_gain,
    group_shift,
    out_weight,
    inner_weight,
):
    devices = lax.axis_size("row")
    position = lax.axis_index("row")
    per_frame = devices // FRAMES
    slot = position // per_frame
    height = frames.shape[1]
    strip = frames.shape[2]
    own_rows = hidden_state.shape[0]
    frame_width = hidden_state.shape[2]
    tokens = to_tokens(frames)
    embedded = jnp.dot(tokens, patch_weight, preferred_element_type=jnp.float32) + patch_bias
    centred = embedded - jnp.mean(embedded, axis=1, keepdims=True)
    inv_spread = lax.rsqrt(jnp.mean(centred * centred, axis=1, keepdims=True) + eps_norm)
    normed = centred * inv_spread
    slot_mask = (jnp.arange(FRAMES, dtype=jnp.int32) == slot).astype(jnp.float32)
    partial_pool = slot_mask[:, None] * jnp.sum(normed * norm_gain, axis=0)[None, :]
    grouped = hidden_state.reshape(own_rows, FRAMES, frame_width, GROUPS, -1)
    first_sum = jnp.sum(grouped, axis=(0, 1, 2, 4), dtype=jnp.float32)
    second_sum = jnp.sum(jnp.square(grouped.astype(jnp.float32)), axis=(0, 1, 2, 4))
    pooled_sum, first_total, second_total = lax.psum((partial_pool, first_sum, second_sum), "row")
    frame_tokens = height // PATCH * (strip * per_frame // PATCH)
    pooled = pooled_sum / frame_tokens
    head_full = head_weight.astype(jnp.float32)
    before = jnp.dot(pooled, head_full, precision=lax.Precision.HIGHEST) + head_bias
    pulled = jnp.dot(head_out * silu_slope(before), head_full.T, precision=lax.Precision.HIGHEST)
    picked = jnp.sum((picks[:, None] == frame_owner[None, :]).astype(jnp.float32), axis=0)
    slot_grad = jnp.dot(slot_mask * picked, pulled, precision=lax.Precision.HIGHEST)
    scaled = norm_gain * slot_grad
    token_grad = inv_spread * (
        scaled - jnp.mean(scaled) - normed * jnp.mean(scaled * normed, axis=1, keepdims=True)
    )
    patch_grad = lax.dot_general(
        token_grad.astype(jnp.bfloat16),
        patch_weight,
        (((1,), (1,)), ((), ())),
        preferred_element_type=jnp.float32,
    )
    pixel_local = from_tokens(patch_grad, height, strip).astype(jnp.bfloat16)
    arrived = lax.all_to_all(pixel_local, "row", split_axis=1, concat_axis=2, tiled=True)
    by_slot = arrived.reshape(3, own_rows, FRAMES, frame_width)
    owner_table = (frame_owner[:, None] == jnp.arange(FRAMES, dtype=jnp.int32)[None, :]).astype(
        jnp.bfloat16
    )
    ordered = jnp.einsum(
        "krbw,bf->krfw", by_slot, owner_table, preferred_element_type=jnp.float32
    ).astype(jnp.bfloat16)
    cell_total = own_rows * devices * FRAMES * frame_width * (hidden_state.shape[3] // GROUPS)
    group_mean = first_total / cell_total
    inverse = lax.rsqrt(second_total / cell_total - group_mean * group_mean + eps_norm)
    pixel_padded = extended(ordered, (("row", 1),), 1)
    slope_in = pixel_back(pixel_padded, out_weight, own_rows)
    state_grad = group_back(
        hidden_state, slope_in, group_mean, inverse, group_gain, group_shift, cell_total
    )
    grad_padded = extended(state_grad, (("row", 0),), 1)
    return inner_back(grad_padded, inner_weight, own_rows).astype(jnp.bfloat16)


def split_rows(row):
    high = row.astype(jnp.bfloat16).astype(jnp.float32)
    rest = row - high
    middle = rest.astype(jnp.bfloat16).astype(jnp.float32)
    low = rest - middle
    index = lax.broadcasted_iota(jnp.int32, (8, row.shape[1]), 0)
    stacked = jnp.where(
        index == 0, high, jnp.where(index == 1, middle, jnp.where(index == 2, low, 0.0))
    )
    return stacked.astype(jnp.bfloat16)


def fused_kernel(
    n,
    frames_any,
    owner_any,
    picks_any,
    patch_any,
    patch_bias_any,
    norm_gain_any,
    head_any,
    head_bias_any,
    head_out_any,
    hidden_any,
    group_gain_any,
    group_shift_any,
    out_weight_any,
    inner_any,
    ready,
    normed_ref,
    terms,
    turned,
    frames,
    owner,
    picks,
    wide_rows,
    group_rows,
    out_weight,
    patch_w,
    head_w,
    hidden,
    inner_w,
    pixels,
    tokens,
    sent,
    arrived,
    by_frame,
    columns,
    taps,
    band,
    slope,
    cells,
    factor,
    centred_cells,
    sums_one,
    sums_two,
    local_sem,
    send_sem,
    recv_sem,
):
    me = lax.axis_index("row")
    strip, height = frames.shape[1], frames.shape[2]
    patch_rows = height // PATCH
    own = hidden.shape[0] - 2
    wide = hidden.shape[2]
    channels = hidden.shape[3]
    line = FRAMES * wide
    pitch = wide + 1
    per_group = channels // GROUPS
    cell_total = own * n * FRAMES * wide * per_group
    window = wide // 2 + 1
    piece = 3 * window
    slot_lanes = 64
    half = arrived.shape[1]

    def peer(offset):
        target = me
        step = 1
        while step < n:
            if offset // step % 2:
                target = target + step * (1 - 2 * lax.rem(lax.div(me, step), 2))
            step *= 2
        return target

    farthest_first = range(n - 1, 0, -1)

    barrier = pltpu.get_barrier_semaphore()
    for offset in farthest_first:
        pl.semaphore_signal(barrier, inc=1, device_id={"row": peer(offset)}, device_id_type=MESH)

    load_frames = pltpu.make_async_copy(frames_any, frames, local_sem.at[0])
    load_hidden = pltpu.make_async_copy(hidden_any, hidden.at[pl.ds(1, own)], local_sem.at[1])
    pix, width = patch_w.shape
    third, part_rows = pix // 3, width // 2
    load_patch = [
        pltpu.make_async_copy(
            patch_any.at[pl.ds(part * third, third)],
            patch_w.at[pl.ds(part * third, third)],
            local_sem.at[2 + part],
        )
        for part in range(3)
    ]
    load_head = [
        pltpu.make_async_copy(
            head_any.at[pl.ds(part * part_rows, part_rows)],
            head_w.at[pl.ds(part * part_rows, part_rows)],
            local_sem.at[5 + part],
        )
        for part in range(2)
    ]
    load_inner = pltpu.make_async_copy(inner_any, inner_w, local_sem.at[7])
    load_out = pltpu.make_async_copy(out_weight_any, out_weight, local_sem.at[7])
    load_owner = pltpu.make_async_copy(owner_any, owner, local_sem.at[7])
    load_picks = pltpu.make_async_copy(picks_any, picks, local_sem.at[7])
    load_wide = [
        pltpu.make_async_copy(source, wide_rows.at[index], local_sem.at[1])
        for index, source in enumerate((patch_bias_any, norm_gain_any, head_bias_any, head_out_any))
    ]
    load_group = [
        pltpu.make_async_copy(source, group_rows.at[index], local_sem.at[7])
        for index, source in enumerate((group_gain_any, group_shift_any))
    ]
    load_frames.start()
    load_hidden.start()
    for load in load_wide:
        load.start()
    for load in load_patch + load_head:
        load.start()
    load_owner.start()
    load_picks.start()
    for load in load_group:
        load.start()
    load_out.start()
    load_inner.start()

    group_row = lax.broadcasted_iota(jnp.int32, (channels, channels), 0) // per_group
    group_col = lax.broadcasted_iota(jnp.int32, (channels, channels), 1) // per_group
    same_group = (group_row == group_col).astype(jnp.bfloat16)
    eight = lax.broadcasted_iota(jnp.int32, (8, channels), 0)
    spot = lax.broadcasted_iota(jnp.int32, (2, channels), 0)

    def group_sums(first, second):
        part = lax.rem(eight, 4)
        row = jnp.where(eight < 4, first, second)
        high = row.astype(jnp.bfloat16).astype(jnp.float32)
        rest = row - high
        middle = rest.astype(jnp.bfloat16).astype(jnp.float32)
        stacked = jnp.where(
            part == 0, high, jnp.where(part == 1, middle, jnp.where(part == 2, rest - middle, 0.0))
        )
        summed = jnp.dot(
            stacked.astype(jnp.bfloat16), same_group, preferred_element_type=jnp.float32
        )
        return (
            jnp.sum(summed[0:4], axis=0, keepdims=True),
            jnp.sum(summed[4:8], axis=0, keepdims=True),
        )

    def tree_sum(blocks):
        while len(blocks) > 1:
            blocks = [
                blocks[at] + blocks[at + 1] if at + 1 < len(blocks) else blocks[at]
                for at in range(0, len(blocks), 2)
            ]
        return blocks[0]

    def over_devices(buffer):
        return tree_sum([buffer[slot] for slot in range(n)])

    load_frames.wait()
    for colour in range(3):
        pixels[colour] = frames[colour].astype(jnp.float32).T
    tokens[...] = jnp.zeros_like(tokens)
    for colour in range(3):
        for line_in in range(PATCH):
            at = (colour * PATCH + line_in) * PATCH
            tokens[0:patch_rows, at : at + PATCH] = pixels[
                colour, pl.ds(line_in, patch_rows, stride=PATCH), :
            ]
    sent[...] = jnp.zeros_like(sent)

    load_hidden.wait()
    pltpu.make_async_copy(wide_rows, wide_rows, local_sem.at[1]).wait()
    first = jnp.zeros((1, channels), jnp.float32)
    second = jnp.zeros((1, channels), jnp.float32)
    for row in range(own):
        state = hidden[1 + row].reshape(line, channels).astype(jnp.float32)
        first = first + jnp.sum(state, axis=0, keepdims=True)
        second = second + jnp.sum(state * state, axis=0, keepdims=True)
    first, second = group_sums(first, second)
    sums_one[me] = jnp.where(spot == 0, first, second)

    embedded = wide_rows[0]
    for part in range(3):
        load_patch[part].wait()
        embedded = embedded + jnp.dot(
            tokens[:, part * third : (part + 1) * third].astype(jnp.bfloat16),
            patch_w[part * third : (part + 1) * third],
            preferred_element_type=jnp.float32,
        )
    centred = embedded - jnp.mean(embedded, axis=1, keepdims=True)
    inv_spread = lax.rsqrt(jnp.mean(centred * centred, axis=1, keepdims=True) + eps_norm)
    normed = centred * inv_spread
    gain = wide_rows[1]
    pooled = jnp.sum((normed * gain)[0:patch_rows], axis=0, keepdims=True) / patch_rows
    split_pool = split_rows(pooled)
    before = wide_rows[2]
    for part in range(2):
        load_head[part].wait()
        before = before + jnp.sum(
            jnp.dot(
                split_pool[:, part * part_rows : (part + 1) * part_rows],
                head_w[part * part_rows : (part + 1) * part_rows],
                preferred_element_type=jnp.float32,
            ),
            axis=0,
            keepdims=True,
        )
    pulled = jnp.sum(
        lax.dot_general(
            split_rows(wide_rows[3] * silu_slope(before)),
            head_w[...],
            (((1,), (1,)), ((), ())),
            preferred_element_type=jnp.float32,
        ),
        axis=0,
        keepdims=True,
    )
    load_owner.wait()
    load_picks.wait()
    pltpu.make_async_copy(group_rows, group_rows, local_sem.at[7]).wait()
    load_out.wait()
    load_inner.wait()
    mine = owner[me]
    picked = jnp.float32(0.0)
    for pick in range(picks.shape[0]):
        picked = picked + jnp.where(picks[pick] == mine, jnp.float32(1.0), jnp.float32(0.0))
    scaled = gain * (picked * pulled)
    token_grad = inv_spread * (
        scaled
        - jnp.mean(scaled, axis=1, keepdims=True)
        - normed * jnp.mean(scaled * normed, axis=1, keepdims=True)
    )
    token_grad = token_grad.astype(jnp.bfloat16)
    sixth = pix // 6
    cuts = (0, 3, 6)
    patch_grad = jnp.concatenate(
        [
            lax.dot_general(
                token_grad,
                patch_w[low * sixth : high * sixth],
                (((1,), (1,)), ((), ())),
                preferred_element_type=jnp.float32,
            )
            for low, high in zip(cuts[:-1], cuts[1:])
        ],
        axis=1,
    )
    patch_grad = patch_grad.astype(jnp.bfloat16).astype(jnp.float32)
    for line_in in range(PATCH):
        lines = [
            patch_grad[:, (colour * PATCH + line_in) * PATCH : (colour * PATCH + line_in + 1) * PATCH]
            for colour in range(3)
        ]
        joined = jnp.concatenate(
            [line_of[:, 0:window] for line_of in lines]
            + [jnp.zeros((lines[0].shape[0], slot_lanes - 2 * piece), jnp.float32)]
            + [line_of[:, wide - window : wide] for line_of in lines],
            axis=1,
        )
        for patch_row in range(patch_rows):
            at = 2 + patch_row * PATCH + line_in
            sent[at, :, 0:slot_lanes] = joined[patch_row : patch_row + 1]
            if at >= half:
                sent[at - half, :, slot_lanes : 2 * slot_lanes] = joined[patch_row : patch_row + 1]

    pl.semaphore_wait(barrier, n - 1)

    def send_sums(buffer, kind, offset):
        pltpu.make_async_remote_copy(
            src_ref=buffer.at[me],
            dst_ref=buffer.at[me],
            send_sem=send_sem,
            recv_sem=recv_sem.at[kind],
            device_id={"row": peer(offset)},
            device_id_type=MESH,
        ).start()

    def from_peers(buffer, kind):
        others = buffer.at[pl.ds(0, n - 1)]
        pltpu.make_async_copy(others, others, recv_sem.at[kind]).wait()

    def to_peers(buffer):
        others = buffer.at[pl.ds(0, n - 1)]
        pltpu.make_async_copy(others, others, send_sem).wait()

    for offset in farthest_first:
        target = peer(offset)
        pltpu.make_async_remote_copy(
            src_ref=sent.at[pl.ds(target * own, half)],
            dst_ref=arrived.at[me],
            send_sem=send_sem,
            recv_sem=recv_sem.at[1],
            device_id={"row": target},
            device_id_type=MESH,
        ).start()
        send_sums(sums_one, 0, offset)
    to_right = pltpu.make_async_remote_copy(
        src_ref=hidden_any.at[pl.ds(own - 1, 1)],
        dst_ref=hidden.at[pl.ds(0, 1)],
        send_sem=send_sem,
        recv_sem=recv_sem.at[3],
        device_id={"row": lax.rem(me + 1, n)},
        device_id_type=MESH,
    )
    to_left = pltpu.make_async_remote_copy(
        src_ref=hidden_any.at[pl.ds(0, 1)],
        dst_ref=hidden.at[pl.ds(own + 1, 1)],
        send_sem=send_sem,
        recv_sem=recv_sem.at[4],
        device_id={"row": lax.rem(me + n - 1, n)},
        device_id_type=MESH,
    )

    @pl.when(me < n - 1)
    def _():
        to_right.start()

    @pl.when(me > 0)
    def _():
        to_left.start()

    @pl.when(me == 0)
    def _():
        hidden[0] = jnp.zeros(hidden.shape[1:], hidden.dtype)

    @pl.when(me == n - 1)
    def _():
        hidden[own + 1] = jnp.zeros(hidden.shape[1:], hidden.dtype)

    arrived[me] = sent[pl.ds(me * own, half)]

    taps[...] = jnp.zeros_like(taps)
    for time_tap in range(3):
        for row_tap in range(3):
            for col_tap in range(3):
                at = ((time_tap * 3 + row_tap) * 3 + col_tap) * 3
                taps[at : at + 3] = out_weight[time_tap, row_tap, col_tap].astype(jnp.float32)
    flat_taps = taps[...].astype(jnp.bfloat16)
    depth = band.shape[0]
    entry = lax.broadcasted_iota(jnp.int32, (depth, channels), 0)
    tap_lane = lax.broadcasted_iota(jnp.int32, (depth, channels), 1)
    tap_of = entry // piece
    column = lax.rem(entry, window)
    first_lane = (
        (lax.rem(tap_of, 3) * 3 + tap_of // 3) * 9 + lax.rem(entry, piece) // window - 3 * column
    )
    for output in range(window):
        col_tap = output + 1 - column
        chosen = (
            (tap_lane == first_lane + 3 * (output + 1))
            & (col_tap >= 0)
            & (col_tap < 3)
            & (entry < 9 * piece)
        )
        band[:, output * channels : (output + 1) * channels] = jnp.dot(
            chosen.astype(jnp.float32).astype(jnp.bfloat16),
            flat_taps,
            preferred_element_type=jnp.float32,
        ).astype(jnp.bfloat16)
    columns[...] = jnp.zeros_like(columns)
    by_frame[...] = jnp.zeros_like(by_frame)

    slot_of = []
    for frame in range(FRAMES):
        found = jnp.int32(0)
        for slot in range(n):
            found = jnp.where(owner[slot] == frame, jnp.int32(slot), found)
        slot_of.append(found)


    def spread_cells(row):
        for frame in range(FRAMES):
            at = (row * FRAMES + frame) * pitch
            cells[at : at + wide] = hidden[row, frame].astype(jnp.float32)

    for row in range(1, own + 1):
        spread_cells(row)

    for row_tap in range(3):
        for col_tap in range(3):
            part = pl.ds(col_tap * channels, channels)
            for time_tap in range(3):
                block = inner_w[time_tap, row_tap, col_tap].T
                turned[2 - row_tap, 2 - time_tap, part, 0:channels] = block
                turned[2 - row_tap, 3 - time_tap, part, channels:] = block
            empty = jnp.zeros((channels, channels), jnp.bfloat16)
            turned[2 - row_tap, 3, part, 0:channels] = empty
            turned[2 - row_tap, 0, part, channels:] = empty
    from_peers(sums_one, 0)
    from_peers(arrived, 1)
    means = over_devices(sums_one) / cell_total
    group_mean = means[0:1]
    inverse = lax.rsqrt(means[1:2] - group_mean * group_mean + eps_norm)
    group_gain = group_rows[0]
    group_shift = group_rows[1]
    def pixel_taps(row, block):
        for row_tap in range(3):
            for time_tap in range(3):
                at = (row_tap * 3 + time_tap) * piece
                source = row - row_tap + 2
                for side in range(2):
                    lane = source // half * slot_lanes + side * (slot_lanes - piece)
                    columns[block[side] : block[side] + FRAMES, at : at + piece] = by_frame[
                        source % half, 2 - time_tap : 2 - time_tap + FRAMES, lane : lane + piece
                    ]

    spread = inverse * group_gain

    def state_terms(part):
        centred = cells[part] - group_mean
        return centred, silu_slope(centred * spread + group_shift)

    own_cells = own * FRAMES
    for w in range(wide):
        part = pl.ds(FRAMES * pitch + w, own_cells, stride=pitch)
        centred_cells[w], factor[w] = state_terms(part)
    for frame in range(FRAMES):
        for row in range(half):
            by_frame[row, frame : frame + 1, :] = arrived[slot_of[frame], row]
    for row in range(1, own + 1):
        pixel_taps(row, ((row - 1) * FRAMES, own_cells + (row - 1) * FRAMES))
    left = columns[0 : 2 * own_cells].astype(jnp.bfloat16)
    firsts, seconds = [], []
    for output in range(0, window, 2):
        lanes = pl.ds(output * channels, min(2, window - output) * channels)
        several = jnp.dot(left, band[:, lanes], preferred_element_type=jnp.float32)
        for index in range(several.shape[1] // channels):
            for side in range(2):
                w = output + index + side * (wide - window)
                if side == 0 and output + index == window - 1 or side == 1 and output + index == 0:
                    continue
                upstream = (
                    several[
                        side * own_cells : (side + 1) * own_cells,
                        index * channels : (index + 1) * channels,
                    ]
                    * factor[w]
                )
                slope[pl.ds(FRAMES * pitch + w, own_cells, stride=pitch)] = upstream
                firsts.append(jnp.sum(upstream.reshape(-1, 8, channels), axis=0))
                seconds.append(
                    jnp.sum((upstream * centred_cells[w]).reshape(-1, 8, channels), axis=0)
                )
    first = tree_sum(firsts)
    second = tree_sum(seconds)
    first = jnp.sum(first, axis=0, keepdims=True) * group_gain
    second = jnp.sum(second, axis=0, keepdims=True) * spread
    sums_two[me] = jnp.where(spot == 0, first, second)
    for offset in farthest_first:
        send_sums(sums_two, 2, offset)


    @pl.when(me < n - 1)
    def _():
        to_left.wait_recv()

    @pl.when(me > 0)
    def _():
        to_right.wait_recv()

    for index, row in enumerate((0, own + 1)):
        pixel_taps(row, (2 * own_cells + index * FRAMES, 2 * own_cells + (2 + index) * FRAMES))
        spread_cells(row)
    left = columns[2 * own_cells :].astype(jnp.bfloat16)
    for output in range(window):
        several = jnp.dot(
            left,
            band[:, output * channels : (output + 1) * channels],
            preferred_element_type=jnp.float32,
        )
        for side in range(2):
            if side == 0 and output == window - 1 or side == 1 and output == 0:
                continue
            for index, row in enumerate((0, own + 1)):
                part = pl.ds(
                    row * FRAMES * pitch + output + side * (wide - window), FRAMES, stride=pitch
                )
                at = (2 * side + index) * FRAMES
                slope[part] = several[at : at + FRAMES] * state_terms(part)[1]
    for cell in range((own + 2) * FRAMES):
        part = pl.ds(cell * wide, wide)
        ready[part] = slope[cell * pitch : cell * pitch + wide] * spread
        state = hidden[cell // FRAMES, cell % FRAMES].astype(jnp.float32)
        normed_ref[part] = (state - group_mean) * inverse

    to_peers(sums_one)
    to_peers(arrived)
    to_peers(sums_two)

    @pl.when(me < n - 1)
    def _():
        to_right.wait_send()

    @pl.when(me > 0)
    def _():
        to_left.wait_send()

    from_peers(sums_two, 2)
    total = over_devices(sums_two)
    lane = lax.broadcasted_iota(jnp.int32, total.shape, 1)
    step = 1
    while step < per_group:
        total = total + jnp.where(
            lax.rem(lane // step, 2) == 0,
            pltpu.roll(total, channels - step, 1),
            pltpu.roll(total, step, 1),
        )
        step *= 2
    terms[0:2] = total * (inverse / cell_total)


def last_kernel(n, ready, normed_ref, terms, turned, out_any, windows, out, out_sem):
    me = lax.axis_index("row")
    own = out.shape[0]
    wide = out.shape[3]
    channels = out.shape[4]
    line = FRAMES * wide
    windows[:, FRAMES // 2] = jnp.zeros((own + 2, 2, wide, 3 * channels), jnp.bfloat16)
    position = lax.rem(lax.broadcasted_iota(jnp.int32, (line, channels), 0), wide)
    for row in range(own + 2):
        part = pl.ds(row * line, line)
        state_grad = ready[part] - terms[0:1] - normed_ref[part] * terms[1:2]
        if row == 0:
            state_grad = jnp.where(me > 0, state_grad, 0.0)
        if row == own + 1:
            state_grad = jnp.where(me < n - 1, state_grad, 0.0)
        after = jnp.where(position == wide - 1, 0.0, pltpu.roll(state_grad, line - 1, 0))
        earlier = jnp.where(position == 0, 0.0, pltpu.roll(state_grad, 1, 0))
        for col_tap, shifted in enumerate((after, state_grad, earlier)):
            windows[row, 0 : FRAMES // 2, :, :, col_tap * channels : (col_tap + 1) * channels] = (
                shifted.astype(jnp.bfloat16).reshape(FRAMES // 2, 2, wide, channels)
            )
    half_line = line // 2
    taken = jnp.concatenate(
        [
            windows[
                above : above + own, ahead // 2 : ahead // 2 + FRAMES // 2, ahead % 2
            ].reshape(own * half_line, 3 * channels)
            for above in range(3)
            for ahead in range(4)
        ],
        axis=1,
    )
    summed = jnp.dot(
        taken,
        turned[...].reshape(12 * 3 * channels, 2 * channels),
        preferred_element_type=jnp.float32,
    )
    for row in range(own):
        for side in range(2):
            out[row, :, side] = (
                summed[
                    row * half_line : (row + 1) * half_line, side * channels : (side + 1) * channels
                ]
                .reshape(FRAMES // 2, wide, channels)
                .astype(jnp.bfloat16)
            )
        pltpu.make_async_copy(out.at[row], out_any.at[row], out_sem).start()
    pltpu.make_async_copy(out, out_any, out_sem).wait()


def one_frame_each(
    frames,
    frame_owner,
    picks,
    patch_weight,
    patch_bias,
    norm_gain,
    head_weight,
    head_bias,
    head_out,
    hidden_state,
    group_gain,
    group_shift,
    out_weight,
    inner_weight,
):
    n = lax.axis_size("row")
    own, frame_count, wide, channels = hidden_state.shape
    height, strip = frames.shape[1:]
    pix, width = patch_weight.shape
    window = wide // 2 + 1
    depth = -(-27 * window // 128) * 128
    cells = (own + 2) * frame_count * wide
    f32, bf16 = jnp.float32, jnp.bfloat16
    vmem = pl.BlockSpec(memory_space=pltpu.VMEM)
    dma = pltpu.SemaphoreType.DMA
    passed = [
        pltpu.VMEM((cells, channels), f32),
        pltpu.VMEM((cells, channels), f32),
        pltpu.VMEM((8, channels), f32),
        pltpu.VMEM((3, 4, 3 * channels, 2 * channels), bf16),
    ]
    kept = pl.pallas_call(
        functools.partial(fused_kernel, n),
        out_shape=passed,
        in_specs=[pl.BlockSpec(memory_space=pltpu.HBM)] * 14,
        out_specs=[vmem] * 4,
        scratch_shapes=[
            pltpu.VMEM((3, strip, height), bf16),
            pltpu.SMEM(frame_owner.shape, jnp.int32),
            pltpu.SMEM(picks.shape, jnp.int32),
            pltpu.VMEM((4, 1, width), f32),
            pltpu.VMEM((2, 1, channels), f32),
            pltpu.VMEM(out_weight.shape, bf16),
            pltpu.VMEM((pix, width), bf16),
            pltpu.VMEM(head_weight.shape, bf16),
            pltpu.VMEM((own + 2, frame_count, wide, channels), bf16),
            pltpu.VMEM(inner_weight.shape, bf16),
            pltpu.VMEM(frames.shape, f32),
            pltpu.VMEM((-(-(height // PATCH) // 8) * 8, pix), f32),
            pltpu.VMEM((height + 4, 1, 128), f32),
            pltpu.VMEM((n, (own + 5) // 2, 1, 128), f32),
            pltpu.VMEM(((own + 5) // 2, frame_count + 8, 128), f32),
            pltpu.VMEM((2 * (own + 2) * frame_count, depth), f32),
            pltpu.VMEM((128, channels), f32),
            pltpu.VMEM((depth, window * channels), bf16),
            pltpu.VMEM(((own + 2) * frame_count * (wide + 1), channels), f32),
            pltpu.VMEM(((own + 2) * frame_count * (wide + 1), channels), f32),
            pltpu.VMEM((wide, own * frame_count, channels), f32),
            pltpu.VMEM((wide, own * frame_count, channels), f32),
            pltpu.VMEM((n, 2, channels), f32),
            pltpu.VMEM((n, 2, channels), f32),
            dma((8,)),
            dma,
            dma((5,)),
        ],
        compiler_params=pltpu.CompilerParams(
            collective_id=0, has_side_effects=True, vmem_limit_bytes=32 << 20
        ),
    )(
        *(
            pltpu.with_memory_space_constraint(array, pltpu.HBM)
            for array in (
                frames.transpose(0, 2, 1),
                frame_owner,
                picks,
                patch_weight,
                patch_bias[None],
                norm_gain[None],
                head_weight,
                head_bias[None],
                head_out[None],
                hidden_state,
                group_gain[None],
                group_shift[None],
                out_weight,
                inner_weight,
            )
        )
    )
    out_shape = (own, frame_count // 2, 2, wide, channels)
    return pl.pallas_call(
        functools.partial(last_kernel, n),
        out_shape=jax.ShapeDtypeStruct(out_shape, bf16),
        in_specs=[vmem] * 4,
        out_specs=pl.BlockSpec(memory_space=pltpu.HBM),
        scratch_shapes=[
            pltpu.VMEM((own + 2, frame_count // 2 + 1, 2, wide, 3 * channels), bf16),
            pltpu.VMEM(out_shape, bf16),
            dma,
        ],
        compiler_params=pltpu.CompilerParams(vmem_limit_bytes=32 << 20),
    )(*kept).reshape(hidden_state.shape)


def solution(mesh):
    body = one_frame_each if mesh.shape["row"] == FRAMES else per_device
    return jax.shard_map(
        body,
        mesh=mesh,
        in_specs=(
            P(None, None, ("clip", "row")),
            P("clip"),
            P("clip"),
            P(),
            P(),
            P(),
            P(),
            P(),
            P(),
            P(("clip", "row"), None, None, None),
            P(),
            P(),
            P(),
            P(),
        ),
        out_specs=P(("clip", "row"), None, None, None),
        check_vma=False,
    )
```

```python
import functools

import jax
import jax.numpy as jnp
from jax import lax
from jax.experimental import pallas as pl
from jax.experimental.pallas import tpu as pltpu
from jax.sharding import PartitionSpec as P

PATCH = 16
GROUPS = 32
FRAMES = 16


eps_norm = 1e-06
MESH = pl.DeviceIdType.MESH


def extended(block, sides, width):
    for axis, dim in sides:
        count = lax.axis_size(axis)
        forward = [(i, i + 1) for i in range(count - 1)]
        backward = [(target, source) for source, target in forward]
        low = lax.ppermute(
            lax.slice_in_dim(block, block.shape[dim] - width, None, axis=dim), axis, forward
        )
        high = lax.ppermute(lax.slice_in_dim(block, 0, width, axis=dim), axis, backward)
        block = jnp.concatenate([low, block, high], axis=dim)
    return block


def silu_slope(values):
    sigmoid = jax.nn.sigmoid(values)
    return sigmoid * (1.0 + values * (1.0 - sigmoid))


def to_tokens(pixels):
    channels, height, columns = pixels.shape
    shaped = pixels.reshape(channels, height // PATCH, PATCH, columns // PATCH, PATCH)
    return shaped.transpose(1, 3, 0, 2, 4).reshape(
        height // PATCH * (columns // PATCH), channels * PATCH * PATCH
    )


def from_tokens(token_grads, height, columns):
    shaped = token_grads.reshape(height // PATCH, columns // PATCH, 3, PATCH, PATCH)
    return shaped.transpose(2, 0, 3, 1, 4).reshape(3, height, columns)


def pixel_back(padded, out_weight, amount):
    frame_count = padded.shape[2]
    columns = padded.shape[3]
    widened = jnp.pad(padded, ((0, 0), (0, 0), (0, 2), (1, 1)))
    windows = []
    for time_tap in range(3):
        for row_tap in range(3):
            for col_tap in range(3):
                windows.append(
                    widened[
                        :,
                        2 - row_tap : 2 - row_tap + amount,
                        2 - time_tap : 2 - time_tap + frame_count,
                        2 - col_tap : 2 - col_tap + columns,
                    ]
                )
    stacked = jnp.stack(windows, 0).reshape(27 * 3, amount * frame_count * columns)
    kernel = out_weight.reshape(27 * 3, out_weight.shape[4])
    summed = lax.dot_general(
        stacked, kernel, (((0,), (0,)), ((), ())), preferred_element_type=jnp.float32
    )
    return summed.reshape(amount, frame_count, columns, out_weight.shape[4])


def inner_back(padded, inner_weight, amount):
    frame_count = padded.shape[1]
    columns = padded.shape[2]
    channel_count = padded.shape[3]
    widened = jnp.pad(padded, ((0, 0), (0, 2), (1, 1), (0, 0)))
    summed = jnp.zeros((amount * frame_count * columns, inner_weight.shape[3]), jnp.float32)
    for time_tap in range(3):
        windows = []
        for row_tap in range(3):
            for col_tap in range(3):
                windows.append(
                    widened[
                        2 - row_tap : 2 - row_tap + amount,
                        2 - time_tap : 2 - time_tap + frame_count,
                        2 - col_tap : 2 - col_tap + columns,
                        :,
                    ]
                )
        joined = jnp.concatenate(windows, axis=3).reshape(
            amount * frame_count * columns, 9 * channel_count
        )
        kernel = jnp.transpose(inner_weight[time_tap], (0, 1, 3, 2)).reshape(
            9 * channel_count, inner_weight.shape[3]
        )
        summed = summed + jnp.dot(joined, kernel, preferred_element_type=jnp.float32)
    return summed.reshape(amount, frame_count, columns, inner_weight.shape[3])


def group_back(state_rows, slope_in, group_mean, inverse, group_gain, group_shift, cell_total):
    grouped = state_rows.astype(jnp.float32).reshape(state_rows.shape[:3] + (GROUPS, -1))
    gain_table = group_gain.reshape(GROUPS, -1)
    shift_table = group_shift.reshape(GROUPS, -1)
    normed_state = (grouped - group_mean[:, None]) * inverse[:, None]
    affine = normed_state * gain_table + shift_table
    upstream = slope_in.reshape(grouped.shape) * silu_slope(affine) * gain_table
    group_terms = lax.psum(
        (jnp.sum(upstream, axis=(0, 1, 2, 4)), jnp.sum(upstream * normed_state, axis=(0, 1, 2, 4))),
        "row",
    )
    first_part = group_terms[0] / cell_total
    second_part = group_terms[1] / cell_total
    state_grad = (upstream - first_part[:, None] - normed_state * second_part[:, None]) * inverse[
        :, None
    ]
    return state_grad.reshape(state_rows.shape).astype(jnp.bfloat16)


def per_device(
    frames,
    frame_owner,
    picks,
    patch_weight,
    patch_bias,
    norm_gain,
    head_weight,
    head_bias,
    head_out,
    hidden_state,
    group_gain,
    group_shift,
    out_weight,
    inner_weight,
):
    devices = lax.axis_size("row")
    position = lax.axis_index("row")
    per_frame = devices // FRAMES
    slot = position // per_frame
    height = frames.shape[1]
    strip = frames.shape[2]
    own_rows = hidden_state.shape[0]
    frame_width = hidden_state.shape[2]
    tokens = to_tokens(frames)
    embedded = jnp.dot(tokens, patch_weight, preferred_element_type=jnp.float32) + patch_bias
    centred = embedded - jnp.mean(embedded, axis=1, keepdims=True)
    inv_spread = lax.rsqrt(jnp.mean(centred * centred, axis=1, keepdims=True) + eps_norm)
    normed = centred * inv_spread
    slot_mask = (jnp.arange(FRAMES, dtype=jnp.int32) == slot).astype(jnp.float32)
    partial_pool = slot_mask[:, None] * jnp.sum(normed * norm_gain, axis=0)[None, :]
    grouped = hidden_state.reshape(own_rows, FRAMES, frame_width, GROUPS, -1)
    first_sum = jnp.sum(grouped, axis=(0, 1, 2, 4), dtype=jnp.float32)
    second_sum = jnp.sum(jnp.square(grouped.astype(jnp.float32)), axis=(0, 1, 2, 4))
    pooled_sum, first_total, second_total = lax.psum((partial_pool, first_sum, second_sum), "row")
    frame_tokens = height // PATCH * (strip * per_frame // PATCH)
    pooled = pooled_sum / frame_tokens
    head_full = head_weight.astype(jnp.float32)
    before = jnp.dot(pooled, head_full, precision=lax.Precision.HIGHEST) + head_bias
    pulled = jnp.dot(head_out * silu_slope(before), head_full.T, precision=lax.Precision.HIGHEST)
    picked = jnp.sum((picks[:, None] == frame_owner[None, :]).astype(jnp.float32), axis=0)
    slot_grad = jnp.dot(slot_mask * picked, pulled, precision=lax.Precision.HIGHEST)
    scaled = norm_gain * slot_grad
    token_grad = inv_spread * (
        scaled - jnp.mean(scaled) - normed * jnp.mean(scaled * normed, axis=1, keepdims=True)
    )
    patch_grad = lax.dot_general(
        token_grad.astype(jnp.bfloat16),
        patch_weight,
        (((1,), (1,)), ((), ())),
        preferred_element_type=jnp.float32,
    )
    pixel_local = from_tokens(patch_grad, height, strip).astype(jnp.bfloat16)
    arrived = lax.all_to_all(pixel_local, "row", split_axis=1, concat_axis=2, tiled=True)
    by_slot = arrived.reshape(3, own_rows, FRAMES, frame_width)
    owner_table = (frame_owner[:, None] == jnp.arange(FRAMES, dtype=jnp.int32)[None, :]).astype(
        jnp.bfloat16
    )
    ordered = jnp.einsum(
        "krbw,bf->krfw", by_slot, owner_table, preferred_element_type=jnp.float32
    ).astype(jnp.bfloat16)
    cell_total = own_rows * devices * FRAMES * frame_width * (hidden_state.shape[3] // GROUPS)
    group_mean = first_total / cell_total
    inverse = lax.rsqrt(second_total / cell_total - group_mean * group_mean + eps_norm)
    pixel_padded = extended(ordered, (("row", 1),), 1)
    slope_in = pixel_back(pixel_padded, out_weight, own_rows)
    state_grad = group_back(
        hidden_state, slope_in, group_mean, inverse, group_gain, group_shift, cell_total
    )
    grad_padded = extended(state_grad, (("row", 0),), 1)
    return inner_back(grad_padded, inner_weight, own_rows).astype(jnp.bfloat16)


def split_rows(row):
    high = row.astype(jnp.bfloat16).astype(jnp.float32)
    rest = row - high
    middle = rest.astype(jnp.bfloat16).astype(jnp.float32)
    low = rest - middle
    index = lax.broadcasted_iota(jnp.int32, (8, row.shape[1]), 0)
    stacked = jnp.where(
        index == 0, high, jnp.where(index == 1, middle, jnp.where(index == 2, low, 0.0))
    )
    return stacked.astype(jnp.bfloat16)


def fused_kernel(
    n,
    frames_any,
    owner_any,
    picks_any,
    patch_any,
    patch_bias_any,
    norm_gain_any,
    head_any,
    head_bias_any,
    head_out_any,
    hidden_any,
    group_gain_any,
    group_shift_any,
    out_weight_any,
    inner_any,
    ready,
    normed_ref,
    terms,
    turned,
    paired,
    frames,
    owner,
    picks,
    wide_rows,
    group_rows,
    out_weight,
    patch_w,
    head_w,
    hidden,
    inner_w,
    pixels,
    tokens,
    sent,
    arrived,
    by_frame,
    columns,
    taps,
    band,
    slope,
    cells,
    factor,
    centred_cells,
    sums_one,
    sums_two,
    local_sem,
    send_sem,
    recv_sem,
):
    me = lax.axis_index("row")
    strip, height = frames.shape[1], frames.shape[2]
    patch_rows = height // PATCH
    own = hidden.shape[0] - 2
    wide = hidden.shape[2]
    channels = hidden.shape[3]
    line = FRAMES * wide
    pitch = wide + 1
    per_group = channels // GROUPS
    cell_total = own * n * FRAMES * wide * per_group
    window = wide // 2 + 1
    piece = 3 * window
    slot_lanes = 64
    half = arrived.shape[1]

    def peer(offset):
        target = me
        step = 1
        while step < n:
            if offset // step % 2:
                target = target + step * (1 - 2 * lax.rem(lax.div(me, step), 2))
            step *= 2
        return target

    farthest_first = range(n - 1, 0, -1)

    barrier = pltpu.get_barrier_semaphore()
    for offset in farthest_first:
        pl.semaphore_signal(barrier, inc=1, device_id={"row": peer(offset)}, device_id_type=MESH)

    load_frames = pltpu.make_async_copy(frames_any, frames, local_sem.at[0])
    load_hidden = pltpu.make_async_copy(hidden_any, hidden.at[pl.ds(1, own)], local_sem.at[1])
    pix, width = patch_w.shape
    third, part_rows = pix // 3, width // 2
    load_patch = [
        pltpu.make_async_copy(
            patch_any.at[pl.ds(part * third, third)],
            patch_w.at[pl.ds(part * third, third)],
            local_sem.at[2 + part],
        )
        for part in range(3)
    ]
    load_head = [
        pltpu.make_async_copy(
            head_any.at[pl.ds(part * part_rows, part_rows)],
            head_w.at[pl.ds(part * part_rows, part_rows)],
            local_sem.at[5 + part],
        )
        for part in range(2)
    ]
    load_inner = pltpu.make_async_copy(inner_any, inner_w, local_sem.at[7])
    load_out = pltpu.make_async_copy(out_weight_any, out_weight, local_sem.at[7])
    load_owner = pltpu.make_async_copy(owner_any, owner, local_sem.at[7])
    load_picks = pltpu.make_async_copy(picks_any, picks, local_sem.at[7])
    load_wide = [
        pltpu.make_async_copy(source, wide_rows.at[index], local_sem.at[1])
        for index, source in enumerate((patch_bias_any, norm_gain_any, head_bias_any, head_out_any))
    ]
    load_group = [
        pltpu.make_async_copy(source, group_rows.at[index], local_sem.at[7])
        for index, source in enumerate((group_gain_any, group_shift_any))
    ]
    load_frames.start()
    load_hidden.start()
    for load in load_wide:
        load.start()
    for load in load_patch + load_head:
        load.start()
    load_owner.start()
    load_picks.start()
    for load in load_group:
        load.start()
    load_out.start()
    load_inner.start()

    group_row = lax.broadcasted_iota(jnp.int32, (channels, channels), 0) // per_group
    group_col = lax.broadcasted_iota(jnp.int32, (channels, channels), 1) // per_group
    same_group = (group_row == group_col).astype(jnp.bfloat16)
    eight = lax.broadcasted_iota(jnp.int32, (8, channels), 0)
    spot = lax.broadcasted_iota(jnp.int32, (2, channels), 0)

    def group_sums(first, second):
        part = lax.rem(eight, 4)
        row = jnp.where(eight < 4, first, second)
        high = row.astype(jnp.bfloat16).astype(jnp.float32)
        rest = row - high
        middle = rest.astype(jnp.bfloat16).astype(jnp.float32)
        stacked = jnp.where(
            part == 0, high, jnp.where(part == 1, middle, jnp.where(part == 2, rest - middle, 0.0))
        )
        summed = jnp.dot(
            stacked.astype(jnp.bfloat16), same_group, preferred_element_type=jnp.float32
        )
        return (
            jnp.sum(summed[0:4], axis=0, keepdims=True),
            jnp.sum(summed[4:8], axis=0, keepdims=True),
        )

    def tree_sum(blocks):
        while len(blocks) > 1:
            blocks = [
                blocks[at] + blocks[at + 1] if at + 1 < len(blocks) else blocks[at]
                for at in range(0, len(blocks), 2)
            ]
        return blocks[0]

    def over_devices(buffer):
        return tree_sum([buffer[slot] for slot in range(n)])

    load_frames.wait()
    for colour in range(3):
        pixels[colour] = frames[colour].astype(jnp.float32).T
    tokens[...] = jnp.zeros_like(tokens)
    for colour in range(3):
        for line_in in range(PATCH):
            at = (colour * PATCH + line_in) * PATCH
            tokens[0:patch_rows, at : at + PATCH] = pixels[
                colour, pl.ds(line_in, patch_rows, stride=PATCH), :
            ]
    sent[...] = jnp.zeros_like(sent)

    load_hidden.wait()
    pltpu.make_async_copy(wide_rows, wide_rows, local_sem.at[1]).wait()
    first = jnp.zeros((1, channels), jnp.float32)
    second = jnp.zeros((1, channels), jnp.float32)
    for row in range(own):
        state = hidden[1 + row].reshape(line, channels).astype(jnp.float32)
        first = first + jnp.sum(state, axis=0, keepdims=True)
        second = second + jnp.sum(state * state, axis=0, keepdims=True)
    first, second = group_sums(first, second)
    sums_one[me] = jnp.where(spot == 0, first, second)

    embedded = wide_rows[0]
    for part in range(3):
        load_patch[part].wait()
        embedded = embedded + jnp.dot(
            tokens[:, part * third : (part + 1) * third].astype(jnp.bfloat16),
            patch_w[part * third : (part + 1) * third],
            preferred_element_type=jnp.float32,
        )
    centred = embedded - jnp.mean(embedded, axis=1, keepdims=True)
    inv_spread = lax.rsqrt(jnp.mean(centred * centred, axis=1, keepdims=True) + eps_norm)
    normed = centred * inv_spread
    gain = wide_rows[1]
    pooled = jnp.sum((normed * gain)[0:patch_rows], axis=0, keepdims=True) / patch_rows
    split_pool = split_rows(pooled)
    before = wide_rows[2]
    for part in range(2):
        load_head[part].wait()
        before = before + jnp.sum(
            jnp.dot(
                split_pool[:, part * part_rows : (part + 1) * part_rows],
                head_w[part * part_rows : (part + 1) * part_rows],
                preferred_element_type=jnp.float32,
            ),
            axis=0,
            keepdims=True,
        )
    pulled = jnp.sum(
        lax.dot_general(
            split_rows(wide_rows[3] * silu_slope(before)),
            head_w[...],
            (((1,), (1,)), ((), ())),
            preferred_element_type=jnp.float32,
        ),
        axis=0,
        keepdims=True,
    )
    load_owner.wait()
    load_picks.wait()
    pltpu.make_async_copy(group_rows, group_rows, local_sem.at[7]).wait()
    load_out.wait()
    load_inner.wait()
    mine = owner[me]
    picked = jnp.float32(0.0)
    for pick in range(picks.shape[0]):
        picked = picked + jnp.where(picks[pick] == mine, jnp.float32(1.0), jnp.float32(0.0))
    scaled = gain * (picked * pulled)
    token_grad = inv_spread * (
        scaled
        - jnp.mean(scaled, axis=1, keepdims=True)
        - normed * jnp.mean(scaled * normed, axis=1, keepdims=True)
    )
    token_grad = token_grad.astype(jnp.bfloat16)
    sixth = pix // 6
    cuts = (0, 3, 6)
    patch_grad = jnp.concatenate(
        [
            lax.dot_general(
                token_grad,
                patch_w[low * sixth : high * sixth],
                (((1,), (1,)), ((), ())),
                preferred_element_type=jnp.float32,
            )
            for low, high in zip(cuts[:-1], cuts[1:])
        ],
        axis=1,
    )
    patch_grad = patch_grad.astype(jnp.bfloat16).astype(jnp.float32)
    for line_in in range(PATCH):
        lines = [
            patch_grad[:, (colour * PATCH + line_in) * PATCH : (colour * PATCH + line_in + 1) * PATCH]
            for colour in range(3)
        ]
        joined = jnp.concatenate(
            [line_of[:, 0:window] for line_of in lines]
            + [jnp.zeros((lines[0].shape[0], slot_lanes - 2 * piece), jnp.float32)]
            + [line_of[:, wide - window : wide] for line_of in lines],
            axis=1,
        )
        for patch_row in range(patch_rows):
            at = 2 + patch_row * PATCH + line_in
            sent[at, :, 0:slot_lanes] = joined[patch_row : patch_row + 1]
            if at >= half:
                sent[at - half, :, slot_lanes : 2 * slot_lanes] = joined[patch_row : patch_row + 1]

    pl.semaphore_wait(barrier, n - 1)

    def send_sums(buffer, kind, offset):
        pltpu.make_async_remote_copy(
            src_ref=buffer.at[me],
            dst_ref=buffer.at[me],
            send_sem=send_sem,
            recv_sem=recv_sem.at[kind],
            device_id={"row": peer(offset)},
            device_id_type=MESH,
        ).start()

    def from_peers(buffer, kind):
        others = buffer.at[pl.ds(0, n - 1)]
        pltpu.make_async_copy(others, others, recv_sem.at[kind]).wait()

    def to_peers(buffer):
        others = buffer.at[pl.ds(0, n - 1)]
        pltpu.make_async_copy(others, others, send_sem).wait()

    for offset in farthest_first:
        target = peer(offset)
        pltpu.make_async_remote_copy(
            src_ref=sent.at[pl.ds(target * own, half)],
            dst_ref=arrived.at[me],
            send_sem=send_sem,
            recv_sem=recv_sem.at[1],
            device_id={"row": target},
            device_id_type=MESH,
        ).start()
        send_sums(sums_one, 0, offset)
    to_right = pltpu.make_async_remote_copy(
        src_ref=hidden_any.at[pl.ds(own - 1, 1)],
        dst_ref=hidden.at[pl.ds(0, 1)],
        send_sem=send_sem,
        recv_sem=recv_sem.at[3],
        device_id={"row": lax.rem(me + 1, n)},
        device_id_type=MESH,
    )
    to_left = pltpu.make_async_remote_copy(
        src_ref=hidden_any.at[pl.ds(0, 1)],
        dst_ref=hidden.at[pl.ds(own + 1, 1)],
        send_sem=send_sem,
        recv_sem=recv_sem.at[4],
        device_id={"row": lax.rem(me + n - 1, n)},
        device_id_type=MESH,
    )

    @pl.when(me < n - 1)
    def _():
        to_right.start()

    @pl.when(me > 0)
    def _():
        to_left.start()

    @pl.when(me == 0)
    def _():
        hidden[0] = jnp.zeros(hidden.shape[1:], hidden.dtype)

    @pl.when(me == n - 1)
    def _():
        hidden[own + 1] = jnp.zeros(hidden.shape[1:], hidden.dtype)

    arrived[me] = sent[pl.ds(me * own, half)]

    taps[...] = jnp.zeros_like(taps)
    for time_tap in range(3):
        for row_tap in range(3):
            for col_tap in range(3):
                at = ((time_tap * 3 + row_tap) * 3 + col_tap) * 3
                taps[at : at + 3] = out_weight[time_tap, row_tap, col_tap].astype(jnp.float32)
    flat_taps = taps[...].astype(jnp.bfloat16)
    depth = band.shape[0]
    entry = lax.broadcasted_iota(jnp.int32, (depth, channels), 0)
    tap_lane = lax.broadcasted_iota(jnp.int32, (depth, channels), 1)
    tap_of = entry // piece
    column = lax.rem(entry, window)
    first_lane = (
        (lax.rem(tap_of, 3) * 3 + tap_of // 3) * 9 + lax.rem(entry, piece) // window - 3 * column
    )
    for output in range(window):
        col_tap = output + 1 - column
        chosen = (
            (tap_lane == first_lane + 3 * (output + 1))
            & (col_tap >= 0)
            & (col_tap < 3)
            & (entry < 9 * piece)
        )
        band[:, output * channels : (output + 1) * channels] = jnp.dot(
            chosen.astype(jnp.float32).astype(jnp.bfloat16),
            flat_taps,
            preferred_element_type=jnp.float32,
        ).astype(jnp.bfloat16)
    columns[...] = jnp.zeros_like(columns)
    by_frame[...] = jnp.zeros_like(by_frame)

    slot_of = []
    for frame in range(FRAMES):
        found = jnp.int32(0)
        for slot in range(n):
            found = jnp.where(owner[slot] == frame, jnp.int32(slot), found)
        slot_of.append(found)


    def spread_cells(row):
        for frame in range(FRAMES):
            at = (row * FRAMES + frame) * pitch
            cells[at : at + wide] = hidden[row, frame].astype(jnp.float32)

    for row in range(1, own + 1):
        spread_cells(row)

    empty = jnp.zeros((channels, channels), jnp.bfloat16)
    for row_tap in range(3):
        above = 2 - row_tap
        for col_tap in range(3):
            part = pl.ds(col_tap * channels, channels)
            blocks = [inner_w[time_tap, row_tap, col_tap].T for time_tap in range(3)]
            for ahead in range(2):
                turned[above, ahead, part, 0:channels] = blocks[1 - ahead]
                turned[above, ahead, part, channels:] = blocks[2 - ahead]
            for side in range(2):
                at = (2 - col_tap + side) * channels
                for kind in range(2):
                    paired[kind, above, at : at + channels, side * channels : (side + 1) * channels] = (
                        blocks[2 - 2 * kind]
                    )
        for kind in range(2):
            paired[kind, above, 3 * channels :, 0:channels] = empty
            paired[kind, above, 0:channels, channels:] = empty

    from_peers(sums_one, 0)
    from_peers(arrived, 1)
    means = over_devices(sums_one) / cell_total
    group_mean = means[0:1]
    inverse = lax.rsqrt(means[1:2] - group_mean * group_mean + eps_norm)
    group_gain = group_rows[0]
    group_shift = group_rows[1]
    def pixel_taps(row, block):
        for row_tap in range(3):
            for time_tap in range(3):
                at = (row_tap * 3 + time_tap) * piece
                source = row - row_tap + 2
                for side in range(2):
                    lane = source // half * slot_lanes + side * (slot_lanes - piece)
                    columns[block[side] : block[side] + FRAMES, at : at + piece] = by_frame[
                        source % half, 2 - time_tap : 2 - time_tap + FRAMES, lane : lane + piece
                    ]

    spread = inverse * group_gain

    def state_terms(part):
        centred = cells[part] - group_mean
        return centred, silu_slope(centred * spread + group_shift)

    own_cells = own * FRAMES
    for w in range(wide):
        part = pl.ds(FRAMES * pitch + w, own_cells, stride=pitch)
        centred_cells[w], factor[w] = state_terms(part)
    for frame in range(FRAMES):
        for row in range(half):
            by_frame[row, frame : frame + 1, :] = arrived[slot_of[frame], row]
    for row in range(1, own + 1):
        pixel_taps(row, ((row - 1) * FRAMES, own_cells + (row - 1) * FRAMES))
    left = columns[0 : 2 * own_cells].astype(jnp.bfloat16)
    firsts, seconds = [], []
    for output in range(0, window, 2):
        lanes = pl.ds(output * channels, min(2, window - output) * channels)
        several = jnp.dot(left, band[:, lanes], preferred_element_type=jnp.float32)
        for index in range(several.shape[1] // channels):
            for side in range(2):
                w = output + index + side * (wide - window)
                if side == 0 and output + index == window - 1 or side == 1 and output + index == 0:
                    continue
                upstream = (
                    several[
                        side * own_cells : (side + 1) * own_cells,
                        index * channels : (index + 1) * channels,
                    ]
                    * factor[w]
                )
                slope[pl.ds(FRAMES * pitch + w, own_cells, stride=pitch)] = upstream
                firsts.append(jnp.sum(upstream.reshape(-1, 8, channels), axis=0))
                seconds.append(
                    jnp.sum((upstream * centred_cells[w]).reshape(-1, 8, channels), axis=0)
                )
    first = tree_sum(firsts)
    second = tree_sum(seconds)
    first = jnp.sum(first, axis=0, keepdims=True) * group_gain
    second = jnp.sum(second, axis=0, keepdims=True) * spread
    sums_two[me] = jnp.where(spot == 0, first, second)
    for offset in farthest_first:
        send_sums(sums_two, 2, offset)


    @pl.when(me < n - 1)
    def _():
        to_left.wait_recv()

    @pl.when(me > 0)
    def _():
        to_right.wait_recv()

    for index, row in enumerate((0, own + 1)):
        pixel_taps(row, (2 * own_cells + index * FRAMES, 2 * own_cells + (2 + index) * FRAMES))
        spread_cells(row)
    left = columns[2 * own_cells :].astype(jnp.bfloat16)
    for output in range(window):
        several = jnp.dot(
            left,
            band[:, output * channels : (output + 1) * channels],
            preferred_element_type=jnp.float32,
        )
        for side in range(2):
            if side == 0 and output == window - 1 or side == 1 and output == 0:
                continue
            for index, row in enumerate((0, own + 1)):
                part = pl.ds(
                    row * FRAMES * pitch + output + side * (wide - window), FRAMES, stride=pitch
                )
                at = (2 * side + index) * FRAMES
                slope[part] = several[at : at + FRAMES] * state_terms(part)[1]
    for cell in range((own + 2) * FRAMES):
        part = pl.ds(cell * wide, wide)
        ready[part] = slope[cell * pitch : cell * pitch + wide] * spread
        state = hidden[cell // FRAMES, cell % FRAMES].astype(jnp.float32)
        normed_ref[part] = (state - group_mean) * inverse

    to_peers(sums_one)
    to_peers(arrived)
    to_peers(sums_two)

    @pl.when(me < n - 1)
    def _():
        to_right.wait_send()

    @pl.when(me > 0)
    def _():
        to_left.wait_send()

    from_peers(sums_two, 2)
    total = over_devices(sums_two)
    lane = lax.broadcasted_iota(jnp.int32, total.shape, 1)
    step = 1
    while step < per_group:
        total = total + jnp.where(
            lax.rem(lane // step, 2) == 0,
            pltpu.roll(total, channels - step, 1),
            pltpu.roll(total, step, 1),
        )
        step *= 2
    terms[0:2] = total * (inverse / cell_total)


def last_kernel(
    n, ready, normed_ref, terms, turned, paired, out_any, padded, windows, pairs, rest, out, out_sem
):
    me = lax.axis_index("row")
    own = out.shape[0]
    wide = out.shape[3]
    channels = out.shape[4]
    line = FRAMES * wide
    windows[:, FRAMES // 2] = jnp.zeros((own + 2, 2, wide, 3 * channels), jnp.bfloat16)
    pairs[1, :, FRAMES // 2 - 1] = jnp.zeros((own + 2, wide // 2, 4 * channels), jnp.bfloat16)
    pitch = wide + 1
    blank = jnp.zeros((1, channels), jnp.float32)
    for cell in range((own + 2) * FRAMES + 1):
        padded[cell * pitch : cell * pitch + 1] = blank
    first_part = jnp.broadcast_to(terms[0:1], (wide, channels))
    second_part = jnp.broadcast_to(terms[1:2], (wide, channels))
    for row in range(own + 2):
        for frame in range(FRAMES):
            cell = row * FRAMES + frame
            part = pl.ds(cell * wide, wide)
            state_grad = ready[part] - first_part - normed_ref[part] * second_part
            if row == 0:
                state_grad = jnp.where(me > 0, state_grad, 0.0)
            if row == own + 1:
                state_grad = jnp.where(me < n - 1, state_grad, 0.0)
            at = cell * pitch + 1
            padded[at : at + wide] = state_grad
            for col_tap in range(3):
                windows[
                    row, frame // 2, frame % 2, :, col_tap * channels : (col_tap + 1) * channels
                ] = padded[at + 1 - col_tap : at + 1 - col_tap + wide].astype(jnp.bfloat16)
            kind, step = frame % 2, frame // 2 - frame % 2
            if step >= 0:
                for index in range(4):
                    pairs[kind, row, step, :, index * channels : (index + 1) * channels] = padded[
                        pl.ds(cell * pitch + index, wide // 2, stride=2)
                    ].astype(jnp.bfloat16)
    half_line = line // 2
    for kind in range(2):
        left = jnp.concatenate(
            [
                pairs[kind, above : above + own].reshape(own * half_line // 2, 4 * channels)
                for above in range(3)
            ],
            axis=1,
        )
        both = jnp.dot(
            left,
            paired[kind].reshape(12 * channels, 2 * channels),
            preferred_element_type=jnp.float32,
        )
        for side in range(2):
            rest[kind, pl.ds(side, own * half_line // 2, stride=2)] = both[
                :, side * channels : (side + 1) * channels
            ]
    taken = jnp.concatenate(
        [
            windows[
                above : above + own, ahead // 2 : ahead // 2 + FRAMES // 2, ahead % 2
            ].reshape(own * half_line, 3 * channels)
            for above in range(3)
            for ahead in (1, 2)
        ],
        axis=1,
    )
    summed = jnp.dot(
        taken,
        turned[...].reshape(6 * 3 * channels, 2 * channels),
        preferred_element_type=jnp.float32,
    )
    for row in range(own):
        for side in range(2):
            out[row, :, side] = (
                (
                    summed[
                        row * half_line : (row + 1) * half_line,
                        side * channels : (side + 1) * channels,
                    ]
                    + rest[side, row * half_line : (row + 1) * half_line]
                )
                .reshape(FRAMES // 2, wide, channels)
                .astype(jnp.bfloat16)
            )
        pltpu.make_async_copy(out.at[row], out_any.at[row], out_sem).start()
    pltpu.make_async_copy(out, out_any, out_sem).wait()


def one_frame_each(
    frames,
    frame_owner,
    picks,
    patch_weight,
    patch_bias,
    norm_gain,
    head_weight,
    head_bias,
    head_out,
    hidden_state,
    group_gain,
    group_shift,
    out_weight,
    inner_weight,
):
    n = lax.axis_size("row")
    own, frame_count, wide, channels = hidden_state.shape
    height, strip = frames.shape[1:]
    pix, width = patch_weight.shape
    window = wide // 2 + 1
    depth = -(-27 * window // 128) * 128
    cells = (own + 2) * frame_count * wide
    f32, bf16 = jnp.float32, jnp.bfloat16
    vmem = pl.BlockSpec(memory_space=pltpu.VMEM)
    dma = pltpu.SemaphoreType.DMA
    passed = [
        pltpu.VMEM((cells, channels), f32),
        pltpu.VMEM((cells, channels), f32),
        pltpu.VMEM((8, channels), f32),
        pltpu.VMEM((3, 2, 3 * channels, 2 * channels), bf16),
        pltpu.VMEM((2, 3, 4 * channels, 2 * channels), bf16),
    ]
    kept = pl.pallas_call(
        functools.partial(fused_kernel, n),
        out_shape=passed,
        in_specs=[pl.BlockSpec(memory_space=pltpu.HBM)] * 14,
        out_specs=[vmem] * 5,
        scratch_shapes=[
            pltpu.VMEM((3, strip, height), bf16),
            pltpu.SMEM(frame_owner.shape, jnp.int32),
            pltpu.SMEM(picks.shape, jnp.int32),
            pltpu.VMEM((4, 1, width), f32),
            pltpu.VMEM((2, 1, channels), f32),
            pltpu.VMEM(out_weight.shape, bf16),
            pltpu.VMEM((pix, width), bf16),
            pltpu.VMEM(head_weight.shape, bf16),
            pltpu.VMEM((own + 2, frame_count, wide, channels), bf16),
            pltpu.VMEM(inner_weight.shape, bf16),
            pltpu.VMEM(frames.shape, f32),
            pltpu.VMEM((-(-(height // PATCH) // 8) * 8, pix), f32),
            pltpu.VMEM((height + 4, 1, 128), f32),
            pltpu.VMEM((n, (own + 5) // 2, 1, 128), f32),
            pltpu.VMEM(((own + 5) // 2, frame_count + 8, 128), f32),
            pltpu.VMEM((2 * (own + 2) * frame_count, depth), f32),
            pltpu.VMEM((128, channels), f32),
            pltpu.VMEM((depth, window * channels), bf16),
            pltpu.VMEM(((own + 2) * frame_count * (wide + 1), channels), f32),
            pltpu.VMEM(((own + 2) * frame_count * (wide + 1), channels), f32),
            pltpu.VMEM((wide, own * frame_count, channels), f32),
            pltpu.VMEM((wide, own * frame_count, channels), f32),
            pltpu.VMEM((n, 2, channels), f32),
            pltpu.VMEM((n, 2, channels), f32),
            dma((8,)),
            dma,
            dma((5,)),
        ],
        compiler_params=pltpu.CompilerParams(
            collective_id=0, has_side_effects=True, vmem_limit_bytes=32 << 20
        ),
    )(
        *(
            pltpu.with_memory_space_constraint(array, pltpu.HBM)
            for array in (
                frames.transpose(0, 2, 1),
                frame_owner,
                picks,
                patch_weight,
                patch_bias[None],
                norm_gain[None],
                head_weight,
                head_bias[None],
                head_out[None],
                hidden_state,
                group_gain[None],
                group_shift[None],
                out_weight,
                inner_weight,
            )
        )
    )
    out_shape = (own, frame_count // 2, 2, wide, channels)
    return pl.pallas_call(
        functools.partial(last_kernel, n),
        out_shape=jax.ShapeDtypeStruct(out_shape, bf16),
        in_specs=[vmem] * 5,
        out_specs=pl.BlockSpec(memory_space=pltpu.HBM),
        scratch_shapes=[
            pltpu.VMEM((-(-((own + 2) * frame_count * (wide + 1) + 1) // 8) * 8, channels), f32),
            pltpu.VMEM((own + 2, frame_count // 2 + 1, 2, wide, 3 * channels), bf16),
            pltpu.VMEM((2, own + 2, frame_count // 2, wide // 2, 4 * channels), bf16),
            pltpu.VMEM((2, own * frame_count * wide // 2, channels), f32),
            pltpu.VMEM(out_shape, bf16),
            dma,
        ],
        compiler_params=pltpu.CompilerParams(vmem_limit_bytes=32 << 20),
    )(*kept).reshape(hidden_state.shape)


def solution(mesh):
    body = one_frame_each if mesh.shape["row"] == FRAMES else per_device
    return jax.shard_map(
        body,
        mesh=mesh,
        in_specs=(
            P(None, None, ("clip", "row")),
            P("clip"),
            P("clip"),
            P(),
            P(),
            P(),
            P(),
            P(),
            P(),
            P(("clip", "row"), None, None, None),
            P(),
            P(),
            P(),
            P(),
        ),
        out_specs=P(("clip", "row"), None, None, None),
        check_vma=False,
    )
```

```python
import functools

import jax
import jax.numpy as jnp
from jax import lax
from jax.experimental import pallas as pl
from jax.experimental.pallas import tpu as pltpu
from jax.sharding import PartitionSpec as P

PATCH = 16
GROUPS = 32
FRAMES = 16


eps_norm = 1e-06
MESH = pl.DeviceIdType.MESH


def extended(block, sides, width):
    for axis, dim in sides:
        count = lax.axis_size(axis)
        forward = [(i, i + 1) for i in range(count - 1)]
        backward = [(target, source) for source, target in forward]
        low = lax.ppermute(
            lax.slice_in_dim(block, block.shape[dim] - width, None, axis=dim), axis, forward
        )
        high = lax.ppermute(lax.slice_in_dim(block, 0, width, axis=dim), axis, backward)
        block = jnp.concatenate([low, block, high], axis=dim)
    return block


def silu_slope(values):
    sigmoid = jax.nn.sigmoid(values)
    return sigmoid * (1.0 + values * (1.0 - sigmoid))


def to_tokens(pixels):
    channels, height, columns = pixels.shape
    shaped = pixels.reshape(channels, height // PATCH, PATCH, columns // PATCH, PATCH)
    return shaped.transpose(1, 3, 0, 2, 4).reshape(
        height // PATCH * (columns // PATCH), channels * PATCH * PATCH
    )


def from_tokens(token_grads, height, columns):
    shaped = token_grads.reshape(height // PATCH, columns // PATCH, 3, PATCH, PATCH)
    return shaped.transpose(2, 0, 3, 1, 4).reshape(3, height, columns)


def pixel_back(padded, out_weight, amount):
    frame_count = padded.shape[2]
    columns = padded.shape[3]
    widened = jnp.pad(padded, ((0, 0), (0, 0), (0, 2), (1, 1)))
    windows = []
    for time_tap in range(3):
        for row_tap in range(3):
            for col_tap in range(3):
                windows.append(
                    widened[
                        :,
                        2 - row_tap : 2 - row_tap + amount,
                        2 - time_tap : 2 - time_tap + frame_count,
                        2 - col_tap : 2 - col_tap + columns,
                    ]
                )
    stacked = jnp.stack(windows, 0).reshape(27 * 3, amount * frame_count * columns)
    kernel = out_weight.reshape(27 * 3, out_weight.shape[4])
    summed = lax.dot_general(
        stacked, kernel, (((0,), (0,)), ((), ())), preferred_element_type=jnp.float32
    )
    return summed.reshape(amount, frame_count, columns, out_weight.shape[4])


def inner_back(padded, inner_weight, amount):
    frame_count = padded.shape[1]
    columns = padded.shape[2]
    channel_count = padded.shape[3]
    widened = jnp.pad(padded, ((0, 0), (0, 2), (1, 1), (0, 0)))
    summed = jnp.zeros((amount * frame_count * columns, inner_weight.shape[3]), jnp.float32)
    for time_tap in range(3):
        windows = []
        for row_tap in range(3):
            for col_tap in range(3):
                windows.append(
                    widened[
                        2 - row_tap : 2 - row_tap + amount,
                        2 - time_tap : 2 - time_tap + frame_count,
                        2 - col_tap : 2 - col_tap + columns,
                        :,
                    ]
                )
        joined = jnp.concatenate(windows, axis=3).reshape(
            amount * frame_count * columns, 9 * channel_count
        )
        kernel = jnp.transpose(inner_weight[time_tap], (0, 1, 3, 2)).reshape(
            9 * channel_count, inner_weight.shape[3]
        )
        summed = summed + jnp.dot(joined, kernel, preferred_element_type=jnp.float32)
    return summed.reshape(amount, frame_count, columns, inner_weight.shape[3])


def group_back(state_rows, slope_in, group_mean, inverse, group_gain, group_shift, cell_total):
    grouped = state_rows.astype(jnp.float32).reshape(state_rows.shape[:3] + (GROUPS, -1))
    gain_table = group_gain.reshape(GROUPS, -1)
    shift_table = group_shift.reshape(GROUPS, -1)
    normed_state = (grouped - group_mean[:, None]) * inverse[:, None]
    affine = normed_state * gain_table + shift_table
    upstream = slope_in.reshape(grouped.shape) * silu_slope(affine) * gain_table
    group_terms = lax.psum(
        (jnp.sum(upstream, axis=(0, 1, 2, 4)), jnp.sum(upstream * normed_state, axis=(0, 1, 2, 4))),
        "row",
    )
    first_part = group_terms[0] / cell_total
    second_part = group_terms[1] / cell_total
    state_grad = (upstream - first_part[:, None] - normed_state * second_part[:, None]) * inverse[
        :, None
    ]
    return state_grad.reshape(state_rows.shape).astype(jnp.bfloat16)


def per_device(
    frames,
    frame_owner,
    picks,
    patch_weight,
    patch_bias,
    norm_gain,
    head_weight,
    head_bias,
    head_out,
    hidden_state,
    group_gain,
    group_shift,
    out_weight,
    inner_weight,
):
    devices = lax.axis_size("row")
    position = lax.axis_index("row")
    per_frame = devices // FRAMES
    slot = position // per_frame
    height = frames.shape[1]
    strip = frames.shape[2]
    own_rows = hidden_state.shape[0]
    frame_width = hidden_state.shape[2]
    tokens = to_tokens(frames)
    embedded = jnp.dot(tokens, patch_weight, preferred_element_type=jnp.float32) + patch_bias
    centred = embedded - jnp.mean(embedded, axis=1, keepdims=True)
    inv_spread = lax.rsqrt(jnp.mean(centred * centred, axis=1, keepdims=True) + eps_norm)
    normed = centred * inv_spread
    slot_mask = (jnp.arange(FRAMES, dtype=jnp.int32) == slot).astype(jnp.float32)
    partial_pool = slot_mask[:, None] * jnp.sum(normed * norm_gain, axis=0)[None, :]
    grouped = hidden_state.reshape(own_rows, FRAMES, frame_width, GROUPS, -1)
    first_sum = jnp.sum(grouped, axis=(0, 1, 2, 4), dtype=jnp.float32)
    second_sum = jnp.sum(jnp.square(grouped.astype(jnp.float32)), axis=(0, 1, 2, 4))
    pooled_sum, first_total, second_total = lax.psum((partial_pool, first_sum, second_sum), "row")
    frame_tokens = height // PATCH * (strip * per_frame // PATCH)
    pooled = pooled_sum / frame_tokens
    head_full = head_weight.astype(jnp.float32)
    before = jnp.dot(pooled, head_full, precision=lax.Precision.HIGHEST) + head_bias
    pulled = jnp.dot(head_out * silu_slope(before), head_full.T, precision=lax.Precision.HIGHEST)
    picked = jnp.sum((picks[:, None] == frame_owner[None, :]).astype(jnp.float32), axis=0)
    slot_grad = jnp.dot(slot_mask * picked, pulled, precision=lax.Precision.HIGHEST)
    scaled = norm_gain * slot_grad
    token_grad = inv_spread * (
        scaled - jnp.mean(scaled) - normed * jnp.mean(scaled * normed, axis=1, keepdims=True)
    )
    patch_grad = lax.dot_general(
        token_grad.astype(jnp.bfloat16),
        patch_weight,
        (((1,), (1,)), ((), ())),
        preferred_element_type=jnp.float32,
    )
    pixel_local = from_tokens(patch_grad, height, strip).astype(jnp.bfloat16)
    arrived = lax.all_to_all(pixel_local, "row", split_axis=1, concat_axis=2, tiled=True)
    by_slot = arrived.reshape(3, own_rows, FRAMES, frame_width)
    owner_table = (frame_owner[:, None] == jnp.arange(FRAMES, dtype=jnp.int32)[None, :]).astype(
        jnp.bfloat16
    )
    ordered = jnp.einsum(
        "krbw,bf->krfw", by_slot, owner_table, preferred_element_type=jnp.float32
    ).astype(jnp.bfloat16)
    cell_total = own_rows * devices * FRAMES * frame_width * (hidden_state.shape[3] // GROUPS)
    group_mean = first_total / cell_total
    inverse = lax.rsqrt(second_total / cell_total - group_mean * group_mean + eps_norm)
    pixel_padded = extended(ordered, (("row", 1),), 1)
    slope_in = pixel_back(pixel_padded, out_weight, own_rows)
    state_grad = group_back(
        hidden_state, slope_in, group_mean, inverse, group_gain, group_shift, cell_total
    )
    grad_padded = extended(state_grad, (("row", 0),), 1)
    return inner_back(grad_padded, inner_weight, own_rows).astype(jnp.bfloat16)


def split_rows(row):
    high = row.astype(jnp.bfloat16).astype(jnp.float32)
    rest = row - high
    middle = rest.astype(jnp.bfloat16).astype(jnp.float32)
    low = rest - middle
    index = lax.broadcasted_iota(jnp.int32, (8, row.shape[1]), 0)
    stacked = jnp.where(
        index == 0, high, jnp.where(index == 1, middle, jnp.where(index == 2, low, 0.0))
    )
    return stacked.astype(jnp.bfloat16)


def fused_kernel(
    n,
    frames_any,
    owner_any,
    picks_any,
    patch_any,
    patch_bias_any,
    norm_gain_any,
    head_any,
    head_bias_any,
    head_out_any,
    hidden_any,
    group_gain_any,
    group_shift_any,
    out_weight_any,
    inner_any,
    ready,
    normed_ref,
    terms,
    turned,
    paired,
    frames,
    owner,
    picks,
    wide_rows,
    group_rows,
    out_weight,
    patch_w,
    head_w,
    hidden,
    inner_w,
    pixels,
    tokens,
    sent,
    arrived,
    by_frame,
    columns,
    taps,
    band,
    slope,
    cells,
    factor,
    centred_cells,
    sums_one,
    sums_two,
    local_sem,
    send_sem,
    recv_sem,
):
    me = lax.axis_index("row")
    strip, height = frames.shape[1], frames.shape[2]
    patch_rows = height // PATCH
    own = hidden.shape[0] - 2
    wide = hidden.shape[2]
    channels = hidden.shape[3]
    line = FRAMES * wide
    pitch = wide + 1
    per_group = channels // GROUPS
    cell_total = own * n * FRAMES * wide * per_group
    window = wide // 2 + 1
    piece = 3 * window
    slot_lanes = 64
    half = arrived.shape[1]

    def peer(offset):
        target = me
        step = 1
        while step < n:
            if offset // step % 2:
                target = target + step * (1 - 2 * lax.rem(lax.div(me, step), 2))
            step *= 2
        return target

    farthest_first = range(n - 1, 0, -1)

    barrier = pltpu.get_barrier_semaphore()
    for offset in farthest_first:
        pl.semaphore_signal(barrier, inc=1, device_id={"row": peer(offset)}, device_id_type=MESH)

    load_frames = pltpu.make_async_copy(frames_any, frames, local_sem.at[0])
    load_hidden = pltpu.make_async_copy(hidden_any, hidden.at[pl.ds(1, own)], local_sem.at[1])
    pix, width = patch_w.shape
    third, part_rows = pix // 3, width // 2
    load_patch = [
        pltpu.make_async_copy(
            patch_any.at[pl.ds(part * third, third)],
            patch_w.at[pl.ds(part * third, third)],
            local_sem.at[2 + part],
        )
        for part in range(3)
    ]
    load_head = [
        pltpu.make_async_copy(
            head_any.at[pl.ds(part * part_rows, part_rows)],
            head_w.at[pl.ds(part * part_rows, part_rows)],
            local_sem.at[5 + part],
        )
        for part in range(2)
    ]
    load_inner = pltpu.make_async_copy(inner_any, inner_w, local_sem.at[7])
    load_out = pltpu.make_async_copy(out_weight_any, out_weight, local_sem.at[7])
    load_owner = pltpu.make_async_copy(owner_any, owner, local_sem.at[7])
    load_picks = pltpu.make_async_copy(picks_any, picks, local_sem.at[7])
    load_wide = [
        pltpu.make_async_copy(source, wide_rows.at[index], local_sem.at[1])
        for index, source in enumerate((patch_bias_any, norm_gain_any, head_bias_any, head_out_any))
    ]
    load_group = [
        pltpu.make_async_copy(source, group_rows.at[index], local_sem.at[7])
        for index, source in enumerate((group_gain_any, group_shift_any))
    ]
    load_frames.start()
    load_hidden.start()
    for load in load_wide:
        load.start()
    for load in load_patch + load_head:
        load.start()
    load_owner.start()
    load_picks.start()
    for load in load_group:
        load.start()
    load_out.start()
    load_inner.start()

    group_row = lax.broadcasted_iota(jnp.int32, (channels, channels), 0) // per_group
    group_col = lax.broadcasted_iota(jnp.int32, (channels, channels), 1) // per_group
    same_group = (group_row == group_col).astype(jnp.bfloat16)
    eight = lax.broadcasted_iota(jnp.int32, (8, channels), 0)
    spot = lax.broadcasted_iota(jnp.int32, (2, channels), 0)

    def group_sums(first, second):
        part = lax.rem(eight, 4)
        row = jnp.where(eight < 4, first, second)
        high = row.astype(jnp.bfloat16).astype(jnp.float32)
        rest = row - high
        middle = rest.astype(jnp.bfloat16).astype(jnp.float32)
        stacked = jnp.where(
            part == 0, high, jnp.where(part == 1, middle, jnp.where(part == 2, rest - middle, 0.0))
        )
        summed = jnp.dot(
            stacked.astype(jnp.bfloat16), same_group, preferred_element_type=jnp.float32
        )
        return (
            jnp.sum(summed[0:4], axis=0, keepdims=True),
            jnp.sum(summed[4:8], axis=0, keepdims=True),
        )

    def tree_sum(blocks):
        while len(blocks) > 1:
            blocks = [
                blocks[at] + blocks[at + 1] if at + 1 < len(blocks) else blocks[at]
                for at in range(0, len(blocks), 2)
            ]
        return blocks[0]

    def over_devices(buffer):
        return tree_sum([buffer[slot] for slot in range(n)])

    load_frames.wait()
    for colour in range(3):
        pixels[colour] = frames[colour].astype(jnp.float32).T
    tokens[...] = jnp.zeros_like(tokens)
    for colour in range(3):
        for line_in in range(PATCH):
            at = (colour * PATCH + line_in) * PATCH
            tokens[0:patch_rows, at : at + PATCH] = pixels[
                colour, pl.ds(line_in, patch_rows, stride=PATCH), :
            ]
    sent[...] = jnp.zeros_like(sent)

    load_hidden.wait()
    pltpu.make_async_copy(wide_rows, wide_rows, local_sem.at[1]).wait()
    first = jnp.zeros((1, channels), jnp.float32)
    second = jnp.zeros((1, channels), jnp.float32)
    for row in range(own):
        state = hidden[1 + row].reshape(line, channels).astype(jnp.float32)
        first = first + jnp.sum(state, axis=0, keepdims=True)
        second = second + jnp.sum(state * state, axis=0, keepdims=True)
    first, second = group_sums(first, second)
    sums_one[me] = jnp.where(spot == 0, first, second)

    embedded = wide_rows[0]
    for part in range(3):
        load_patch[part].wait()
        embedded = embedded + jnp.dot(
            tokens[:, part * third : (part + 1) * third].astype(jnp.bfloat16),
            patch_w[part * third : (part + 1) * third],
            preferred_element_type=jnp.float32,
        )
    centred = embedded - jnp.mean(embedded, axis=1, keepdims=True)
    inv_spread = lax.rsqrt(jnp.mean(centred * centred, axis=1, keepdims=True) + eps_norm)
    normed = centred * inv_spread
    gain = wide_rows[1]
    pooled = jnp.sum((normed * gain)[0:patch_rows], axis=0, keepdims=True) / patch_rows
    split_pool = split_rows(pooled)
    before = wide_rows[2]
    for part in range(2):
        load_head[part].wait()
        before = before + jnp.sum(
            jnp.dot(
                split_pool[:, part * part_rows : (part + 1) * part_rows],
                head_w[part * part_rows : (part + 1) * part_rows],
                preferred_element_type=jnp.float32,
            ),
            axis=0,
            keepdims=True,
        )
    pulled = jnp.sum(
        lax.dot_general(
            split_rows(wide_rows[3] * silu_slope(before)),
            head_w[...],
            (((1,), (1,)), ((), ())),
            preferred_element_type=jnp.float32,
        ),
        axis=0,
        keepdims=True,
    )
    load_owner.wait()
    load_picks.wait()
    pltpu.make_async_copy(group_rows, group_rows, local_sem.at[7]).wait()
    load_out.wait()
    load_inner.wait()
    mine = owner[me]
    picked = jnp.float32(0.0)
    for pick in range(picks.shape[0]):
        picked = picked + jnp.where(picks[pick] == mine, jnp.float32(1.0), jnp.float32(0.0))
    scaled = gain * (picked * pulled)
    token_grad = inv_spread * (
        scaled
        - jnp.mean(scaled, axis=1, keepdims=True)
        - normed * jnp.mean(scaled * normed, axis=1, keepdims=True)
    )
    token_grad = token_grad.astype(jnp.bfloat16)
    sixth = pix // 6
    cuts = (0, 3, 6)
    patch_grad = jnp.concatenate(
        [
            lax.dot_general(
                token_grad,
                patch_w[low * sixth : high * sixth],
                (((1,), (1,)), ((), ())),
                preferred_element_type=jnp.float32,
            )
            for low, high in zip(cuts[:-1], cuts[1:])
        ],
        axis=1,
    )
    patch_grad = patch_grad.astype(jnp.bfloat16).astype(jnp.float32)
    for line_in in range(PATCH):
        lines = [
            patch_grad[:, (colour * PATCH + line_in) * PATCH : (colour * PATCH + line_in + 1) * PATCH]
            for colour in range(3)
        ]
        joined = jnp.concatenate(
            [line_of[:, 0:window] for line_of in lines]
            + [jnp.zeros((lines[0].shape[0], slot_lanes - 2 * piece), jnp.float32)]
            + [line_of[:, wide - window : wide] for line_of in lines],
            axis=1,
        )
        for patch_row in range(patch_rows):
            at = 2 + patch_row * PATCH + line_in
            sent[at, :, 0:slot_lanes] = joined[patch_row : patch_row + 1]
            if at >= half:
                sent[at - half, :, slot_lanes : 2 * slot_lanes] = joined[patch_row : patch_row + 1]

    pl.semaphore_wait(barrier, n - 1)

    def send_sums(buffer, kind, offset):
        pltpu.make_async_remote_copy(
            src_ref=buffer.at[me],
            dst_ref=buffer.at[me],
            send_sem=send_sem,
            recv_sem=recv_sem.at[kind],
            device_id={"row": peer(offset)},
            device_id_type=MESH,
        ).start()

    def from_peers(buffer, kind):
        others = buffer.at[pl.ds(0, n - 1)]
        pltpu.make_async_copy(others, others, recv_sem.at[kind]).wait()

    def to_peers(buffer):
        others = buffer.at[pl.ds(0, n - 1)]
        pltpu.make_async_copy(others, others, send_sem).wait()

    for offset in farthest_first:
        target = peer(offset)
        pltpu.make_async_remote_copy(
            src_ref=sent.at[pl.ds(target * own, half)],
            dst_ref=arrived.at[me],
            send_sem=send_sem,
            recv_sem=recv_sem.at[1],
            device_id={"row": target},
            device_id_type=MESH,
        ).start()
        send_sums(sums_one, 0, offset)
    to_right = pltpu.make_async_remote_copy(
        src_ref=hidden_any.at[pl.ds(own - 1, 1)],
        dst_ref=hidden.at[pl.ds(0, 1)],
        send_sem=send_sem,
        recv_sem=recv_sem.at[3],
        device_id={"row": lax.rem(me + 1, n)},
        device_id_type=MESH,
    )
    to_left = pltpu.make_async_remote_copy(
        src_ref=hidden_any.at[pl.ds(0, 1)],
        dst_ref=hidden.at[pl.ds(own + 1, 1)],
        send_sem=send_sem,
        recv_sem=recv_sem.at[4],
        device_id={"row": lax.rem(me + n - 1, n)},
        device_id_type=MESH,
    )

    @pl.when(me < n - 1)
    def _():
        to_right.start()

    @pl.when(me > 0)
    def _():
        to_left.start()

    @pl.when(me == 0)
    def _():
        hidden[0] = jnp.zeros(hidden.shape[1:], hidden.dtype)

    @pl.when(me == n - 1)
    def _():
        hidden[own + 1] = jnp.zeros(hidden.shape[1:], hidden.dtype)

    arrived[me] = sent[pl.ds(me * own, half)]

    taps[...] = jnp.zeros_like(taps)
    for time_tap in range(3):
        for row_tap in range(3):
            for col_tap in range(3):
                at = ((time_tap * 3 + row_tap) * 3 + col_tap) * 3
                taps[at : at + 3] = out_weight[time_tap, row_tap, col_tap].astype(jnp.float32)
    flat_taps = taps[...].astype(jnp.bfloat16)
    depth = band.shape[0]
    entry = lax.broadcasted_iota(jnp.int32, (depth, channels), 0)
    tap_lane = lax.broadcasted_iota(jnp.int32, (depth, channels), 1)
    tap_of = entry // piece
    column = lax.rem(entry, window)
    first_lane = (
        (lax.rem(tap_of, 3) * 3 + tap_of // 3) * 9 + lax.rem(entry, piece) // window - 3 * column
    )
    for output in range(window):
        col_tap = output + 1 - column
        chosen = (
            (tap_lane == first_lane + 3 * (output + 1))
            & (col_tap >= 0)
            & (col_tap < 3)
            & (entry < 9 * piece)
        )
        band[:, output * channels : (output + 1) * channels] = jnp.dot(
            chosen.astype(jnp.float32).astype(jnp.bfloat16),
            flat_taps,
            preferred_element_type=jnp.float32,
        ).astype(jnp.bfloat16)
    columns[...] = jnp.zeros_like(columns)
    by_frame[...] = jnp.zeros_like(by_frame)

    slot_of = []
    for frame in range(FRAMES):
        found = jnp.int32(0)
        for slot in range(n):
            found = jnp.where(owner[slot] == frame, jnp.int32(slot), found)
        slot_of.append(found)


    def spread_cells(row):
        for frame in range(FRAMES):
            at = (row * FRAMES + frame) * pitch
            cells[at : at + wide] = hidden[row, frame].astype(jnp.float32)

    for row in range(1, own + 1):
        spread_cells(row)

    empty = jnp.zeros((channels, channels), jnp.bfloat16)
    for row_tap in range(3):
        above = 2 - row_tap
        for col_tap in range(3):
            part = pl.ds(col_tap * channels, channels)
            blocks = [inner_w[time_tap, row_tap, col_tap].T for time_tap in range(3)]
            for ahead in range(2):
                turned[above, ahead, part, 0:channels] = blocks[1 - ahead]
                turned[above, ahead, part, channels:] = blocks[2 - ahead]
            for side in range(2):
                at = (2 - col_tap + side) * channels
                for kind in range(2):
                    paired[kind, above, at : at + channels, side * channels : (side + 1) * channels] = (
                        blocks[2 - 2 * kind]
                    )
        for kind in range(2):
            paired[kind, above, 3 * channels :, 0:channels] = empty
            paired[kind, above, 0:channels, channels:] = empty

    from_peers(sums_one, 0)
    from_peers(arrived, 1)
    means = over_devices(sums_one) / cell_total
    group_mean = means[0:1]
    inverse = lax.rsqrt(means[1:2] - group_mean * group_mean + eps_norm)
    group_gain = group_rows[0]
    group_shift = group_rows[1]
    def pixel_taps(row, block):
        for row_tap in range(3):
            for time_tap in range(3):
                at = (row_tap * 3 + time_tap) * piece
                source = row - row_tap + 2
                for side in range(2):
                    lane = source // half * slot_lanes + side * (slot_lanes - piece)
                    columns[block[side] : block[side] + FRAMES, at : at + piece] = by_frame[
                        source % half, 2 - time_tap : 2 - time_tap + FRAMES, lane : lane + piece
                    ]

    spread = inverse * group_gain

    def state_terms(part):
        centred = cells[part] - group_mean
        return centred, silu_slope(centred * spread + group_shift)

    own_cells = own * FRAMES
    for w in range(wide):
        part = pl.ds(FRAMES * pitch + w, own_cells, stride=pitch)
        centred_cells[w], factor[w] = state_terms(part)
    for frame in range(FRAMES):
        for row in range(half):
            by_frame[row, frame : frame + 1, :] = arrived[slot_of[frame], row]
    for row in range(1, own + 1):
        pixel_taps(row, ((row - 1) * FRAMES, own_cells + (row - 1) * FRAMES))
    left = columns[0 : 2 * own_cells].astype(jnp.bfloat16)
    firsts, seconds = [], []
    for output in range(0, window, 2):
        lanes = pl.ds(output * channels, min(2, window - output) * channels)
        several = jnp.dot(left, band[:, lanes], preferred_element_type=jnp.float32)
        for index in range(several.shape[1] // channels):
            for side in range(2):
                w = output + index + side * (wide - window)
                if side == 0 and output + index == window - 1 or side == 1 and output + index == 0:
                    continue
                upstream = (
                    several[
                        side * own_cells : (side + 1) * own_cells,
                        index * channels : (index + 1) * channels,
                    ]
                    * factor[w]
                )
                slope[pl.ds(FRAMES * pitch + w, own_cells, stride=pitch)] = upstream
                firsts.append(jnp.sum(upstream.reshape(-1, 8, channels), axis=0))
                seconds.append(
                    jnp.sum((upstream * centred_cells[w]).reshape(-1, 8, channels), axis=0)
                )
    first = tree_sum(firsts)
    second = tree_sum(seconds)
    first = jnp.sum(first, axis=0, keepdims=True) * group_gain
    second = jnp.sum(second, axis=0, keepdims=True) * spread
    sums_two[me] = jnp.where(spot == 0, first, second)
    for offset in farthest_first:
        send_sums(sums_two, 2, offset)


    @pl.when(me < n - 1)
    def _():
        to_left.wait_recv()

    @pl.when(me > 0)
    def _():
        to_right.wait_recv()

    for index, row in enumerate((0, own + 1)):
        pixel_taps(row, (2 * own_cells + index * FRAMES, 2 * own_cells + (2 + index) * FRAMES))
        spread_cells(row)
    left = columns[2 * own_cells :].astype(jnp.bfloat16)
    for output in range(window):
        several = jnp.dot(
            left,
            band[:, output * channels : (output + 1) * channels],
            preferred_element_type=jnp.float32,
        )
        for side in range(2):
            if side == 0 and output == window - 1 or side == 1 and output == 0:
                continue
            for index, row in enumerate((0, own + 1)):
                part = pl.ds(
                    row * FRAMES * pitch + output + side * (wide - window), FRAMES, stride=pitch
                )
                at = (2 * side + index) * FRAMES
                slope[part] = several[at : at + FRAMES] * state_terms(part)[1]
    terms[2:3] = inverse / cell_total
    for cell in range((own + 2) * FRAMES):
        part = pl.ds(cell * wide, wide)
        ready[part] = slope[cell * pitch : cell * pitch + wide] * spread
        state = hidden[cell // FRAMES, cell % FRAMES].astype(jnp.float32)
        normed_ref[part] = (state - group_mean) * inverse

    to_peers(sums_one)
    to_peers(arrived)
    to_peers(sums_two)

    @pl.when(me < n - 1)
    def _():
        to_right.wait_send()

    @pl.when(me > 0)
    def _():
        to_left.wait_send()

    from_peers(sums_two, 2)
    terms[0:2] = over_devices(sums_two)


def last_kernel(
    n, ready, normed_ref, terms, turned, paired, out_any, padded, windows, pairs, rest, out, out_sem
):
    me = lax.axis_index("row")
    own = out.shape[0]
    wide = out.shape[3]
    channels = out.shape[4]
    line = FRAMES * wide
    windows[:, FRAMES // 2, 0] = jnp.zeros((own + 2, wide, 3 * channels), jnp.bfloat16)
    pairs[1, :, FRAMES // 2 - 1] = jnp.zeros((own + 2, wide // 2, 4 * channels), jnp.bfloat16)
    pitch = wide + 1
    blank = jnp.zeros((1, channels), jnp.float32)
    for cell in range((own + 2) * FRAMES + 1):
        padded[cell * pitch : cell * pitch + 1] = blank
    total = terms[0:2]
    lane = lax.broadcasted_iota(jnp.int32, total.shape, 1)
    step = 1
    while step < channels // GROUPS:
        total = total + jnp.where(
            lax.rem(lane // step, 2) == 0,
            pltpu.roll(total, channels - step, 1),
            pltpu.roll(total, step, 1),
        )
        step *= 2
    total = total * terms[2:3]
    first_part = jnp.broadcast_to(total[0:1], (wide, channels))
    second_part = jnp.broadcast_to(total[1:2], (wide, channels))
    for row in range(own + 2):
        for frame in range(FRAMES):
            cell = row * FRAMES + frame
            part = pl.ds(cell * wide, wide)
            state_grad = ready[part] - first_part - normed_ref[part] * second_part
            if row == 0:
                state_grad = jnp.where(me > 0, state_grad, 0.0)
            if row == own + 1:
                state_grad = jnp.where(me < n - 1, state_grad, 0.0)
            at = cell * pitch + 1
            padded[at : at + wide] = state_grad
            for col_tap in range(3 if frame > 0 else 0):
                windows[
                    row, frame // 2, frame % 2, :, col_tap * channels : (col_tap + 1) * channels
                ] = padded[at + 1 - col_tap : at + 1 - col_tap + wide].astype(jnp.bfloat16)
            kind, step = frame % 2, frame // 2 - frame % 2
            if step >= 0:
                for index in range(4):
                    pairs[kind, row, step, :, index * channels : (index + 1) * channels] = padded[
                        pl.ds(cell * pitch + index, wide // 2, stride=2)
                    ].astype(jnp.bfloat16)
    half_line = line // 2
    for kind in range(2):
        left = jnp.concatenate(
            [
                pairs[kind, above : above + own].reshape(own * half_line // 2, 4 * channels)
                for above in range(3)
            ],
            axis=1,
        )
        both = jnp.dot(
            left,
            paired[kind].reshape(12 * channels, 2 * channels),
            preferred_element_type=jnp.float32,
        )
        for side in range(2):
            rest[kind, pl.ds(side, own * half_line // 2, stride=2)] = both[
                :, side * channels : (side + 1) * channels
            ]
    taken = jnp.concatenate(
        [
            windows[
                above : above + own, ahead // 2 : ahead // 2 + FRAMES // 2, ahead % 2
            ].reshape(own * half_line, 3 * channels)
            for above in range(3)
            for ahead in (1, 2)
        ],
        axis=1,
    )
    summed = jnp.dot(
        taken,
        turned[...].reshape(6 * 3 * channels, 2 * channels),
        preferred_element_type=jnp.float32,
    )
    for row in range(own):
        for side in range(2):
            out[row, :, side] = (
                (
                    summed[
                        row * half_line : (row + 1) * half_line,
                        side * channels : (side + 1) * channels,
                    ]
                    + rest[side, row * half_line : (row + 1) * half_line]
                )
                .reshape(FRAMES // 2, wide, channels)
                .astype(jnp.bfloat16)
            )
        pltpu.make_async_copy(out.at[row], out_any.at[row], out_sem).start()
    pltpu.make_async_copy(out, out_any, out_sem).wait()


def one_frame_each(
    frames,
    frame_owner,
    picks,
    patch_weight,
    patch_bias,
    norm_gain,
    head_weight,
    head_bias,
    head_out,
    hidden_state,
    group_gain,
    group_shift,
    out_weight,
    inner_weight,
):
    n = lax.axis_size("row")
    own, frame_count, wide, channels = hidden_state.shape
    height, strip = frames.shape[1:]
    pix, width = patch_weight.shape
    window = wide // 2 + 1
    depth = -(-27 * window // 128) * 128
    cells = (own + 2) * frame_count * wide
    f32, bf16 = jnp.float32, jnp.bfloat16
    vmem = pl.BlockSpec(memory_space=pltpu.VMEM)
    dma = pltpu.SemaphoreType.DMA
    passed = [
        pltpu.VMEM((cells, channels), f32),
        pltpu.VMEM((cells, channels), f32),
        pltpu.VMEM((8, channels), f32),
        pltpu.VMEM((3, 2, 3 * channels, 2 * channels), bf16),
        pltpu.VMEM((2, 3, 4 * channels, 2 * channels), bf16),
    ]
    kept = pl.pallas_call(
        functools.partial(fused_kernel, n),
        out_shape=passed,
        in_specs=[pl.BlockSpec(memory_space=pltpu.HBM)] * 14,
        out_specs=[vmem] * 5,
        scratch_shapes=[
            pltpu.VMEM((3, strip, height), bf16),
            pltpu.SMEM(frame_owner.shape, jnp.int32),
            pltpu.SMEM(picks.shape, jnp.int32),
            pltpu.VMEM((4, 1, width), f32),
            pltpu.VMEM((2, 1, channels), f32),
            pltpu.VMEM(out_weight.shape, bf16),
            pltpu.VMEM((pix, width), bf16),
            pltpu.VMEM(head_weight.shape, bf16),
            pltpu.VMEM((own + 2, frame_count, wide, channels), bf16),
            pltpu.VMEM(inner_weight.shape, bf16),
            pltpu.VMEM(frames.shape, f32),
            pltpu.VMEM((-(-(height // PATCH) // 8) * 8, pix), f32),
            pltpu.VMEM((height + 4, 1, 128), f32),
            pltpu.VMEM((n, (own + 5) // 2, 1, 128), f32),
            pltpu.VMEM(((own + 5) // 2, frame_count + 8, 128), f32),
            pltpu.VMEM((2 * (own + 2) * frame_count, depth), f32),
            pltpu.VMEM((128, channels), f32),
            pltpu.VMEM((depth, window * channels), bf16),
            pltpu.VMEM(((own + 2) * frame_count * (wide + 1), channels), f32),
            pltpu.VMEM(((own + 2) * frame_count * (wide + 1), channels), f32),
            pltpu.VMEM((wide, own * frame_count, channels), f32),
            pltpu.VMEM((wide, own * frame_count, channels), f32),
            pltpu.VMEM((n, 2, channels), f32),
            pltpu.VMEM((n, 2, channels), f32),
            dma((8,)),
            dma,
            dma((5,)),
        ],
        compiler_params=pltpu.CompilerParams(
            collective_id=0, has_side_effects=True, vmem_limit_bytes=32 << 20
        ),
    )(
        *(
            pltpu.with_memory_space_constraint(array, pltpu.HBM)
            for array in (
                frames.transpose(0, 2, 1),
                frame_owner,
                picks,
                patch_weight,
                patch_bias[None],
                norm_gain[None],
                head_weight,
                head_bias[None],
                head_out[None],
                hidden_state,
                group_gain[None],
                group_shift[None],
                out_weight,
                inner_weight,
            )
        )
    )
    out_shape = (own, frame_count // 2, 2, wide, channels)
    return pl.pallas_call(
        functools.partial(last_kernel, n),
        out_shape=jax.ShapeDtypeStruct(out_shape, bf16),
        in_specs=[vmem] * 5,
        out_specs=pl.BlockSpec(memory_space=pltpu.HBM),
        scratch_shapes=[
            pltpu.VMEM((-(-((own + 2) * frame_count * (wide + 1) + 1) // 8) * 8, channels), f32),
            pltpu.VMEM((own + 2, frame_count // 2 + 1, 2, wide, 3 * channels), bf16),
            pltpu.VMEM((2, own + 2, frame_count // 2, wide // 2, 4 * channels), bf16),
            pltpu.VMEM((2, own * frame_count * wide // 2, channels), f32),
            pltpu.VMEM(out_shape, bf16),
            dma,
        ],
        compiler_params=pltpu.CompilerParams(vmem_limit_bytes=32 << 20),
    )(*kept).reshape(hidden_state.shape)


def solution(mesh):
    body = one_frame_each if mesh.shape["row"] == FRAMES else per_device
    return jax.shard_map(
        body,
        mesh=mesh,
        in_specs=(
            P(None, None, ("clip", "row")),
            P("clip"),
            P("clip"),
            P(),
            P(),
            P(),
            P(),
            P(),
            P(),
            P(("clip", "row"), None, None, None),
            P(),
            P(),
            P(),
            P(),
        ),
        out_specs=P(("clip", "row"), None, None, None),
        check_vma=False,
    )
```

```python
import functools

import jax
import jax.numpy as jnp
from jax import lax
from jax.experimental import pallas as pl
from jax.experimental.pallas import tpu as pltpu
from jax.sharding import PartitionSpec as P

PATCH = 16
GROUPS = 32
FRAMES = 16


eps_norm = 1e-06
MESH = pl.DeviceIdType.MESH


def extended(block, sides, width):
    for axis, dim in sides:
        count = lax.axis_size(axis)
        forward = [(i, i + 1) for i in range(count - 1)]
        backward = [(target, source) for source, target in forward]
        low = lax.ppermute(
            lax.slice_in_dim(block, block.shape[dim] - width, None, axis=dim), axis, forward
        )
        high = lax.ppermute(lax.slice_in_dim(block, 0, width, axis=dim), axis, backward)
        block = jnp.concatenate([low, block, high], axis=dim)
    return block


def silu_slope(values):
    sigmoid = jax.nn.sigmoid(values)
    return sigmoid * (1.0 + values * (1.0 - sigmoid))


def to_tokens(pixels):
    channels, height, columns = pixels.shape
    shaped = pixels.reshape(channels, height // PATCH, PATCH, columns // PATCH, PATCH)
    return shaped.transpose(1, 3, 0, 2, 4).reshape(
        height // PATCH * (columns // PATCH), channels * PATCH * PATCH
    )


def from_tokens(token_grads, height, columns):
    shaped = token_grads.reshape(height // PATCH, columns // PATCH, 3, PATCH, PATCH)
    return shaped.transpose(2, 0, 3, 1, 4).reshape(3, height, columns)


def pixel_back(padded, out_weight, amount):
    frame_count = padded.shape[2]
    columns = padded.shape[3]
    widened = jnp.pad(padded, ((0, 0), (0, 0), (0, 2), (1, 1)))
    windows = []
    for time_tap in range(3):
        for row_tap in range(3):
            for col_tap in range(3):
                windows.append(
                    widened[
                        :,
                        2 - row_tap : 2 - row_tap + amount,
                        2 - time_tap : 2 - time_tap + frame_count,
                        2 - col_tap : 2 - col_tap + columns,
                    ]
                )
    stacked = jnp.stack(windows, 0).reshape(27 * 3, amount * frame_count * columns)
    kernel = out_weight.reshape(27 * 3, out_weight.shape[4])
    summed = lax.dot_general(
        stacked, kernel, (((0,), (0,)), ((), ())), preferred_element_type=jnp.float32
    )
    return summed.reshape(amount, frame_count, columns, out_weight.shape[4])


def inner_back(padded, inner_weight, amount):
    frame_count = padded.shape[1]
    columns = padded.shape[2]
    channel_count = padded.shape[3]
    widened = jnp.pad(padded, ((0, 0), (0, 2), (1, 1), (0, 0)))
    summed = jnp.zeros((amount * frame_count * columns, inner_weight.shape[3]), jnp.float32)
    for time_tap in range(3):
        windows = []
        for row_tap in range(3):
            for col_tap in range(3):
                windows.append(
                    widened[
                        2 - row_tap : 2 - row_tap + amount,
                        2 - time_tap : 2 - time_tap + frame_count,
                        2 - col_tap : 2 - col_tap + columns,
                        :,
                    ]
                )
        joined = jnp.concatenate(windows, axis=3).reshape(
            amount * frame_count * columns, 9 * channel_count
        )
        kernel = jnp.transpose(inner_weight[time_tap], (0, 1, 3, 2)).reshape(
            9 * channel_count, inner_weight.shape[3]
        )
        summed = summed + jnp.dot(joined, kernel, preferred_element_type=jnp.float32)
    return summed.reshape(amount, frame_count, columns, inner_weight.shape[3])


def group_back(state_rows, slope_in, group_mean, inverse, group_gain, group_shift, cell_total):
    grouped = state_rows.astype(jnp.float32).reshape(state_rows.shape[:3] + (GROUPS, -1))
    gain_table = group_gain.reshape(GROUPS, -1)
    shift_table = group_shift.reshape(GROUPS, -1)
    normed_state = (grouped - group_mean[:, None]) * inverse[:, None]
    affine = normed_state * gain_table + shift_table
    upstream = slope_in.reshape(grouped.shape) * silu_slope(affine) * gain_table
    group_terms = lax.psum(
        (jnp.sum(upstream, axis=(0, 1, 2, 4)), jnp.sum(upstream * normed_state, axis=(0, 1, 2, 4))),
        "row",
    )
    first_part = group_terms[0] / cell_total
    second_part = group_terms[1] / cell_total
    state_grad = (upstream - first_part[:, None] - normed_state * second_part[:, None]) * inverse[
        :, None
    ]
    return state_grad.reshape(state_rows.shape).astype(jnp.bfloat16)


def per_device(
    frames,
    frame_owner,
    picks,
    patch_weight,
    patch_bias,
    norm_gain,
    head_weight,
    head_bias,
    head_out,
    hidden_state,
    group_gain,
    group_shift,
    out_weight,
    inner_weight,
):
    devices = lax.axis_size("row")
    position = lax.axis_index("row")
    per_frame = devices // FRAMES
    slot = position // per_frame
    height = frames.shape[1]
    strip = frames.shape[2]
    own_rows = hidden_state.shape[0]
    frame_width = hidden_state.shape[2]
    tokens = to_tokens(frames)
    embedded = jnp.dot(tokens, patch_weight, preferred_element_type=jnp.float32) + patch_bias
    centred = embedded - jnp.mean(embedded, axis=1, keepdims=True)
    inv_spread = lax.rsqrt(jnp.mean(centred * centred, axis=1, keepdims=True) + eps_norm)
    normed = centred * inv_spread
    slot_mask = (jnp.arange(FRAMES, dtype=jnp.int32) == slot).astype(jnp.float32)
    partial_pool = slot_mask[:, None] * jnp.sum(normed * norm_gain, axis=0)[None, :]
    grouped = hidden_state.reshape(own_rows, FRAMES, frame_width, GROUPS, -1)
    first_sum = jnp.sum(grouped, axis=(0, 1, 2, 4), dtype=jnp.float32)
    second_sum = jnp.sum(jnp.square(grouped.astype(jnp.float32)), axis=(0, 1, 2, 4))
    pooled_sum, first_total, second_total = lax.psum((partial_pool, first_sum, second_sum), "row")
    frame_tokens = height // PATCH * (strip * per_frame // PATCH)
    pooled = pooled_sum / frame_tokens
    head_full = head_weight.astype(jnp.float32)
    before = jnp.dot(pooled, head_full, precision=lax.Precision.HIGHEST) + head_bias
    pulled = jnp.dot(head_out * silu_slope(before), head_full.T, precision=lax.Precision.HIGHEST)
    picked = jnp.sum((picks[:, None] == frame_owner[None, :]).astype(jnp.float32), axis=0)
    slot_grad = jnp.dot(slot_mask * picked, pulled, precision=lax.Precision.HIGHEST)
    scaled = norm_gain * slot_grad
    token_grad = inv_spread * (
        scaled - jnp.mean(scaled) - normed * jnp.mean(scaled * normed, axis=1, keepdims=True)
    )
    patch_grad = lax.dot_general(
        token_grad.astype(jnp.bfloat16),
        patch_weight,
        (((1,), (1,)), ((), ())),
        preferred_element_type=jnp.float32,
    )
    pixel_local = from_tokens(patch_grad, height, strip).astype(jnp.bfloat16)
    arrived = lax.all_to_all(pixel_local, "row", split_axis=1, concat_axis=2, tiled=True)
    by_slot = arrived.reshape(3, own_rows, FRAMES, frame_width)
    owner_table = (frame_owner[:, None] == jnp.arange(FRAMES, dtype=jnp.int32)[None, :]).astype(
        jnp.bfloat16
    )
    ordered = jnp.einsum(
        "krbw,bf->krfw", by_slot, owner_table, preferred_element_type=jnp.float32
    ).astype(jnp.bfloat16)
    cell_total = own_rows * devices * FRAMES * frame_width * (hidden_state.shape[3] // GROUPS)
    group_mean = first_total / cell_total
    inverse = lax.rsqrt(second_total / cell_total - group_mean * group_mean + eps_norm)
    pixel_padded = extended(ordered, (("row", 1),), 1)
    slope_in = pixel_back(pixel_padded, out_weight, own_rows)
    state_grad = group_back(
        hidden_state, slope_in, group_mean, inverse, group_gain, group_shift, cell_total
    )
    grad_padded = extended(state_grad, (("row", 0),), 1)
    return inner_back(grad_padded, inner_weight, own_rows).astype(jnp.bfloat16)


def split_rows(row):
    high = row.astype(jnp.bfloat16).astype(jnp.float32)
    rest = row - high
    middle = rest.astype(jnp.bfloat16).astype(jnp.float32)
    low = rest - middle
    index = lax.broadcasted_iota(jnp.int32, (8, row.shape[1]), 0)
    stacked = jnp.where(
        index == 0, high, jnp.where(index == 1, middle, jnp.where(index == 2, low, 0.0))
    )
    return stacked.astype(jnp.bfloat16)


def fused_kernel(
    n,
    frames_any,
    owner_any,
    picks_any,
    patch_any,
    patch_bias_any,
    norm_gain_any,
    head_any,
    head_bias_any,
    head_out_any,
    hidden_any,
    group_gain_any,
    group_shift_any,
    out_weight_any,
    inner_any,
    ready,
    normed_ref,
    terms,
    turned,
    paired,
    frames,
    owner,
    picks,
    wide_rows,
    group_rows,
    out_weight,
    patch_w,
    head_w,
    hidden,
    inner_w,
    pixels,
    tokens,
    sent,
    arrived,
    by_frame,
    columns,
    taps,
    band,
    slope,
    cells,
    sums_one,
    sums_two,
    local_sem,
    send_sem,
    recv_sem,
):
    me = lax.axis_index("row")
    strip, height = frames.shape[1], frames.shape[2]
    patch_rows = height // PATCH
    own = hidden.shape[0] - 2
    wide = hidden.shape[2]
    channels = hidden.shape[3]
    line = FRAMES * wide
    pitch = wide + 1
    per_group = channels // GROUPS
    cell_total = own * n * FRAMES * wide * per_group
    window = wide // 2 + 1
    piece = 3 * window
    slot_lanes = 64
    half = arrived.shape[1]

    def peer(offset):
        target = me
        step = 1
        while step < n:
            if offset // step % 2:
                target = target + step * (1 - 2 * lax.rem(lax.div(me, step), 2))
            step *= 2
        return target

    farthest_first = range(n - 1, 0, -1)

    barrier = pltpu.get_barrier_semaphore()
    for offset in farthest_first:
        pl.semaphore_signal(barrier, inc=1, device_id={"row": peer(offset)}, device_id_type=MESH)

    load_frames = pltpu.make_async_copy(frames_any, frames, local_sem.at[0])
    load_hidden = pltpu.make_async_copy(hidden_any, hidden.at[pl.ds(1, own)], local_sem.at[1])
    pix, width = patch_w.shape
    third, part_rows = pix // 3, width // 2
    pieces = ((0, 2 * third), (2 * third, pix))
    load_patch = [
        pltpu.make_async_copy(
            patch_any.at[pl.ds(low, high - low)],
            patch_w.at[pl.ds(low, high - low)],
            local_sem.at[2 + part],
        )
        for part, (low, high) in enumerate(pieces)
    ]
    load_head = [
        pltpu.make_async_copy(
            head_any.at[pl.ds(part * part_rows, part_rows)],
            head_w.at[pl.ds(part * part_rows, part_rows)],
            local_sem.at[4 + part],
        )
        for part in range(2)
    ]
    load_inner = pltpu.make_async_copy(inner_any, inner_w, local_sem.at[6])
    load_out = pltpu.make_async_copy(out_weight_any, out_weight, local_sem.at[6])
    load_owner = pltpu.make_async_copy(owner_any, owner, local_sem.at[6])
    load_picks = pltpu.make_async_copy(picks_any, picks, local_sem.at[6])
    load_wide = [
        pltpu.make_async_copy(source, wide_rows.at[index], local_sem.at[1])
        for index, source in enumerate((patch_bias_any, norm_gain_any, head_bias_any, head_out_any))
    ]
    load_group = [
        pltpu.make_async_copy(source, group_rows.at[index], local_sem.at[6])
        for index, source in enumerate((group_gain_any, group_shift_any))
    ]
    load_frames.start()
    load_hidden.start()
    for load in load_wide:
        load.start()
    for load in load_patch + load_head:
        load.start()
    load_owner.start()
    load_picks.start()
    for load in load_group:
        load.start()
    load_out.start()
    load_inner.start()

    group_row = lax.broadcasted_iota(jnp.int32, (channels, channels), 0) // per_group
    group_col = lax.broadcasted_iota(jnp.int32, (channels, channels), 1) // per_group
    same_group = (group_row == group_col).astype(jnp.bfloat16)
    eight = lax.broadcasted_iota(jnp.int32, (8, channels), 0)
    spot = lax.broadcasted_iota(jnp.int32, (2, channels), 0)

    def group_sums(first, second):
        part = lax.rem(eight, 4)
        row = jnp.where(eight < 4, first, second)
        high = row.astype(jnp.bfloat16).astype(jnp.float32)
        rest = row - high
        middle = rest.astype(jnp.bfloat16).astype(jnp.float32)
        stacked = jnp.where(
            part == 0, high, jnp.where(part == 1, middle, jnp.where(part == 2, rest - middle, 0.0))
        )
        summed = jnp.dot(
            stacked.astype(jnp.bfloat16), same_group, preferred_element_type=jnp.float32
        )
        return (
            jnp.sum(summed[0:4], axis=0, keepdims=True),
            jnp.sum(summed[4:8], axis=0, keepdims=True),
        )

    def tree_sum(blocks):
        while len(blocks) > 1:
            blocks = [
                blocks[at] + blocks[at + 1] if at + 1 < len(blocks) else blocks[at]
                for at in range(0, len(blocks), 2)
            ]
        return blocks[0]

    def over_devices(buffer):
        return tree_sum([buffer[slot] for slot in range(n)])

    load_frames.wait()
    for colour in range(3):
        pixels[colour] = frames[colour].astype(jnp.float32).T
    tokens[...] = jnp.zeros_like(tokens)
    for colour in range(3):
        for line_in in range(PATCH):
            at = (colour * PATCH + line_in) * PATCH
            tokens[0:patch_rows, at : at + PATCH] = pixels[
                colour, pl.ds(line_in, patch_rows, stride=PATCH), :
            ]
    sent[...] = jnp.zeros_like(sent)

    load_hidden.wait()
    pltpu.make_async_copy(wide_rows, wide_rows, local_sem.at[1]).wait()
    first = jnp.zeros((1, channels), jnp.float32)
    second = jnp.zeros((1, channels), jnp.float32)
    for row in range(own):
        state = hidden[1 + row].reshape(line, channels).astype(jnp.float32)
        first = first + jnp.sum(state, axis=0, keepdims=True)
        second = second + jnp.sum(state * state, axis=0, keepdims=True)
    first, second = group_sums(first, second)
    sums_one[me] = jnp.where(spot == 0, first, second)

    embedded = wide_rows[0]
    for part, (low, high) in enumerate(pieces):
        load_patch[part].wait()
        embedded = embedded + jnp.dot(
            tokens[:, low:high].astype(jnp.bfloat16),
            patch_w[low:high],
            preferred_element_type=jnp.float32,
        )
    centred = embedded - jnp.mean(embedded, axis=1, keepdims=True)
    inv_spread = lax.rsqrt(jnp.mean(centred * centred, axis=1, keepdims=True) + eps_norm)
    normed = centred * inv_spread
    gain = wide_rows[1]
    pooled = jnp.sum((normed * gain)[0:patch_rows], axis=0, keepdims=True) / patch_rows
    split_pool = split_rows(pooled)
    before = wide_rows[2]
    for part in range(2):
        load_head[part].wait()
        before = before + jnp.sum(
            jnp.dot(
                split_pool[:, part * part_rows : (part + 1) * part_rows],
                head_w[part * part_rows : (part + 1) * part_rows],
                preferred_element_type=jnp.float32,
            ),
            axis=0,
            keepdims=True,
        )
    pulled = jnp.sum(
        lax.dot_general(
            split_rows(wide_rows[3] * silu_slope(before)),
            head_w[...],
            (((1,), (1,)), ((), ())),
            preferred_element_type=jnp.float32,
        ),
        axis=0,
        keepdims=True,
    )
    load_owner.wait()
    load_picks.wait()
    pltpu.make_async_copy(group_rows, group_rows, local_sem.at[6]).wait()
    load_out.wait()
    load_inner.wait()
    mine = owner[me]
    picked = jnp.float32(0.0)
    for pick in range(picks.shape[0]):
        picked = picked + jnp.where(picks[pick] == mine, jnp.float32(1.0), jnp.float32(0.0))
    scaled = gain * (picked * pulled)
    token_grad = inv_spread * (
        scaled
        - jnp.mean(scaled, axis=1, keepdims=True)
        - normed * jnp.mean(scaled * normed, axis=1, keepdims=True)
    )
    token_grad = token_grad.astype(jnp.bfloat16)
    sixth = pix // 6
    cuts = (0, 3, 6)
    patch_grad = jnp.concatenate(
        [
            lax.dot_general(
                token_grad,
                patch_w[low * sixth : high * sixth],
                (((1,), (1,)), ((), ())),
                preferred_element_type=jnp.float32,
            )
            for low, high in zip(cuts[:-1], cuts[1:])
        ],
        axis=1,
    )
    patch_grad = patch_grad.astype(jnp.bfloat16).astype(jnp.float32)
    for line_in in range(PATCH):
        lines = [
            patch_grad[:, (colour * PATCH + line_in) * PATCH : (colour * PATCH + line_in + 1) * PATCH]
            for colour in range(3)
        ]
        joined = jnp.concatenate(
            [line_of[:, 0:window] for line_of in lines]
            + [jnp.zeros((lines[0].shape[0], slot_lanes - 2 * piece), jnp.float32)]
            + [line_of[:, wide - window : wide] for line_of in lines],
            axis=1,
        )
        for patch_row in range(patch_rows):
            at = 2 + patch_row * PATCH + line_in
            sent[at, :, 0:slot_lanes] = joined[patch_row : patch_row + 1]
            if at >= half:
                sent[at - half, :, slot_lanes : 2 * slot_lanes] = joined[patch_row : patch_row + 1]

    pl.semaphore_wait(barrier, n - 1)

    def send_sums(buffer, kind, offset):
        pltpu.make_async_remote_copy(
            src_ref=buffer.at[me],
            dst_ref=buffer.at[me],
            send_sem=send_sem,
            recv_sem=recv_sem.at[kind],
            device_id={"row": peer(offset)},
            device_id_type=MESH,
        ).start()

    def from_peers(buffer, kind):
        others = buffer.at[pl.ds(0, n - 1)]
        pltpu.make_async_copy(others, others, recv_sem.at[kind]).wait()

    def to_peers(buffer):
        others = buffer.at[pl.ds(0, n - 1)]
        pltpu.make_async_copy(others, others, send_sem).wait()

    for offset in farthest_first:
        target = peer(offset)
        pltpu.make_async_remote_copy(
            src_ref=sent.at[pl.ds(target * own, half)],
            dst_ref=arrived.at[me],
            send_sem=send_sem,
            recv_sem=recv_sem.at[1],
            device_id={"row": target},
            device_id_type=MESH,
        ).start()
        send_sums(sums_one, 0, offset)
    to_right = pltpu.make_async_remote_copy(
        src_ref=hidden_any.at[pl.ds(own - 1, 1)],
        dst_ref=hidden.at[pl.ds(0, 1)],
        send_sem=send_sem,
        recv_sem=recv_sem.at[3],
        device_id={"row": lax.rem(me + 1, n)},
        device_id_type=MESH,
    )
    to_left = pltpu.make_async_remote_copy(
        src_ref=hidden_any.at[pl.ds(0, 1)],
        dst_ref=hidden.at[pl.ds(own + 1, 1)],
        send_sem=send_sem,
        recv_sem=recv_sem.at[4],
        device_id={"row": lax.rem(me + n - 1, n)},
        device_id_type=MESH,
    )

    @pl.when(me < n - 1)
    def _():
        to_right.start()

    @pl.when(me > 0)
    def _():
        to_left.start()

    @pl.when(me == 0)
    def _():
        hidden[0] = jnp.zeros(hidden.shape[1:], hidden.dtype)

    @pl.when(me == n - 1)
    def _():
        hidden[own + 1] = jnp.zeros(hidden.shape[1:], hidden.dtype)

    arrived[me] = sent[pl.ds(me * own, half)]

    taps[...] = jnp.zeros_like(taps)
    for time_tap in range(3):
        for row_tap in range(3):
            for col_tap in range(3):
                at = ((time_tap * 3 + row_tap) * 3 + col_tap) * 3
                taps[at : at + 3] = out_weight[time_tap, row_tap, col_tap].astype(jnp.float32)
    flat_taps = taps[...].astype(jnp.bfloat16)
    depth = band.shape[0]
    entry = lax.broadcasted_iota(jnp.int32, (depth, channels), 0)
    tap_lane = lax.broadcasted_iota(jnp.int32, (depth, channels), 1)
    tap_of = entry // piece
    column = lax.rem(entry, window)
    first_lane = (
        (lax.rem(tap_of, 3) * 3 + tap_of // 3) * 9 + lax.rem(entry, piece) // window - 3 * column
    )
    for output in range(window):
        col_tap = output + 1 - column
        chosen = (
            (tap_lane == first_lane + 3 * (output + 1))
            & (col_tap >= 0)
            & (col_tap < 3)
            & (entry < 9 * piece)
        )
        band[:, output * channels : (output + 1) * channels] = jnp.dot(
            chosen.astype(jnp.float32).astype(jnp.bfloat16),
            flat_taps,
            preferred_element_type=jnp.float32,
        ).astype(jnp.bfloat16)
    columns[...] = jnp.zeros_like(columns)
    by_frame[...] = jnp.zeros_like(by_frame)

    slot_of = []
    for frame in range(FRAMES):
        found = jnp.int32(0)
        for slot in range(n):
            found = jnp.where(owner[slot] == frame, jnp.int32(slot), found)
        slot_of.append(found)


    def spread_cells(row):
        for frame in range(FRAMES):
            at = (row * FRAMES + frame) * pitch
            cells[at : at + wide] = hidden[row, frame].astype(jnp.float32)

    for row in range(1, own + 1):
        spread_cells(row)

    empty = jnp.zeros((channels, channels), jnp.bfloat16)
    for row_tap in range(3):
        above = 2 - row_tap
        for col_tap in range(3):
            part = pl.ds(col_tap * channels, channels)
            blocks = [inner_w[time_tap, row_tap, col_tap].T for time_tap in range(3)]
            for ahead in range(2):
                turned[above, ahead, part, 0:channels] = blocks[1 - ahead]
                turned[above, ahead, part, channels:] = blocks[2 - ahead]
            for side in range(2):
                at = (2 - col_tap + side) * channels
                for kind in range(2):
                    paired[kind, above, at : at + channels, side * channels : (side + 1) * channels] = (
                        blocks[2 - 2 * kind]
                    )
        for kind in range(2):
            paired[kind, above, 3 * channels :, 0:channels] = empty
            paired[kind, above, 0:channels, channels:] = empty

    from_peers(sums_one, 0)
    from_peers(arrived, 1)
    means = over_devices(sums_one) / cell_total
    group_mean = means[0:1]
    inverse = lax.rsqrt(means[1:2] - group_mean * group_mean + eps_norm)
    group_gain = group_rows[0]
    group_shift = group_rows[1]
    def pixel_taps(row, block):
        for row_tap in range(3):
            for time_tap in range(3):
                at = (row_tap * 3 + time_tap) * piece
                source = row - row_tap + 2
                for side in range(2):
                    lane = source // half * slot_lanes + side * (slot_lanes - piece)
                    columns[block[side] : block[side] + FRAMES, at : at + piece] = by_frame[
                        source % half, 2 - time_tap : 2 - time_tap + FRAMES, lane : lane + piece
                    ]

    spread = inverse * group_gain

    def state_terms(part):
        centred = cells[part] - group_mean
        return centred, silu_slope(centred * spread + group_shift)

    own_cells = own * FRAMES
    for frame in range(FRAMES):
        for row in range(half):
            by_frame[row, frame : frame + 1, :] = arrived[slot_of[frame], row]
    for row in range(1, own + 1):
        pixel_taps(row, ((row - 1) * FRAMES, own_cells + (row - 1) * FRAMES))
    left = columns[0 : 2 * own_cells].astype(jnp.bfloat16)
    first = jnp.zeros((8, channels), jnp.float32)
    second = jnp.zeros((8, channels), jnp.float32)
    for output in range(0, window, 2):
        lanes = pl.ds(output * channels, min(2, window - output) * channels)
        several = jnp.dot(left, band[:, lanes], preferred_element_type=jnp.float32)
        for index in range(several.shape[1] // channels):
            for side in range(2):
                w = output + index + side * (wide - window)
                if side == 0 and output + index == window - 1 or side == 1 and output + index == 0:
                    continue
                centred, slope_factor = state_terms(
                    pl.ds(FRAMES * pitch + w, own_cells, stride=pitch)
                )
                upstream = (
                    several[
                        side * own_cells : (side + 1) * own_cells,
                        index * channels : (index + 1) * channels,
                    ]
                    * slope_factor
                )
                first = first + jnp.sum(upstream.reshape(-1, 8, channels), axis=0)
                second = second + jnp.sum(
                    (upstream * centred).reshape(-1, 8, channels), axis=0
                )
    first = jnp.sum(first, axis=0, keepdims=True) * group_gain
    second = jnp.sum(second, axis=0, keepdims=True) * spread
    sums_two[me] = jnp.where(spot == 0, first, second)
    for offset in farthest_first:
        send_sums(sums_two, 2, offset)


    @pl.when(me < n - 1)
    def _():
        to_left.wait_recv()

    @pl.when(me > 0)
    def _():
        to_right.wait_recv()

    for index, row in enumerate((0, own + 1)):
        pixel_taps(row, (2 * own_cells + index * FRAMES, 2 * own_cells + (2 + index) * FRAMES))
        spread_cells(row)
    left = columns[...].astype(jnp.bfloat16)
    for output in range(window):
        several = jnp.dot(
            left,
            band[:, output * channels : (output + 1) * channels],
            preferred_element_type=jnp.float32,
        )
        for side in range(2):
            if side == 0 and output == window - 1 or side == 1 and output == 0:
                continue
            w = output + side * (wide - window)
            part = pl.ds(FRAMES * pitch + w, own_cells, stride=pitch)
            slope[part] = (
                several[side * own_cells : (side + 1) * own_cells] * state_terms(part)[1]
            )
            for index, row in enumerate((0, own + 1)):
                part = pl.ds(row * FRAMES * pitch + w, FRAMES, stride=pitch)
                at = 2 * own_cells + (2 * side + index) * FRAMES
                slope[part] = several[at : at + FRAMES] * state_terms(part)[1]
    terms[2:3] = inverse / cell_total
    for cell in range((own + 2) * FRAMES):
        part = pl.ds(cell * wide, wide)
        ready[part] = slope[cell * pitch : cell * pitch + wide] * spread
        state = hidden[cell // FRAMES, cell % FRAMES].astype(jnp.float32)
        normed_ref[part] = (state - group_mean) * inverse

    to_peers(sums_one)
    to_peers(arrived)
    to_peers(sums_two)

    @pl.when(me < n - 1)
    def _():
        to_right.wait_send()

    @pl.when(me > 0)
    def _():
        to_left.wait_send()

    from_peers(sums_two, 2)
    terms[0:2] = over_devices(sums_two)


def last_kernel(
    n, ready, normed_ref, terms, turned, paired, out_any, padded, windows, pairs, rest, out, out_sem
):
    me = lax.axis_index("row")
    own = out.shape[0]
    wide = out.shape[3]
    channels = out.shape[4]
    line = FRAMES * wide
    windows[:, FRAMES // 2, 0] = jnp.zeros((own + 2, wide, 3 * channels), jnp.bfloat16)
    pairs[1, :, FRAMES // 2 - 1] = jnp.zeros((own + 2, wide // 2, 4 * channels), jnp.bfloat16)
    pitch = wide + 1
    blank = jnp.zeros((1, channels), jnp.float32)
    for cell in range((own + 2) * FRAMES + 1):
        padded[cell * pitch : cell * pitch + 1] = blank
    total = terms[0:2]
    lane = lax.broadcasted_iota(jnp.int32, total.shape, 1)
    step = 1
    while step < channels // GROUPS:
        total = total + jnp.where(
            lax.rem(lane // step, 2) == 0,
            pltpu.roll(total, channels - step, 1),
            pltpu.roll(total, step, 1),
        )
        step *= 2
    total = total * terms[2:3]
    first_part = jnp.broadcast_to(total[0:1], (wide, channels))
    second_part = jnp.broadcast_to(total[1:2], (wide, channels))
    for row in range(own + 2):
        for frame in range(FRAMES):
            cell = row * FRAMES + frame
            part = pl.ds(cell * wide, wide)
            state_grad = ready[part] - first_part - normed_ref[part] * second_part
            if row == 0:
                state_grad = jnp.where(me > 0, state_grad, 0.0)
            if row == own + 1:
                state_grad = jnp.where(me < n - 1, state_grad, 0.0)
            at = cell * pitch + 1
            padded[at : at + wide] = state_grad
            for col_tap in range(3 if frame > 0 else 0):
                windows[
                    row, frame // 2, frame % 2, :, col_tap * channels : (col_tap + 1) * channels
                ] = padded[at + 1 - col_tap : at + 1 - col_tap + wide].astype(jnp.bfloat16)
            kind, step = frame % 2, frame // 2 - frame % 2
            if step >= 0:
                for index in range(4):
                    pairs[kind, row, step, :, index * channels : (index + 1) * channels] = padded[
                        pl.ds(cell * pitch + index, wide // 2, stride=2)
                    ].astype(jnp.bfloat16)
    half_line = line // 2
    for kind in range(2):
        left = jnp.concatenate(
            [
                pairs[kind, above : above + own].reshape(own * half_line // 2, 4 * channels)
                for above in range(3)
            ],
            axis=1,
        )
        both = jnp.dot(
            left,
            paired[kind].reshape(12 * channels, 2 * channels),
            preferred_element_type=jnp.float32,
        )
        for side in range(2):
            rest[kind, pl.ds(side, own * half_line // 2, stride=2)] = both[
                :, side * channels : (side + 1) * channels
            ]
    taken = jnp.concatenate(
        [
            windows[
                above : above + own, ahead // 2 : ahead // 2 + FRAMES // 2, ahead % 2
            ].reshape(own * half_line, 3 * channels)
            for above in range(3)
            for ahead in (1, 2)
        ],
        axis=1,
    )
    summed = jnp.dot(
        taken,
        turned[...].reshape(6 * 3 * channels, 2 * channels),
        preferred_element_type=jnp.float32,
    )
    for row in range(own):
        for side in range(2):
            out[row, :, side] = (
                (
                    summed[
                        row * half_line : (row + 1) * half_line,
                        side * channels : (side + 1) * channels,
                    ]
                    + rest[side, row * half_line : (row + 1) * half_line]
                )
                .reshape(FRAMES // 2, wide, channels)
                .astype(jnp.bfloat16)
            )
        pltpu.make_async_copy(out.at[row], out_any.at[row], out_sem).start()
    pltpu.make_async_copy(out, out_any, out_sem).wait()


def one_frame_each(
    frames,
    frame_owner,
    picks,
    patch_weight,
    patch_bias,
    norm_gain,
    head_weight,
    head_bias,
    head_out,
    hidden_state,
    group_gain,
    group_shift,
    out_weight,
    inner_weight,
):
    n = lax.axis_size("row")
    own, frame_count, wide, channels = hidden_state.shape
    height, strip = frames.shape[1:]
    pix, width = patch_weight.shape
    window = wide // 2 + 1
    depth = -(-27 * window // 128) * 128
    cells = (own + 2) * frame_count * wide
    f32, bf16 = jnp.float32, jnp.bfloat16
    vmem = pl.BlockSpec(memory_space=pltpu.VMEM)
    dma = pltpu.SemaphoreType.DMA
    passed = [
        pltpu.VMEM((cells, channels), f32),
        pltpu.VMEM((cells, channels), f32),
        pltpu.VMEM((8, channels), f32),
        pltpu.VMEM((3, 2, 3 * channels, 2 * channels), bf16),
        pltpu.VMEM((2, 3, 4 * channels, 2 * channels), bf16),
    ]
    kept = pl.pallas_call(
        functools.partial(fused_kernel, n),
        out_shape=passed,
        in_specs=[pl.BlockSpec(memory_space=pltpu.HBM)] * 14,
        out_specs=[vmem] * 5,
        scratch_shapes=[
            pltpu.VMEM((3, strip, height), bf16),
            pltpu.SMEM(frame_owner.shape, jnp.int32),
            pltpu.SMEM(picks.shape, jnp.int32),
            pltpu.VMEM((4, 1, width), f32),
            pltpu.VMEM((2, 1, channels), f32),
            pltpu.VMEM(out_weight.shape, bf16),
            pltpu.VMEM((pix, width), bf16),
            pltpu.VMEM(head_weight.shape, bf16),
            pltpu.VMEM((own + 2, frame_count, wide, channels), bf16),
            pltpu.VMEM(inner_weight.shape, bf16),
            pltpu.VMEM(frames.shape, f32),
            pltpu.VMEM((-(-(height // PATCH) // 8) * 8, pix), f32),
            pltpu.VMEM((height + 4, 1, 128), f32),
            pltpu.VMEM((n, (own + 5) // 2, 1, 128), f32),
            pltpu.VMEM(((own + 5) // 2, frame_count + 8, 128), f32),
            pltpu.VMEM((2 * (own + 2) * frame_count, depth), f32),
            pltpu.VMEM((128, channels), f32),
            pltpu.VMEM((depth, window * channels), bf16),
            pltpu.VMEM(((own + 2) * frame_count * (wide + 1), channels), f32),
            pltpu.VMEM(((own + 2) * frame_count * (wide + 1), channels), f32),
            pltpu.VMEM((n, 2, channels), f32),
            pltpu.VMEM((n, 2, channels), f32),
            dma((7,)),
            dma,
            dma((5,)),
        ],
        compiler_params=pltpu.CompilerParams(
            collective_id=0, has_side_effects=True, vmem_limit_bytes=32 << 20
        ),
    )(
        *(
            pltpu.with_memory_space_constraint(array, pltpu.HBM)
            for array in (
                frames.transpose(0, 2, 1),
                frame_owner,
                picks,
                patch_weight,
                patch_bias[None],
                norm_gain[None],
                head_weight,
                head_bias[None],
                head_out[None],
                hidden_state,
                group_gain[None],
                group_shift[None],
                out_weight,
                inner_weight,
            )
        )
    )
    out_shape = (own, frame_count // 2, 2, wide, channels)
    return pl.pallas_call(
        functools.partial(last_kernel, n),
        out_shape=jax.ShapeDtypeStruct(out_shape, bf16),
        in_specs=[vmem] * 5,
        out_specs=pl.BlockSpec(memory_space=pltpu.HBM),
        scratch_shapes=[
            pltpu.VMEM((-(-((own + 2) * frame_count * (wide + 1) + 1) // 8) * 8, channels), f32),
            pltpu.VMEM((own + 2, frame_count // 2 + 1, 2, wide, 3 * channels), bf16),
            pltpu.VMEM((2, own + 2, frame_count // 2, wide // 2, 4 * channels), bf16),
            pltpu.VMEM((2, own * frame_count * wide // 2, channels), f32),
            pltpu.VMEM(out_shape, bf16),
            dma,
        ],
        compiler_params=pltpu.CompilerParams(vmem_limit_bytes=32 << 20),
    )(*kept).reshape(hidden_state.shape)


def solution(mesh):
    body = one_frame_each if mesh.shape["row"] == FRAMES else per_device
    return jax.shard_map(
        body,
        mesh=mesh,
        in_specs=(
            P(None, None, ("clip", "row")),
            P("clip"),
            P("clip"),
            P(),
            P(),
            P(),
            P(),
            P(),
            P(),
            P(("clip", "row"), None, None, None),
            P(),
            P(),
            P(),
            P(),
        ),
        out_specs=P(("clip", "row"), None, None, None),
        check_vma=False,
    )
```

```python
import functools

import jax
import jax.numpy as jnp
from jax import lax
from jax.experimental import pallas as pl
from jax.experimental.pallas import tpu as pltpu
from jax.sharding import PartitionSpec as P

PATCH = 16
GROUPS = 32
FRAMES = 16


eps_norm = 1e-06
MESH = pl.DeviceIdType.MESH


def extended(block, sides, width):
    for axis, dim in sides:
        count = lax.axis_size(axis)
        forward = [(i, i + 1) for i in range(count - 1)]
        backward = [(target, source) for source, target in forward]
        low = lax.ppermute(
            lax.slice_in_dim(block, block.shape[dim] - width, None, axis=dim), axis, forward
        )
        high = lax.ppermute(lax.slice_in_dim(block, 0, width, axis=dim), axis, backward)
        block = jnp.concatenate([low, block, high], axis=dim)
    return block


def silu_slope(values):
    sigmoid = jax.nn.sigmoid(values)
    return sigmoid * (1.0 + values * (1.0 - sigmoid))


def to_tokens(pixels):
    channels, height, columns = pixels.shape
    shaped = pixels.reshape(channels, height // PATCH, PATCH, columns // PATCH, PATCH)
    return shaped.transpose(1, 3, 0, 2, 4).reshape(
        height // PATCH * (columns // PATCH), channels * PATCH * PATCH
    )


def from_tokens(token_grads, height, columns):
    shaped = token_grads.reshape(height // PATCH, columns // PATCH, 3, PATCH, PATCH)
    return shaped.transpose(2, 0, 3, 1, 4).reshape(3, height, columns)


def pixel_back(padded, out_weight, amount):
    frame_count = padded.shape[2]
    columns = padded.shape[3]
    widened = jnp.pad(padded, ((0, 0), (0, 0), (0, 2), (1, 1)))
    windows = []
    for time_tap in range(3):
        for row_tap in range(3):
            for col_tap in range(3):
                windows.append(
                    widened[
                        :,
                        2 - row_tap : 2 - row_tap + amount,
                        2 - time_tap : 2 - time_tap + frame_count,
                        2 - col_tap : 2 - col_tap + columns,
                    ]
                )
    stacked = jnp.stack(windows, 0).reshape(27 * 3, amount * frame_count * columns)
    kernel = out_weight.reshape(27 * 3, out_weight.shape[4])
    summed = lax.dot_general(
        stacked, kernel, (((0,), (0,)), ((), ())), preferred_element_type=jnp.float32
    )
    return summed.reshape(amount, frame_count, columns, out_weight.shape[4])


def inner_back(padded, inner_weight, amount):
    frame_count = padded.shape[1]
    columns = padded.shape[2]
    channel_count = padded.shape[3]
    widened = jnp.pad(padded, ((0, 0), (0, 2), (1, 1), (0, 0)))
    summed = jnp.zeros((amount * frame_count * columns, inner_weight.shape[3]), jnp.float32)
    for time_tap in range(3):
        windows = []
        for row_tap in range(3):
            for col_tap in range(3):
                windows.append(
                    widened[
                        2 - row_tap : 2 - row_tap + amount,
                        2 - time_tap : 2 - time_tap + frame_count,
                        2 - col_tap : 2 - col_tap + columns,
                        :,
                    ]
                )
        joined = jnp.concatenate(windows, axis=3).reshape(
            amount * frame_count * columns, 9 * channel_count
        )
        kernel = jnp.transpose(inner_weight[time_tap], (0, 1, 3, 2)).reshape(
            9 * channel_count, inner_weight.shape[3]
        )
        summed = summed + jnp.dot(joined, kernel, preferred_element_type=jnp.float32)
    return summed.reshape(amount, frame_count, columns, inner_weight.shape[3])


def group_back(state_rows, slope_in, group_mean, inverse, group_gain, group_shift, cell_total):
    grouped = state_rows.astype(jnp.float32).reshape(state_rows.shape[:3] + (GROUPS, -1))
    gain_table = group_gain.reshape(GROUPS, -1)
    shift_table = group_shift.reshape(GROUPS, -1)
    normed_state = (grouped - group_mean[:, None]) * inverse[:, None]
    affine = normed_state * gain_table + shift_table
    upstream = slope_in.reshape(grouped.shape) * silu_slope(affine) * gain_table
    group_terms = lax.psum(
        (jnp.sum(upstream, axis=(0, 1, 2, 4)), jnp.sum(upstream * normed_state, axis=(0, 1, 2, 4))),
        "row",
    )
    first_part = group_terms[0] / cell_total
    second_part = group_terms[1] / cell_total
    state_grad = (upstream - first_part[:, None] - normed_state * second_part[:, None]) * inverse[
        :, None
    ]
    return state_grad.reshape(state_rows.shape).astype(jnp.bfloat16)


def per_device(
    frames,
    frame_owner,
    picks,
    patch_weight,
    patch_bias,
    norm_gain,
    head_weight,
    head_bias,
    head_out,
    hidden_state,
    group_gain,
    group_shift,
    out_weight,
    inner_weight,
):
    devices = lax.axis_size("row")
    position = lax.axis_index("row")
    per_frame = devices // FRAMES
    slot = position // per_frame
    height = frames.shape[1]
    strip = frames.shape[2]
    own_rows = hidden_state.shape[0]
    frame_width = hidden_state.shape[2]
    tokens = to_tokens(frames)
    embedded = jnp.dot(tokens, patch_weight, preferred_element_type=jnp.float32) + patch_bias
    centred = embedded - jnp.mean(embedded, axis=1, keepdims=True)
    inv_spread = lax.rsqrt(jnp.mean(centred * centred, axis=1, keepdims=True) + eps_norm)
    normed = centred * inv_spread
    slot_mask = (jnp.arange(FRAMES, dtype=jnp.int32) == slot).astype(jnp.float32)
    partial_pool = slot_mask[:, None] * jnp.sum(normed * norm_gain, axis=0)[None, :]
    grouped = hidden_state.reshape(own_rows, FRAMES, frame_width, GROUPS, -1)
    first_sum = jnp.sum(grouped, axis=(0, 1, 2, 4), dtype=jnp.float32)
    second_sum = jnp.sum(jnp.square(grouped.astype(jnp.float32)), axis=(0, 1, 2, 4))
    pooled_sum, first_total, second_total = lax.psum((partial_pool, first_sum, second_sum), "row")
    frame_tokens = height // PATCH * (strip * per_frame // PATCH)
    pooled = pooled_sum / frame_tokens
    head_full = head_weight.astype(jnp.float32)
    before = jnp.dot(pooled, head_full, precision=lax.Precision.HIGHEST) + head_bias
    pulled = jnp.dot(head_out * silu_slope(before), head_full.T, precision=lax.Precision.HIGHEST)
    picked = jnp.sum((picks[:, None] == frame_owner[None, :]).astype(jnp.float32), axis=0)
    slot_grad = jnp.dot(slot_mask * picked, pulled, precision=lax.Precision.HIGHEST)
    scaled = norm_gain * slot_grad
    token_grad = inv_spread * (
        scaled - jnp.mean(scaled) - normed * jnp.mean(scaled * normed, axis=1, keepdims=True)
    )
    patch_grad = lax.dot_general(
        token_grad.astype(jnp.bfloat16),
        patch_weight,
        (((1,), (1,)), ((), ())),
        preferred_element_type=jnp.float32,
    )
    pixel_local = from_tokens(patch_grad, height, strip).astype(jnp.bfloat16)
    arrived = lax.all_to_all(pixel_local, "row", split_axis=1, concat_axis=2, tiled=True)
    by_slot = arrived.reshape(3, own_rows, FRAMES, frame_width)
    owner_table = (frame_owner[:, None] == jnp.arange(FRAMES, dtype=jnp.int32)[None, :]).astype(
        jnp.bfloat16
    )
    ordered = jnp.einsum(
        "krbw,bf->krfw", by_slot, owner_table, preferred_element_type=jnp.float32
    ).astype(jnp.bfloat16)
    cell_total = own_rows * devices * FRAMES * frame_width * (hidden_state.shape[3] // GROUPS)
    group_mean = first_total / cell_total
    inverse = lax.rsqrt(second_total / cell_total - group_mean * group_mean + eps_norm)
    pixel_padded = extended(ordered, (("row", 1),), 1)
    slope_in = pixel_back(pixel_padded, out_weight, own_rows)
    state_grad = group_back(
        hidden_state, slope_in, group_mean, inverse, group_gain, group_shift, cell_total
    )
    grad_padded = extended(state_grad, (("row", 0),), 1)
    return inner_back(grad_padded, inner_weight, own_rows).astype(jnp.bfloat16)


def split_rows(row):
    high = row.astype(jnp.bfloat16).astype(jnp.float32)
    rest = row - high
    middle = rest.astype(jnp.bfloat16).astype(jnp.float32)
    low = rest - middle
    index = lax.broadcasted_iota(jnp.int32, (8, row.shape[1]), 0)
    stacked = jnp.where(
        index == 0, high, jnp.where(index == 1, middle, jnp.where(index == 2, low, 0.0))
    )
    return stacked.astype(jnp.bfloat16)


def fused_kernel(
    n,
    frames_any,
    owner_any,
    picks_any,
    patch_any,
    patch_bias_any,
    norm_gain_any,
    head_any,
    head_bias_any,
    head_out_any,
    hidden_any,
    group_gain_any,
    group_shift_any,
    out_weight_any,
    inner_any,
    ready,
    normed_ref,
    terms,
    turned,
    paired,
    frames,
    owner,
    picks,
    wide_rows,
    group_rows,
    out_weight,
    patch_w,
    head_w,
    hidden,
    inner_w,
    pixels,
    tokens,
    sent,
    arrived,
    by_frame,
    columns,
    taps,
    band,
    slope,
    cells,
    sums_one,
    sums_two,
    local_sem,
    send_sem,
    recv_sem,
):
    me = lax.axis_index("row")
    strip, height = frames.shape[1], frames.shape[2]
    patch_rows = height // PATCH
    own = hidden.shape[0] - 2
    wide = hidden.shape[2]
    channels = hidden.shape[3]
    line = FRAMES * wide
    pitch = wide + 1
    per_group = channels // GROUPS
    cell_total = own * n * FRAMES * wide * per_group
    window = wide // 2 + 1
    piece = 3 * window
    slot_lanes = 64
    half = arrived.shape[1]

    def peer(offset):
        target = me
        step = 1
        while step < n:
            if offset // step % 2:
                target = target + step * (1 - 2 * lax.rem(lax.div(me, step), 2))
            step *= 2
        return target

    farthest_first = range(n - 1, 0, -1)

    barrier = pltpu.get_barrier_semaphore()
    for offset in farthest_first:
        pl.semaphore_signal(barrier, inc=1, device_id={"row": peer(offset)}, device_id_type=MESH)

    load_frames = pltpu.make_async_copy(frames_any, frames, local_sem.at[0])
    load_hidden = pltpu.make_async_copy(hidden_any, hidden.at[pl.ds(1, own)], local_sem.at[1])
    pix, width = patch_w.shape
    third, part_rows = pix // 3, width // 2
    pieces = ((0, 2 * third), (2 * third, pix))
    load_patch = [
        pltpu.make_async_copy(
            patch_any.at[pl.ds(low, high - low)],
            patch_w.at[pl.ds(low, high - low)],
            local_sem.at[2 + part],
        )
        for part, (low, high) in enumerate(pieces)
    ]
    load_head = [
        pltpu.make_async_copy(
            head_any.at[pl.ds(part * part_rows, part_rows)],
            head_w.at[pl.ds(part * part_rows, part_rows)],
            local_sem.at[4 + part],
        )
        for part in range(2)
    ]
    load_inner = pltpu.make_async_copy(inner_any, inner_w, local_sem.at[6])
    load_out = pltpu.make_async_copy(out_weight_any, out_weight, local_sem.at[6])
    load_owner = pltpu.make_async_copy(owner_any, owner, local_sem.at[6])
    load_picks = pltpu.make_async_copy(picks_any, picks, local_sem.at[6])
    load_wide = [
        pltpu.make_async_copy(source, wide_rows.at[index], local_sem.at[1])
        for index, source in enumerate((patch_bias_any, norm_gain_any, head_bias_any, head_out_any))
    ]
    load_group = [
        pltpu.make_async_copy(source, group_rows.at[index], local_sem.at[6])
        for index, source in enumerate((group_gain_any, group_shift_any))
    ]
    load_frames.start()
    load_hidden.start()
    for load in load_wide:
        load.start()
    for load in load_patch + load_head:
        load.start()
    load_owner.start()
    load_picks.start()
    for load in load_group:
        load.start()
    load_out.start()
    load_inner.start()

    group_row = lax.broadcasted_iota(jnp.int32, (channels, channels), 0) // per_group
    group_col = lax.broadcasted_iota(jnp.int32, (channels, channels), 1) // per_group
    same_group = (group_row == group_col).astype(jnp.bfloat16)
    eight = lax.broadcasted_iota(jnp.int32, (8, channels), 0)
    spot = lax.broadcasted_iota(jnp.int32, (2, channels), 0)

    def group_sums(first, second):
        part = lax.rem(eight, 4)
        row = jnp.where(eight < 4, first, second)
        high = row.astype(jnp.bfloat16).astype(jnp.float32)
        rest = row - high
        middle = rest.astype(jnp.bfloat16).astype(jnp.float32)
        stacked = jnp.where(
            part == 0, high, jnp.where(part == 1, middle, jnp.where(part == 2, rest - middle, 0.0))
        )
        summed = jnp.dot(
            stacked.astype(jnp.bfloat16), same_group, preferred_element_type=jnp.float32
        )
        return (
            jnp.sum(summed[0:4], axis=0, keepdims=True),
            jnp.sum(summed[4:8], axis=0, keepdims=True),
        )

    def tree_sum(blocks):
        while len(blocks) > 1:
            blocks = [
                blocks[at] + blocks[at + 1] if at + 1 < len(blocks) else blocks[at]
                for at in range(0, len(blocks), 2)
            ]
        return blocks[0]

    def over_devices(buffer):
        return tree_sum([buffer[slot] for slot in range(n)])

    load_frames.wait()
    for colour in range(3):
        pixels[colour] = frames[colour].astype(jnp.float32).T
    tokens[...] = jnp.zeros_like(tokens)
    for colour in range(3):
        for line_in in range(PATCH):
            at = (colour * PATCH + line_in) * PATCH
            tokens[0:patch_rows, at : at + PATCH] = pixels[
                colour, pl.ds(line_in, patch_rows, stride=PATCH), :
            ]
    sent[...] = jnp.zeros_like(sent)

    load_hidden.wait()
    pltpu.make_async_copy(wide_rows, wide_rows, local_sem.at[1]).wait()
    first = jnp.zeros((1, channels), jnp.float32)
    second = jnp.zeros((1, channels), jnp.float32)
    for row in range(own):
        state = hidden[1 + row].reshape(line, channels).astype(jnp.float32)
        first = first + jnp.sum(state, axis=0, keepdims=True)
        second = second + jnp.sum(state * state, axis=0, keepdims=True)
    first, second = group_sums(first, second)
    sums_one[me] = jnp.where(spot == 0, first, second)

    embedded = wide_rows[0]
    for part, (low, high) in enumerate(pieces):
        load_patch[part].wait()
        embedded = embedded + jnp.dot(
            tokens[:, low:high].astype(jnp.bfloat16),
            patch_w[low:high],
            preferred_element_type=jnp.float32,
        )
    centred = embedded - jnp.mean(embedded, axis=1, keepdims=True)
    inv_spread = lax.rsqrt(jnp.mean(centred * centred, axis=1, keepdims=True) + eps_norm)
    normed = centred * inv_spread
    gain = wide_rows[1]
    pooled = jnp.sum((normed * gain)[0:patch_rows], axis=0, keepdims=True) / patch_rows
    split_pool = split_rows(pooled)
    before = wide_rows[2]
    for part in range(2):
        load_head[part].wait()
        before = before + jnp.sum(
            jnp.dot(
                split_pool[:, part * part_rows : (part + 1) * part_rows],
                head_w[part * part_rows : (part + 1) * part_rows],
                preferred_element_type=jnp.float32,
            ),
            axis=0,
            keepdims=True,
        )
    pulled = jnp.sum(
        lax.dot_general(
            split_rows(wide_rows[3] * silu_slope(before)),
            head_w[...],
            (((1,), (1,)), ((), ())),
            preferred_element_type=jnp.float32,
        ),
        axis=0,
        keepdims=True,
    )
    load_owner.wait()
    load_picks.wait()
    pltpu.make_async_copy(group_rows, group_rows, local_sem.at[6]).wait()
    load_out.wait()
    load_inner.wait()
    mine = owner[me]
    picked = jnp.float32(0.0)
    for pick in range(picks.shape[0]):
        picked = picked + jnp.where(picks[pick] == mine, jnp.float32(1.0), jnp.float32(0.0))
    scaled = gain * (picked * pulled)
    token_grad = inv_spread * (
        scaled
        - jnp.mean(scaled, axis=1, keepdims=True)
        - normed * jnp.mean(scaled * normed, axis=1, keepdims=True)
    )
    token_grad = token_grad.astype(jnp.bfloat16)
    sixth = pix // 6
    cuts = (0, 3, 6)
    patch_grad = jnp.concatenate(
        [
            lax.dot_general(
                token_grad,
                patch_w[low * sixth : high * sixth],
                (((1,), (1,)), ((), ())),
                preferred_element_type=jnp.float32,
            )
            for low, high in zip(cuts[:-1], cuts[1:])
        ],
        axis=1,
    )
    patch_grad = patch_grad.astype(jnp.bfloat16).astype(jnp.float32)
    for line_in in range(PATCH):
        lines = [
            patch_grad[:, (colour * PATCH + line_in) * PATCH : (colour * PATCH + line_in + 1) * PATCH]
            for colour in range(3)
        ]
        joined = jnp.concatenate(
            [line_of[:, 0:window] for line_of in lines]
            + [jnp.zeros((lines[0].shape[0], slot_lanes - 2 * piece), jnp.float32)]
            + [line_of[:, wide - window : wide] for line_of in lines],
            axis=1,
        )
        for patch_row in range(patch_rows):
            at = 2 + patch_row * PATCH + line_in
            sent[at, :, 0:slot_lanes] = joined[patch_row : patch_row + 1]
            if at >= half:
                sent[at - half, :, slot_lanes : 2 * slot_lanes] = joined[patch_row : patch_row + 1]

    pl.semaphore_wait(barrier, n - 1)

    def send_sums(buffer, kind, offset):
        pltpu.make_async_remote_copy(
            src_ref=buffer.at[me],
            dst_ref=buffer.at[me],
            send_sem=send_sem,
            recv_sem=recv_sem.at[kind],
            device_id={"row": peer(offset)},
            device_id_type=MESH,
        ).start()

    def from_peers(buffer, kind):
        others = buffer.at[pl.ds(0, n - 1)]
        pltpu.make_async_copy(others, others, recv_sem.at[kind]).wait()

    def to_peers(buffer):
        others = buffer.at[pl.ds(0, n - 1)]
        pltpu.make_async_copy(others, others, send_sem).wait()

    for offset in farthest_first:
        target = peer(offset)
        pltpu.make_async_remote_copy(
            src_ref=sent.at[pl.ds(target * own, half)],
            dst_ref=arrived.at[me],
            send_sem=send_sem,
            recv_sem=recv_sem.at[1],
            device_id={"row": target},
            device_id_type=MESH,
        ).start()
        send_sums(sums_one, 0, offset)
    to_right = pltpu.make_async_remote_copy(
        src_ref=hidden_any.at[pl.ds(own - 1, 1)],
        dst_ref=hidden.at[pl.ds(0, 1)],
        send_sem=send_sem,
        recv_sem=recv_sem.at[3],
        device_id={"row": lax.rem(me + 1, n)},
        device_id_type=MESH,
    )
    to_left = pltpu.make_async_remote_copy(
        src_ref=hidden_any.at[pl.ds(0, 1)],
        dst_ref=hidden.at[pl.ds(own + 1, 1)],
        send_sem=send_sem,
        recv_sem=recv_sem.at[4],
        device_id={"row": lax.rem(me + n - 1, n)},
        device_id_type=MESH,
    )

    @pl.when(me < n - 1)
    def _():
        to_right.start()

    @pl.when(me > 0)
    def _():
        to_left.start()

    @pl.when(me == 0)
    def _():
        hidden[0] = jnp.zeros(hidden.shape[1:], hidden.dtype)

    @pl.when(me == n - 1)
    def _():
        hidden[own + 1] = jnp.zeros(hidden.shape[1:], hidden.dtype)

    arrived[me] = sent[pl.ds(me * own, half)]

    taps[...] = jnp.zeros_like(taps)
    for time_tap in range(3):
        for row_tap in range(3):
            for col_tap in range(3):
                at = ((time_tap * 3 + row_tap) * 3 + col_tap) * 3
                taps[at : at + 3] = out_weight[time_tap, row_tap, col_tap].astype(jnp.float32)
    flat_taps = taps[...].astype(jnp.bfloat16)
    depth = band.shape[0]
    entry = lax.broadcasted_iota(jnp.int32, (depth, channels), 0)
    tap_lane = lax.broadcasted_iota(jnp.int32, (depth, channels), 1)
    tap_of = entry // piece
    column = lax.rem(entry, window)
    first_lane = (
        (lax.rem(tap_of, 3) * 3 + tap_of // 3) * 9 + lax.rem(entry, piece) // window - 3 * column
    )
    for output in range(window):
        col_tap = output + 1 - column
        chosen = (
            (tap_lane == first_lane + 3 * (output + 1))
            & (col_tap >= 0)
            & (col_tap < 3)
            & (entry < 9 * piece)
        )
        band[:, output * channels : (output + 1) * channels] = jnp.dot(
            chosen.astype(jnp.float32).astype(jnp.bfloat16),
            flat_taps,
            preferred_element_type=jnp.float32,
        ).astype(jnp.bfloat16)
    columns[...] = jnp.zeros_like(columns)
    by_frame[...] = jnp.zeros_like(by_frame)

    slot_of = []
    for frame in range(FRAMES):
        found = jnp.int32(0)
        for slot in range(n):
            found = jnp.where(owner[slot] == frame, jnp.int32(slot), found)
        slot_of.append(found)


    def spread_cells(row):
        for frame in range(FRAMES):
            at = (row * FRAMES + frame) * pitch
            cells[at : at + wide] = hidden[row, frame].astype(jnp.float32)

    for row in range(1, own + 1):
        spread_cells(row)

    empty = jnp.zeros((channels, channels), jnp.bfloat16)
    for row_tap in range(3):
        above = 2 - row_tap
        for col_tap in range(3):
            part = pl.ds(col_tap * channels, channels)
            blocks = [inner_w[time_tap, row_tap, col_tap].T for time_tap in range(3)]
            for ahead in range(2):
                turned[above, ahead, part, 0:channels] = blocks[1 - ahead]
                turned[above, ahead, part, channels:] = blocks[2 - ahead]
            for side in range(2):
                at = (2 - col_tap + side) * channels
                for kind in range(2):
                    paired[kind, above, at : at + channels, side * channels : (side + 1) * channels] = (
                        blocks[2 - 2 * kind]
                    )
        for kind in range(2):
            paired[kind, above, 3 * channels :, 0:channels] = empty
            paired[kind, above, 0:channels, channels:] = empty

    from_peers(sums_one, 0)
    from_peers(arrived, 1)
    means = over_devices(sums_one) / cell_total
    group_mean = means[0:1]
    inverse = lax.rsqrt(means[1:2] - group_mean * group_mean + eps_norm)
    group_gain = group_rows[0]
    group_shift = group_rows[1]
    def pixel_taps(row, block):
        for row_tap in range(3):
            for time_tap in range(3):
                at = (row_tap * 3 + time_tap) * piece
                source = row - row_tap + 2
                for side in range(2):
                    lane = source // half * slot_lanes + side * (slot_lanes - piece)
                    columns[block[side] : block[side] + FRAMES, at : at + piece] = by_frame[
                        source % half, 2 - time_tap : 2 - time_tap + FRAMES, lane : lane + piece
                    ]

    spread = inverse * group_gain

    def state_terms(part):
        centred = cells[part] - group_mean
        return centred, silu_slope(centred * spread + group_shift)

    own_cells = own * FRAMES
    for frame in range(FRAMES):
        for row in range(half):
            by_frame[row, frame : frame + 1, :] = arrived[slot_of[frame], row]
    for row in range(1, own + 1):
        pixel_taps(row, ((row - 1) * FRAMES, own_cells + (row - 1) * FRAMES))
    left = columns[0 : 2 * own_cells].astype(jnp.bfloat16)
    first = jnp.zeros((8, channels), jnp.float32)
    second = jnp.zeros((8, channels), jnp.float32)
    for output in range(0, window, 2):
        lanes = pl.ds(output * channels, min(2, window - output) * channels)
        several = jnp.dot(left, band[:, lanes], preferred_element_type=jnp.float32)
        for index in range(several.shape[1] // channels):
            for side in range(2):
                w = output + index + side * (wide - window)
                if side == 0 and output + index == window - 1 or side == 1 and output + index == 0:
                    continue
                centred, slope_factor = state_terms(
                    pl.ds(FRAMES * pitch + w, own_cells, stride=pitch)
                )
                upstream = (
                    several[
                        side * own_cells : (side + 1) * own_cells,
                        index * channels : (index + 1) * channels,
                    ]
                    * slope_factor
                )
                first = first + jnp.sum(upstream.reshape(-1, 8, channels), axis=0)
                second = second + jnp.sum(
                    (upstream * centred).reshape(-1, 8, channels), axis=0
                )
    first = jnp.sum(first, axis=0, keepdims=True) * group_gain
    second = jnp.sum(second, axis=0, keepdims=True) * spread
    sums_two[me] = jnp.where(spot == 0, first, second)
    for offset in farthest_first:
        send_sums(sums_two, 2, offset)


    @pl.when(me < n - 1)
    def _():
        to_left.wait_recv()

    @pl.when(me > 0)
    def _():
        to_right.wait_recv()

    for index, row in enumerate((0, own + 1)):
        pixel_taps(row, (2 * own_cells + index * FRAMES, 2 * own_cells + (2 + index) * FRAMES))
        spread_cells(row)
    left = columns[...].astype(jnp.bfloat16)
    for output in range(window):
        several = jnp.dot(
            left,
            band[:, output * channels : (output + 1) * channels],
            preferred_element_type=jnp.float32,
        )
        for side in range(2):
            if side == 0 and output == window - 1 or side == 1 and output == 0:
                continue
            w = output + side * (wide - window)
            part = pl.ds(FRAMES * pitch + w, own_cells, stride=pitch)
            slope[part] = (
                several[side * own_cells : (side + 1) * own_cells] * state_terms(part)[1]
            )
            for index, row in enumerate((0, own + 1)):
                part = pl.ds(row * FRAMES * pitch + w, FRAMES, stride=pitch)
                at = 2 * own_cells + (2 * side + index) * FRAMES
                slope[part] = several[at : at + FRAMES] * state_terms(part)[1]
    terms[2:3] = inverse / cell_total
    for cell in range((own + 2) * FRAMES):
        part = pl.ds(cell * wide, wide)
        ready[part] = slope[cell * pitch : cell * pitch + wide] * spread
        state = hidden[cell // FRAMES, cell % FRAMES].astype(jnp.float32)
        normed_ref[part] = (state - group_mean) * inverse

    to_peers(sums_one)
    to_peers(arrived)
    to_peers(sums_two)

    @pl.when(me < n - 1)
    def _():
        to_right.wait_send()

    @pl.when(me > 0)
    def _():
        to_left.wait_send()

    from_peers(sums_two, 2)
    terms[0:2] = over_devices(sums_two)


def last_kernel(
    n, ready, normed_ref, terms, turned, paired, out_any, padded, windows, pairs, rest, out, out_sem
):
    me = lax.axis_index("row")
    own = out.shape[0]
    wide = out.shape[3]
    channels = out.shape[4]
    line = FRAMES * wide
    windows[:, FRAMES // 2, 0] = jnp.zeros((own + 2, wide, 3 * channels), jnp.bfloat16)
    pairs[1, :, FRAMES // 2 - 1] = jnp.zeros((own + 2, wide // 2, 4 * channels), jnp.bfloat16)
    pitch = wide + 1
    blank = jnp.zeros((1, channels), jnp.float32)
    for cell in range((own + 2) * FRAMES + 1):
        padded[cell * pitch : cell * pitch + 1] = blank
    total = terms[0:2]
    lane = lax.broadcasted_iota(jnp.int32, total.shape, 1)
    step = 1
    while step < channels // GROUPS:
        total = total + jnp.where(
            lax.rem(lane // step, 2) == 0,
            pltpu.roll(total, channels - step, 1),
            pltpu.roll(total, step, 1),
        )
        step *= 2
    total = total * terms[2:3]
    first_part = jnp.broadcast_to(total[0:1], (wide, channels))
    second_part = jnp.broadcast_to(total[1:2], (wide, channels))
    for row in range(own + 2):
        for frame in range(FRAMES):
            cell = row * FRAMES + frame
            part = pl.ds(cell * wide, wide)
            state_grad = ready[part] - first_part - normed_ref[part] * second_part
            if row == 0:
                state_grad = jnp.where(me > 0, state_grad, 0.0)
            if row == own + 1:
                state_grad = jnp.where(me < n - 1, state_grad, 0.0)
            at = cell * pitch + 1
            padded[at : at + wide] = state_grad
            for col_tap in range(3 if frame > 0 else 0):
                windows[
                    row, frame // 2, frame % 2, :, col_tap * channels : (col_tap + 1) * channels
                ] = padded[at + 1 - col_tap : at + 1 - col_tap + wide].astype(jnp.bfloat16)
            kind, step = frame % 2, frame // 2 - frame % 2
            if step >= 0:
                for index in range(4):
                    pairs[kind, row, step, :, index * channels : (index + 1) * channels] = padded[
                        pl.ds(cell * pitch + index, wide // 2, stride=2)
                    ].astype(jnp.bfloat16)
    half_line = line // 2
    taken = jnp.concatenate(
        [
            windows[
                above : above + own, ahead // 2 : ahead // 2 + FRAMES // 2, ahead % 2
            ].reshape(own * half_line, 3 * channels)
            for above in range(3)
            for ahead in (1, 2)
        ],
        axis=1,
    )
    summed = jnp.dot(
        taken,
        turned[...].reshape(6 * 3 * channels, 2 * channels),
        preferred_element_type=jnp.float32,
    )
    for kind in range(2):
        left = jnp.concatenate(
            [
                pairs[kind, above : above + own].reshape(own * half_line // 2, 4 * channels)
                for above in range(3)
            ],
            axis=1,
        )
        both = jnp.dot(
            left,
            paired[kind].reshape(12 * channels, 2 * channels),
            preferred_element_type=jnp.float32,
        )
        for side in range(2):
            rest[kind, pl.ds(side, own * half_line // 2, stride=2)] = both[
                :, side * channels : (side + 1) * channels
            ]
    for row in range(own):
        for side in range(2):
            out[row, :, side] = (
                (
                    summed[
                        row * half_line : (row + 1) * half_line,
                        side * channels : (side + 1) * channels,
                    ]
                    + rest[side, row * half_line : (row + 1) * half_line]
                )
                .reshape(FRAMES // 2, wide, channels)
                .astype(jnp.bfloat16)
            )
        pltpu.make_async_copy(out.at[row], out_any.at[row], out_sem).start()
    pltpu.make_async_copy(out, out_any, out_sem).wait()


def one_frame_each(
    frames,
    frame_owner,
    picks,
    patch_weight,
    patch_bias,
    norm_gain,
    head_weight,
    head_bias,
    head_out,
    hidden_state,
    group_gain,
    group_shift,
    out_weight,
    inner_weight,
):
    n = lax.axis_size("row")
    own, frame_count, wide, channels = hidden_state.shape
    height, strip = frames.shape[1:]
    pix, width = patch_weight.shape
    window = wide // 2 + 1
    depth = -(-27 * window // 128) * 128
    cells = (own + 2) * frame_count * wide
    f32, bf16 = jnp.float32, jnp.bfloat16
    vmem = pl.BlockSpec(memory_space=pltpu.VMEM)
    dma = pltpu.SemaphoreType.DMA
    passed = [
        pltpu.VMEM((cells, channels), f32),
        pltpu.VMEM((cells, channels), f32),
        pltpu.VMEM((8, channels), f32),
        pltpu.VMEM((3, 2, 3 * channels, 2 * channels), bf16),
        pltpu.VMEM((2, 3, 4 * channels, 2 * channels), bf16),
    ]
    kept = pl.pallas_call(
        functools.partial(fused_kernel, n),
        out_shape=passed,
        in_specs=[pl.BlockSpec(memory_space=pltpu.HBM)] * 14,
        out_specs=[vmem] * 5,
        scratch_shapes=[
            pltpu.VMEM((3, strip, height), bf16),
            pltpu.SMEM(frame_owner.shape, jnp.int32),
            pltpu.SMEM(picks.shape, jnp.int32),
            pltpu.VMEM((4, 1, width), f32),
            pltpu.VMEM((2, 1, channels), f32),
            pltpu.VMEM(out_weight.shape, bf16),
            pltpu.VMEM((pix, width), bf16),
            pltpu.VMEM(head_weight.shape, bf16),
            pltpu.VMEM((own + 2, frame_count, wide, channels), bf16),
            pltpu.VMEM(inner_weight.shape, bf16),
            pltpu.VMEM(frames.shape, f32),
            pltpu.VMEM((-(-(height // PATCH) // 8) * 8, pix), f32),
            pltpu.VMEM((height + 4, 1, 128), f32),
            pltpu.VMEM((n, (own + 5) // 2, 1, 128), f32),
            pltpu.VMEM(((own + 5) // 2, frame_count + 8, 128), f32),
            pltpu.VMEM((2 * (own + 2) * frame_count, depth), f32),
            pltpu.VMEM((128, channels), f32),
            pltpu.VMEM((depth, window * channels), bf16),
            pltpu.VMEM(((own + 2) * frame_count * (wide + 1), channels), f32),
            pltpu.VMEM(((own + 2) * frame_count * (wide + 1), channels), f32),
            pltpu.VMEM((n, 2, channels), f32),
            pltpu.VMEM((n, 2, channels), f32),
            dma((7,)),
            dma,
            dma((5,)),
        ],
        compiler_params=pltpu.CompilerParams(
            collective_id=0, has_side_effects=True, vmem_limit_bytes=32 << 20
        ),
    )(
        *(
            pltpu.with_memory_space_constraint(array, pltpu.HBM)
            for array in (
                frames.transpose(0, 2, 1),
                frame_owner,
                picks,
                patch_weight,
                patch_bias[None],
                norm_gain[None],
                head_weight,
                head_bias[None],
                head_out[None],
                hidden_state,
                group_gain[None],
                group_shift[None],
                out_weight,
                inner_weight,
            )
        )
    )
    out_shape = (own, frame_count // 2, 2, wide, channels)
    return pl.pallas_call(
        functools.partial(last_kernel, n),
        out_shape=jax.ShapeDtypeStruct(out_shape, bf16),
        in_specs=[vmem] * 5,
        out_specs=pl.BlockSpec(memory_space=pltpu.HBM),
        scratch_shapes=[
            pltpu.VMEM((-(-((own + 2) * frame_count * (wide + 1) + 1) // 8) * 8, channels), f32),
            pltpu.VMEM((own + 2, frame_count // 2 + 1, 2, wide, 3 * channels), bf16),
            pltpu.VMEM((2, own + 2, frame_count // 2, wide // 2, 4 * channels), bf16),
            pltpu.VMEM((2, own * frame_count * wide // 2, channels), f32),
            pltpu.VMEM(out_shape, bf16),
            dma,
        ],
        compiler_params=pltpu.CompilerParams(vmem_limit_bytes=32 << 20),
    )(*kept).reshape(hidden_state.shape)


def solution(mesh):
    body = one_frame_each if mesh.shape["row"] == FRAMES else per_device
    return jax.shard_map(
        body,
        mesh=mesh,
        in_specs=(
            P(None, None, ("clip", "row")),
            P("clip"),
            P("clip"),
            P(),
            P(),
            P(),
            P(),
            P(),
            P(),
            P(("clip", "row"), None, None, None),
            P(),
            P(),
            P(),
            P(),
        ),
        out_specs=P(("clip", "row"), None, None, None),
        check_vma=False,
    )
```
